32 devices in a mesh: group: 2 (over y), row: 8 (over z, x), col: 2 (over core).
Axes of the slice: x: 2, y: 2, z: 4, core: 2. Of those that a mesh axis runs over, the one named last changes fastest.
Arguments:
- map_in: bfloat16 [192, 96, 48], P(('group', 'row'), 'col'), parts along dimension 0, may hold values from -6 to 6
- embedding: bfloat16 [192, 96], P(('group', 'row')), parts along dimension 0, may hold values from -6 to 6
- w_row: bfloat16 [96, 48], replicated, may hold values from -0.625 to 0.625
- w_col: bfloat16 [96, 48], replicated, may hold values from -0.625 to 0.625
- first_kernel_weight: bfloat16 [3, 3, 48, 48], replicated, may hold values from -0.3125 to 0.3125
- first_bias: float32 [48], replicated, may hold values from -0.5 to 0.5
- second_kernel_weight: bfloat16 [3, 3, 48, 48], replicated, may hold values from -0.3125 to 0.3125
- second_bias: float32 [48], replicated, may hold values from -0.5 to 0.5
- w_mix: bfloat16 [48, 48], replicated, may hold values from -0.875 to 0.875
- b_mix: float32 [48], replicated, may hold values from -0.5 to 0.5
- w_head: float32 [48], replicated, may hold values from -0.875 to 0.875
Outputs:
- contacts: float32 [192, 96], P(('group', 'row'), 'col'), parts along dimension 0
The draws below stay inside these ranges and needn't reach their ends.
There are 2 independent parts, one for each index of `group`. The reference program is written for one: setup_inputs(seed, part) draws one part's arguments, and reference() takes and returns one part's arrays. A program takes and returns all parts, laid end to end along the dimension named above; an argument that names none is the same for every part. Nothing has to cross between parts.
All inputs are finite; a program needn't handle non-finite values.
Results may differ from the reference program's by a relative error of at most 0.0055.
Values may be sent and summed in bfloat16 or wider, within the bound.
A program may use at most 64 MiB of HBM per device.

```python
import jax
import jax.numpy as jnp
from jax import lax

CH = 48
E = 96
FIRST_DILATION = 4
SECOND_DILATION = 8
ROWS_DEV = 12
BINS = 96


def level_of(key, extent, shards, smallest, top_value):
    def one(dim, parts):
        steps = jax.random.uniform(jax.random.fold_in(jax.random.fold_in(key, 6), dim), (parts,), jnp.float32, smallest / len(shards), top_value / len(shards))
        return jnp.repeat(jnp.exp(steps), extent[dim] // parts).reshape((-1,) + (1,) * (len(extent) - dim - 1))

    level = one(*shards[0])
    for cut in shards[1:]:
        level = level * one(*cut)
    return level


def noise(stream_key, shape, deviation, most, shards=(), held_as=jnp.bfloat16):
    entries = jax.random.normal(stream_key, shape, jnp.float32) * deviation
    if len(shards) > 0:
        entries = level_of(stream_key, shape, shards, -0.22, 0.18) * entries
    return jnp.clip(entries, min=-most, max=most).astype(held_as)


def setup_inputs(seed: int = 0, part: int = 0) -> dict:
    splits = jax.random.split(jax.random.key(seed), 12)
    part_keys = jax.random.split(jax.random.fold_in(splits[11], part), 12)
    map_in = noise(part_keys[0], (BINS, BINS, CH), 1.0, 6.0, ((0, 8), (1, 2)))
    embedding = noise(part_keys[1], (BINS, E), 1.0, 6.0, ((0, 8),))
    w_row = noise(splits[2], (E, CH), E ** -0.5, 0.625)
    w_col = noise(splits[3], (E, CH), E ** -0.5, 0.625)
    first_kernel_weight = noise(splits[4], (3, 3, CH, CH), (9 * CH) ** -0.5, 0.3125)
    first_bias = jnp.clip(jax.random.uniform(splits[5], (CH,), jnp.float32, -0.5, 0.5), -0.5, 0.5)
    second_kernel_weight = noise(splits[6], (3, 3, CH, CH), (9 * CH) ** -0.5, 0.3125)
    second_bias = jnp.clip(jax.random.uniform(splits[7], (CH,), jnp.float32, -0.5, 0.5), -0.5, 0.5)
    w_mix = noise(splits[8], (CH, CH), CH ** -0.5, 0.875)
    b_mix = jnp.clip(jax.random.uniform(splits[9], (CH,), jnp.float32, -0.5, 0.5), -0.5, 0.5)
    w_head = noise(splits[10], (CH,), CH ** -0.5, 0.875, (), jnp.float32)
    return {"map_in": map_in, "embedding": embedding, "w_row": w_row, "w_col": w_col, "first_kernel_weight": first_kernel_weight, "first_bias": first_bias, "second_kernel_weight": second_kernel_weight, "second_bias": second_bias, "w_mix": w_mix, "b_mix": b_mix, "w_head": w_head}


def residual_block(field, weight, bias, spacing):
    bins_total = field.shape[0]
    block = ROWS_DEV
    padded = jnp.pad(field, ((spacing, spacing), (spacing, spacing), (0, 0)))
    kernel = weight.astype(jnp.float32)

    def one_block(start):
        piece = lax.dynamic_slice_in_dim(padded, start, block + 2 * spacing, 0)
        active = jnp.maximum(piece, 0).astype(jnp.float32)
        convolved = lax.conv_general_dilated(
            active[None], kernel, (1, 1), "VALID", rhs_dilation=(spacing, spacing),
            dimension_numbers=("NHWC", "HWIO", "NHWC"), precision=lax.Precision.HIGHEST)[0]
        own_rows = lax.dynamic_slice_in_dim(field, start, block, 0).astype(jnp.float32)
        return (own_rows + convolved + bias).astype(jnp.bfloat16)

    starts = jnp.arange(bins_total // block, dtype=jnp.int32) * block
    return lax.map(one_block, starts).reshape(field.shape)


def reference(map_in, embedding, w_row, w_col, first_kernel_weight, first_bias, second_kernel_weight, second_bias, w_mix, b_mix, w_head):
    row_terms = jnp.dot(embedding, w_row, preferred_element_type=jnp.float32)
    col_terms = jnp.dot(embedding, w_col, preferred_element_type=jnp.float32)
    contact_grid = (map_in.astype(jnp.float32) + row_terms[:, None, :] + col_terms[None, :, :]).astype(jnp.bfloat16)
    first_layer = residual_block(contact_grid, first_kernel_weight, first_bias, FIRST_DILATION)
    second_layer = residual_block(first_layer, second_kernel_weight, second_bias, SECOND_DILATION)
    block = ROWS_DEV
    mixing = w_mix.astype(jnp.float32)

    def head_block(start):
        own_rows = lax.dynamic_slice_in_dim(second_layer, start, block, 0).astype(jnp.float32)
        mirror = jnp.swapaxes(lax.dynamic_slice_in_dim(second_layer, start, block, 1), 0, 1).astype(jnp.float32)
        symmetric = ((own_rows + mirror) * 0.5).astype(jnp.bfloat16)
        mixture = jnp.einsum("rch,hk->rck", symmetric.astype(jnp.float32), mixing,
                             precision=lax.Precision.HIGHEST) + b_mix
        mixture = jnp.maximum(mixture, 0.0)
        return jnp.sum(mixture * w_head, axis=-1)

    starts = jnp.arange(map_in.shape[0] // block, dtype=jnp.int32) * block
    return lax.map(head_block, starts).reshape(map_in.shape[0], map_in.shape[1])
```

```python
import functools

import jax
import jax.numpy as jnp
from jax import lax
from jax.experimental import pallas as pl
from jax.experimental.pallas import tpu as pltpu
from jax.sharding import PartitionSpec as P

FIRST_DILATION = 4
SECOND_DILATION = 8


def padded(array, sides, width):
    for axis, dim in sides:
        peers, length = (lax.axis_size(axis), array.shape[dim])
        up = [(i, (i + 1) % peers) for i in range(peers - 1)]
        down = [(j, i) for i, j in up]
        last = lax.slice_in_dim(array, length - width, length, axis=dim)
        leading = lax.slice_in_dim(array, 0, width, axis=dim)
        before = lax.ppermute(last, axis, up)
        after = lax.ppermute(leading, axis, down)
        array = jnp.concatenate([before, array, after], axis=dim)
    return array


def swapped(value, axis, bit):
    mask = 2**bit
    pairs = [(source, source ^ mask) for source in range(lax.axis_size(axis))]
    return lax.ppermute(value, axis, pairs)


def dilated_conv(active, weight, spacing, out_rows, out_cols):
    windows = []
    for tap_row in range(3):
        for tap_col in range(3):
            windows.append(
                active[
                    tap_row * spacing : tap_row * spacing + out_rows,
                    tap_col * spacing : tap_col * spacing + out_cols,
                ]
            )
    stacked = jnp.concatenate(windows, axis=-1)
    flat_weight = weight.reshape(9 * weight.shape[2], weight.shape[3])
    return jnp.einsum("rch,hk->rck", stacked, flat_weight, preferred_element_type=jnp.float32)


LANES = 128
HALF = 64
SIDE = 16
PHASES = 4
WIDE = 2 * LANES
TAPS = 5 * LANES
FUSED_VMEM = 8 * 2**20


def one_hot(rows, columns, offsets):
    r = lax.broadcasted_iota(jnp.int32, (rows, columns), 0)
    c = lax.broadcasted_iota(jnp.int32, (rows, columns), 1)
    hit = c == r + offsets[0]
    for offset in offsets[1:]:
        hit = hit | (c == r + offset)
    return jnp.where(hit, 1.0, 0.0)


def mm(a, b, precision=None):
    return jnp.dot(a, b, preferred_element_type=jnp.float32, precision=precision)


def mm_tn(a, b):
    return lax.dot_general(a, b, (((0,), (0,)), ((), ())), preferred_element_type=jnp.float32)


def mm_nt(a, b):
    return lax.dot_general(a, b, (((1,), (1,)), ((), ())), preferred_element_type=jnp.float32)


def fused_kernel(
    n,
    m_hbm,
    e_hbm,
    wr_hbm,
    wc_hbm,
    w1_hbm,
    b1_hbm,
    w2_hbm,
    b2_hbm,
    wm_hbm,
    bm_hbm,
    wh_hbm,
    out_ref,
    pk,
    eb,
    ct,
    xb,
    xs,
    l1,
    xs2,
    wa,
    wb,
    yp,
    sf,
    sb,
    gb,
    tb,
    send,
    recv,
    esend,
    erecv,
    msend,
    mrecv,
    lsem,
    isem,
    m_ref,
    e_ref,
    wr_ref,
    wc_ref,
    w1_ref,
    b1_ref,
    w2_ref,
    b2_ref,
    wm_ref,
    bm_ref,
    wh_ref,
):
    bf, f32 = jnp.bfloat16, jnp.float32
    rows, cols, ch = m_ref.shape
    hr = rows // 2
    groups = rows // PHASES
    blocks = pk.shape[1]
    width = cols + SIDE
    per = cols // rows
    big = LANES // PHASES
    small = ch - big
    R = lax.axis_index("row")
    C = lax.axis_index("col")
    O = 1 - C
    group = lax.axis_index("group")
    mesh_type = pl.DeviceIdType.MESH

    eb[...] = jnp.zeros_like(eb)
    barrier = pltpu.get_barrier_semaphore()
    for k in range(n):
        for col in (C, O):
            if k == 0 and col is C:
                continue
            pl.semaphore_signal(
                barrier, inc=1, device_id=(group, lax.rem(R + k, n), col), device_id_type=mesh_type
            )

    inputs = (
        (m_hbm, m_ref),
        (e_hbm, e_ref),
        (wr_hbm, wr_ref),
        (wc_hbm, wc_ref),
        (w1_hbm, w1_ref),
        (b1_hbm, b1_ref),
        (w2_hbm, w2_ref),
        (b2_hbm, b2_ref),
        (wm_hbm, wm_ref),
        (bm_hbm, bm_ref),
        (wh_hbm, wh_ref),
    )
    loads = [pltpu.make_async_copy(a, b, isem.at[i]) for i, (a, b) in enumerate(inputs)]
    for load in loads:
        load.start()

    h_at = lax.broadcasted_iota(jnp.int32, (ch, WIDE), 0)
    l_at = lax.broadcasted_iota(jnp.int32, (ch, WIDE), 1)
    in_big = l_at < LANES
    spread = jnp.where(
        jnp.where(in_big, l_at % big, big + l_at % small) == h_at, 1.0, 0.0
    )
    lanes = lax.broadcasted_iota(jnp.int32, (1, WIDE), 1)
    phase_of = jnp.where(lanes < LANES, lanes // big, (lanes % HALF) // small)
    spread4 = jnp.where(l_at % HALF == h_at, 1.0, 0.0).astype(bf)
    phase4_of = lanes // HALF
    lane = lax.broadcasted_iota(jnp.int32, (1, LANES), 1)
    lower = lane < HALF

    own_at = pl.multiple_of(SIDE * C, SIDE)
    placed = [jnp.where(phase_of == p, spread, 0.0).astype(bf) for p in range(PHASES)]
    loads[0].wait()
    tile = m_ref[...].reshape(groups, PHASES, cols, ch)
    packed = mm(tile[:, 0].reshape(groups * cols, ch), placed[0])
    for p in range(1, PHASES):
        packed = packed + mm(tile[:, p].reshape(groups * cols, ch), placed[p])
    packed = packed.reshape(groups, cols, WIDE)
    for g in range(groups):
        pk[1, g, pl.ds(own_at, cols), :] = packed[g, :, :LANES].astype(bf)
    for t in range(blocks - groups):
        piece = packed[2 * t, :, LANES:]
        if 2 * t + 1 < groups:
            piece = jnp.where(lower, piece, packed[2 * t + 1, :, LANES:])
        pk[1, groups + t, pl.ds(own_at, cols), :] = piece.astype(bf)
    loads[1].wait()
    eb[R] = e_ref[...]

    pl.semaphore_wait(barrier, 2 * n - 1)

    def remote(src, dst, s, r, row, col):
        return pltpu.make_async_remote_copy(
            src_ref=src,
            dst_ref=dst,
            send_sem=s,
            recv_sem=r,
            device_id=(group, row, col),
            device_id_type=mesh_type,
        )

    def needs(reader, source):
        beside = (source >= (per - 1) * C) & (source <= per + (n - per - 1) * C)
        return beside | (source == reader - 1) | (source == reader + 1)

    embs = []
    for k in range(1, n):
        reader, source = lax.rem(R + k, n), lax.rem(R + n - k, n)
        copy = remote(eb.at[R], eb.at[R], esend.at[k - 1], erecv.at[k - 1], reader, C)
        embs.append((copy, needs(reader, R), needs(R, source)))
        pl.when(embs[-1][1])(copy.start)

    own_src = pk.at[1, :, pl.ds(own_at, cols), :]
    side_src = pk.at[1, :, pl.ds(pl.multiple_of(cols - SIDE - (cols - 2 * SIDE) * C, SIDE), SIDE), :]
    side_at = pl.ds(pl.multiple_of(cols * C, SIDE), SIDE)
    above = jnp.maximum(R - 1, 0)
    below = jnp.minimum(R + 1, n - 1)
    to_below = remote(
        own_src, pk.at[0, :, pl.ds(own_at, cols), :], send.at[0], recv.at[0], below, C
    )
    to_above = remote(
        own_src, pk.at[2, :, pl.ds(own_at, cols), :], send.at[1], recv.at[1], above, C
    )
    to_side = remote(side_src, pk.at[1, :, side_at, :], send.at[2], recv.at[2], R, O)
    side_below = remote(side_src, pk.at[0, :, side_at, :], send.at[3], recv.at[3], below, O)
    side_above = remote(side_src, pk.at[2, :, side_at, :], send.at[4], recv.at[4], above, O)

    @pl.when(R < n - 1)
    def _():
        to_below.start()
        side_below.start()

    @pl.when(R > 0)
    def _():
        to_above.start()
        side_above.start()

    to_side.start()

    def spread_rows(y, phases):
        top, bottom = y[:big], y[big:]
        first = [jnp.where(phases == p, top, 0.0) for p in range(PHASES)]
        second = [jnp.where(phases == p, bottom, 0.0) for p in range(PHASES)]
        return (
            jnp.concatenate(first, axis=0).astype(bf),
            jnp.concatenate(second, axis=0).astype(bf),
        )

    def pack_weight(w_ref, across, phases, dst):
        for a in range(3):
            at = a * TAPS
            for b in range(3):
                first, second = spread_rows(mm(w_ref[a, b], across), phases)
                dst[at + b * LANES : at + (b + 1) * LANES, :] = first
                low = at + 3 * LANES + (0, LANES, HALF)[b]
                dst[low : low + HALF, :] = second
            dst[at + TAPS - HALF : at + TAPS, :] = jnp.zeros((HALF, WIDE), bf)

    exact = lax.Precision.HIGHEST
    for load in loads[2:]:
        load.wait()
    pack_weight(w1_ref, spread.astype(bf), phase_of, wa)
    half_mix = mm(wm_ref[...], spread4) * 0.5
    mix = half_mix.astype(bf)
    pack_weight(w2_ref, mix, phase4_of, wb)
    first, second = spread_rows(half_mix, phase4_of)
    wb[3 * TAPS : 3 * TAPS + LANES, :] = first
    wb[3 * TAPS + LANES : 3 * TAPS + LANES + HALF, :] = second
    wb[3 * TAPS + LANES + HALF :, :] = jnp.zeros((HALF, WIDE), bf)
    bias1 = mm(b1_ref[...], spread, exact)
    bias2 = mm(b2_ref[...], half_mix, exact) + 0.5 * mm(bm_ref[...], spread4.astype(f32), exact)
    head = mm(wh_ref[...], spread4[:, :LANES].astype(f32), exact)
    wr = mm_tn(wr_ref[...], spread.astype(bf)).astype(bf)
    wc = mm_tn(wc_ref[...], spread.astype(bf)).astype(bf)

    for copy, _, arrives in embs:
        pl.when(arrives)(copy.wait_recv)
    for k in range(n):
        ct[k * rows : (k + 1) * rows, :] = mm(eb[k], wc)
    col_terms = ct[pl.ds(pl.multiple_of((n * rows - width) * C, 8), width), :]

    def row_terms(b):
        terms = mm(eb[jnp.clip(R + b - 1, 0, n - 1)], wr)
        out = []
        for g in range(groups):
            total = terms[PHASES * g : PHASES * g + 1]
            for p in range(1, PHASES):
                total = jnp.where(phase_of == p, terms[PHASES * g + p : PHASES * g + p + 1], total)
            out.append(total)
        return out

    col_id = lax.broadcasted_iota(jnp.int32, (width, 1), 0)

    def before(v, d):
        return jnp.where(col_id < d, 0.0, pltpu.roll(v, d, axis=0))

    def after(v, d):
        return jnp.where(col_id >= width - d, 0.0, pltpu.roll(v, width - d, axis=0))

    def put_taps(dst, at, x, y, d):
        dst[at, :, :LANES] = before(x, d).astype(bf)
        dst[at, :, LANES : 2 * LANES] = x.astype(bf)
        dst[at, :, 2 * LANES : 3 * LANES] = after(x, d).astype(bf)
        dst[at, :, 3 * LANES : 4 * LANES] = jnp.where(lower, before(y, d), after(y, d)).astype(bf)
        dst[at, :, 4 * LANES :] = y.astype(bf)

    def base_block(b, valid):
        terms = row_terms(b)
        seconds = []
        for t in range(blocks - groups):
            g = 2 * t
            mine = terms[g][:, LANES:]
            if g + 1 < groups:
                mine = jnp.where(lower, mine, terms[g + 1][:, LANES:])
            v = (pk[b, groups + t].astype(f32) + mine + col_terms[:, LANES:]).astype(bf).astype(f32)
            turned = pltpu.roll(v, HALF, axis=1)
            seconds.append(jnp.where(lower, v, turned))
            seconds.append(jnp.where(lower, turned, v))
        for g in range(groups):
            x = pk[b, g].astype(f32) + terms[g][:, :LANES] + col_terms[:, :LANES]
            x, y = x.astype(bf).astype(f32), seconds[g]
            if valid is not None:
                x, y = jnp.where(valid, x, 0.0), jnp.where(valid, y, 0.0)
            at = b * groups + g
            xb[at, :, :LANES] = x.astype(bf)
            xb[at, :, LANES:] = y.astype(bf)
            put_taps(xs, at, jnp.maximum(x, 0.0), jnp.maximum(y, 0.0), FIRST_DILATION)

    to_side.wait()
    base_block(1, None)

    @pl.when(R > 0)
    def _():
        to_below.wait_recv()
        side_below.wait_recv()

    @pl.when(R < n - 1)
    def _():
        to_above.wait_recv()
        side_above.wait_recv()

    base_block(0, R > 0)
    base_block(2, R < n - 1)

    step = FIRST_DILATION // PHASES
    step2 = SECOND_DILATION // PHASES
    ext = groups + 2 * step2
    skip = groups - step2 - step
    left = jnp.concatenate(
        [
            xs[skip + a * step : skip + a * step + ext].reshape(ext * width, TAPS)
            for a in range(3)
        ],
        axis=1,
    )
    acc = mm(left, wa[...]).reshape(ext, width, WIDE)
    for u in range(ext):
        x = (xb[u + skip + step].astype(f32) + acc[u] + bias1).astype(bf).astype(f32)
        if u < step2:
            x = jnp.where(R > 0, x, 0.0)
        elif u >= step2 + groups:
            x = jnp.where(R < n - 1, x, 0.0)
        else:
            l1[u - step2] = x.astype(bf)
        x = jnp.maximum(x, 0.0)
        put_taps(xs2, u, x[:, :LANES], x[:, LANES:], SECOND_DILATION)

    window = pl.ds(own_at, cols)
    left = [
        xs2[a * step2 : a * step2 + groups, window, :].reshape(groups * cols, TAPS)
        for a in range(3)
    ]
    left.append(l1[:, window, :].reshape(groups * cols, WIDE))
    mixed = (mm(jnp.concatenate(left, axis=1), wb[...]) + bias2).reshape(groups, cols, WIDE)

    def row_of(i):
        g, p = divmod(i, PHASES)
        at = p // 2 * LANES
        return mixed[g, :, at : at + LANES], p % 2

    for i in range(hr):
        (first, at), (second, _) = row_of(i), row_of(i + hr)
        if at == 0:
            second = pltpu.roll(second, HALF, axis=1)
        else:
            first = pltpu.roll(first, HALF, axis=1)
        pair = jnp.where(lower, first, second)
        yp[i] = pair
        for j in range(per):
            sf[j, i * rows : (i + 1) * rows, :] = pair[j * rows : (j + 1) * rows, :]
    used = hr * rows
    for j in range(per):
        sb[j, :used] = sf[j].astype(bf)

    mine = lax.rem(R, per)
    quarter = lax.div(R, per)
    for j in range(per):
        peer = per * C + j
        is_self = (peer == R) & (quarter == C)
        copy = remote(sb.at[j], gb.at[mine], msend.at[j], mrecv.at[mine], peer, quarter)
        local = pltpu.make_async_copy(sb.at[j], gb.at[j], lsem)

        @pl.when(jnp.logical_not(is_self))
        def _():
            copy.start()

        @pl.when(is_self)
        def _():
            local.start()

    early = lax.broadcasted_iota(jnp.int32, (used, 1), 0) % rows < hr
    for j in range(per):
        peer = per * C + j
        is_self = (peer == R) & (quarter == C)
        arrival = remote(sb.at[j], gb.at[j], msend.at[j], mrecv.at[j], peer, quarter)
        local = pltpu.make_async_copy(sb.at[j], gb.at[j], lsem)

        @pl.when(jnp.logical_not(is_self))
        def _():
            arrival.wait_recv()

        @pl.when(is_self)
        def _():
            local.wait()

        piece = gb[j, :used].astype(f32)
        turned = pltpu.roll(piece, HALF, axis=1)
        at = 2 * j * used
        tb[at : at + used, :] = jnp.where(early, piece, turned)
        tb[at + used : at + 2 * used, :] = jnp.where(early, turned, piece)

    halves = jnp.where(
        lax.broadcasted_iota(jnp.int32, (8, LANES), 1) // HALF
        == lax.broadcasted_iota(jnp.int32, (8, LANES), 0),
        1.0,
        0.0,
    ).astype(bf)
    for i in range(hr):
        mirror = jnp.where(
            lower, tb[pl.ds(i, cols, stride=rows), :], tb[pl.ds(i + hr, cols, stride=rows), :]
        )
        z = jnp.maximum(yp[i] + mirror, 0.0) * head
        top = z.astype(bf)
        rest = (z - top.astype(f32)).astype(bf)
        sums = mm_nt(halves, top) + mm_nt(halves, rest)
        out_ref[i : i + 1, :] = sums[0:1]
        out_ref[i + hr : i + hr + 1, :] = sums[1:2]

    @pl.when(R < n - 1)
    def _():
        to_below.wait_send()
        side_below.wait_send()

    @pl.when(R > 0)
    def _():
        to_above.wait_send()
        side_above.wait_send()

    for copy, leaves, _ in embs:
        pl.when(leaves)(copy.wait_send)

    for j in range(per):
        peer = per * C + j
        is_self = (peer == R) & (quarter == C)
        departure = remote(sb.at[j], gb.at[j], msend.at[j], mrecv.at[j], peer, quarter)

        @pl.when(jnp.logical_not(is_self))
        def _():
            departure.wait_send()


def fused(map_in, embedding, w_row, w_col, w1, b1, w2, b2, w_mix, b_mix, w_head):
    rows, cols, ch = map_in.shape
    n = lax.axis_size("row")
    width, per, hr, groups = cols + SIDE, cols // rows, rows // 2, rows // PHASES
    blocks = groups + (groups + 1) // 2
    ext = groups + 2 * SECOND_DILATION // PHASES
    used = hr * rows
    held = -(-used // 16) * 16
    bf, f32 = jnp.bfloat16, jnp.float32
    dma = pltpu.SemaphoreType.DMA
    operands = (
        map_in,
        embedding,
        w_row.T,
        w_col.T,
        w1,
        b1.reshape(1, ch),
        w2,
        b2.reshape(1, ch),
        w_mix,
        b_mix.reshape(1, ch),
        w_head.reshape(1, ch),
    )
    return pl.pallas_call(
        functools.partial(fused_kernel, n),
        out_shape=pltpu.VMEM((rows, cols), f32),
        in_specs=[pl.BlockSpec(memory_space=pl.ANY)] * 11,
        out_specs=pl.BlockSpec(memory_space=pltpu.VMEM),
        scratch_shapes=[
            pltpu.VMEM((3, blocks, width, LANES), bf),
            pltpu.VMEM((n, rows, embedding.shape[1]), bf),
            pltpu.VMEM((n * rows, WIDE), f32),
            pltpu.VMEM((3 * groups, width, WIDE), bf),
            pltpu.VMEM((3 * groups, width, TAPS), bf),
            pltpu.VMEM((groups, width, WIDE), bf),
            pltpu.VMEM((ext, width, TAPS), bf),
            pltpu.VMEM((3 * TAPS, WIDE), bf),
            pltpu.VMEM((3 * TAPS + WIDE, WIDE), bf),
            pltpu.VMEM((hr, cols, LANES), f32),
            pltpu.VMEM((per, used, LANES), f32),
            pltpu.VMEM((per, held, LANES), bf),
            pltpu.VMEM((per, held, LANES), bf),
            pltpu.VMEM((cols * rows, LANES), f32),
            dma((5,)),
            dma((5,)),
            dma((n - 1,)),
            dma((n - 1,)),
            dma((per,)),
            dma((per,)),
            dma,
            dma((11,)),
            *[pltpu.VMEM(x.shape, x.dtype) for x in operands],
        ],
        compiler_params=pltpu.CompilerParams(collective_id=0, has_side_effects=True),
    )(*operands)


def fits(rows, cols, channels, row_count, col_count):
    held = 2 * (cols + SIDE) * (3 * rows // PHASES) * (2 * TAPS + 2 * WIDE)
    weights = 2 * WIDE * (6 * TAPS + WIDE)
    halo = FIRST_DILATION + SECOND_DILATION
    return (
        held + weights <= FUSED_VMEM
        and rows == halo
        and col_count == 2
        and cols % SIDE == 0
        and channels == 48
        and cols * col_count == rows * row_count
    )


def on_device(
    map_in,
    embedding,
    w_row,
    w_col,
    first_kernel_weight,
    first_bias,
    second_kernel_weight,
    second_bias,
    w_mix,
    b_mix,
    w_head,
):
    patch_rows, patch_columns, channels = map_in.shape
    row_count = lax.axis_size("row")
    if fits(patch_rows, patch_columns, channels, row_count, lax.axis_size("col")):
        return fused(
            map_in,
            embedding,
            w_row,
            w_col,
            first_kernel_weight,
            first_bias,
            second_kernel_weight,
            second_bias,
            w_mix,
            b_mix,
            w_head,
        )
    row_at = lax.axis_index("row")
    col_at = lax.axis_index("col")
    all_bins = lax.all_gather(embedding, "row", axis=0, tiled=True)
    row_terms = jnp.dot(all_bins, w_row, preferred_element_type=jnp.float32)
    col_terms = jnp.dot(all_bins, w_col, preferred_element_type=jnp.float32)
    own_rows = lax.dynamic_slice_in_dim(row_terms, row_at * patch_rows, patch_rows, 0)
    own_cols = lax.dynamic_slice_in_dim(col_terms, col_at * patch_columns, patch_columns, 0)
    contact_grid = (
        map_in.astype(jnp.float32) + own_rows[:, None, :] + own_cols[None, :, :]
    ).astype(jnp.bfloat16)
    first_padded = padded(contact_grid, (("row", 0), ("col", 1)), FIRST_DILATION)
    first_layer = (
        contact_grid.astype(jnp.float32)
        + dilated_conv(
            jnp.maximum(first_padded, 0),
            first_kernel_weight,
            FIRST_DILATION,
            patch_rows,
            patch_columns,
        )
        + first_bias
    ).astype(jnp.bfloat16)
    second_padded = padded(first_layer, (("row", 0), ("col", 1)), SECOND_DILATION)
    second_layer = (
        first_layer.astype(jnp.float32)
        + dilated_conv(
            jnp.maximum(second_padded, 0),
            second_kernel_weight,
            SECOND_DILATION,
            patch_rows,
            patch_columns,
        )
        + second_bias
    ).astype(jnp.bfloat16)
    half_rows = patch_rows // 2
    blocks_per = row_count // 2
    arranged = second_layer.reshape(2, half_rows, blocks_per, patch_rows, channels)
    arranged = arranged.transpose(0, 2, 1, 3, 4).reshape(
        2 * blocks_per, half_rows, patch_rows, channels
    )
    exchanged = lax.all_to_all(
        lax.all_to_all(arranged, "row", split_axis=0, concat_axis=0, tiled=True),
        "col",
        split_axis=0,
        concat_axis=0,
        tiled=True,
    )
    exchanged = exchanged.reshape(2, blocks_per, half_rows, patch_rows, channels)
    top_half = row_at // blocks_per
    kept_part = lax.dynamic_index_in_dim(exchanged, top_half, 0, keepdims=False)
    sent_part = lax.dynamic_index_in_dim(exchanged, 1 - top_half, 0, keepdims=False)
    came_back = swapped(sent_part, "row", blocks_per.bit_length() - 1)
    stacked = jnp.where(
        top_half == 0, jnp.stack([kept_part, came_back]), jnp.stack([came_back, kept_part])
    )
    mirrored = stacked.transpose(3, 1, 0, 2, 4).reshape(patch_rows, patch_columns, channels)
    symmetric = ((second_layer.astype(jnp.float32) + mirrored.astype(jnp.float32)) * 0.5).astype(
        jnp.bfloat16
    )
    mixture = (
        jnp.einsum("rch,hk->rck", symmetric, w_mix, preferred_element_type=jnp.float32) + b_mix
    )
    mixture = jnp.maximum(mixture, 0.0)
    return jnp.sum(mixture * w_head, axis=-1)


def solution(mesh):
    placed = (
        P(("group", "row"), "col", None),
        P(("group", "row"), None),
        P(),
        P(),
        P(),
        P(),
        P(),
        P(),
        P(),
        P(),
        P(),
    )
    return jax.shard_map(
        on_device, mesh=mesh, in_specs=placed, out_specs=P(("group", "row"), "col"), check_vma=False
    )
```

```python
import functools

import jax
import jax.numpy as jnp
from jax import lax
from jax.experimental import pallas as pl
from jax.experimental.pallas import tpu as pltpu
from jax.sharding import PartitionSpec as P

FIRST_DILATION = 4
SECOND_DILATION = 8


def padded(array, sides, width):
    for axis, dim in sides:
        peers, length = (lax.axis_size(axis), array.shape[dim])
        up = [(i, (i + 1) % peers) for i in range(peers - 1)]
        down = [(j, i) for i, j in up]
        last = lax.slice_in_dim(array, length - width, length, axis=dim)
        leading = lax.slice_in_dim(array, 0, width, axis=dim)
        before = lax.ppermute(last, axis, up)
        after = lax.ppermute(leading, axis, down)
        array = jnp.concatenate([before, array, after], axis=dim)
    return array


def swapped(value, axis, bit):
    mask = 2**bit
    pairs = [(source, source ^ mask) for source in range(lax.axis_size(axis))]
    return lax.ppermute(value, axis, pairs)


def dilated_conv(active, weight, spacing, out_rows, out_cols):
    windows = []
    for tap_row in range(3):
        for tap_col in range(3):
            windows.append(
                active[
                    tap_row * spacing : tap_row * spacing + out_rows,
                    tap_col * spacing : tap_col * spacing + out_cols,
                ]
            )
    stacked = jnp.concatenate(windows, axis=-1)
    flat_weight = weight.reshape(9 * weight.shape[2], weight.shape[3])
    return jnp.einsum("rch,hk->rck", stacked, flat_weight, preferred_element_type=jnp.float32)


LANES = 128
HALF = 64
SIDE = 16
PHASES = 4
WIDE = 2 * LANES
TAPS = 5 * LANES
FUSED_VMEM = 8 * 2**20


def one_hot(rows, columns, offsets):
    r = lax.broadcasted_iota(jnp.int32, (rows, columns), 0)
    c = lax.broadcasted_iota(jnp.int32, (rows, columns), 1)
    hit = c == r + offsets[0]
    for offset in offsets[1:]:
        hit = hit | (c == r + offset)
    return jnp.where(hit, 1.0, 0.0)


def mm(a, b, precision=None):
    return jnp.dot(a, b, preferred_element_type=jnp.float32, precision=precision)


def mm_tn(a, b):
    return lax.dot_general(a, b, (((0,), (0,)), ((), ())), preferred_element_type=jnp.float32)


def mm_nt(a, b):
    return lax.dot_general(a, b, (((1,), (1,)), ((), ())), preferred_element_type=jnp.float32)


def fused_kernel(
    n,
    m_hbm,
    e_hbm,
    wr_hbm,
    wc_hbm,
    w1_hbm,
    b1_hbm,
    w2_hbm,
    b2_hbm,
    wm_hbm,
    bm_hbm,
    wh_hbm,
    out_ref,
    pk,
    eb,
    ct,
    xb,
    xs,
    l1,
    xs2,
    wa,
    wb,
    yp,
    sf,
    sb,
    gb,
    tb,
    send,
    recv,
    esend,
    erecv,
    msend,
    mrecv,
    mcred,
    hcred,
    ncred,
    ocred,
    qcred,
    lsem,
    isem,
    m_ref,
    e_ref,
    wr_ref,
    wc_ref,
    w1_ref,
    b1_ref,
    w2_ref,
    b2_ref,
    wm_ref,
    bm_ref,
    wh_ref,
):
    bf, f32 = jnp.bfloat16, jnp.float32
    rows, cols, ch = m_ref.shape
    hr = rows // 2
    groups = rows // PHASES
    blocks = pk.shape[1]
    width = cols + SIDE
    per = cols // rows
    big = LANES // PHASES
    small = ch - big
    R = lax.axis_index("row")
    C = lax.axis_index("col")
    O = 1 - C
    group = lax.axis_index("group")
    mesh_type = pl.DeviceIdType.MESH

    eb[...] = jnp.zeros_like(eb)
    quarter = lax.div(R, per)
    mine = lax.rem(R, per)
    odd = lax.rem(R, 2)
    hub = per - C
    across, slant = R + 1 - 2 * odd, R - 1 + 2 * odd
    slants = (slant >= 0) & (slant < n)
    slant = jnp.clip(slant, 0, n - 1)
    beside = ((across, None), (slant, slants))
    barrier = pltpu.get_barrier_semaphore()

    def signal(sem, row, col):
        pl.semaphore_signal(sem, inc=1, device_id=(group, row, col), device_id_type=mesh_type)

    def when(condition, act, *args):
        if condition is None:
            act(*args)
        else:
            pl.when(condition)(functools.partial(act, *args))

    def both(a, b):
        return a if b is None else a & b

    def one(condition):
        return jnp.where(condition, 1, 0)

    def far(peer):
        return (peer != R) & ((quarter != C) | (peer - R >= 2) | (R - peer >= 2))

    at_relay = (R == per) & (C == 1)
    fed = (R >= per) & (C == 0)

    def is_relay(row, col):
        return (row == per) & (col == 1)

    greeted = 0
    for row in range(n):
        apart = (row - R >= 2) | (R - row >= 2)
        pair = apart & jnp.where(C == 0, (jnp.maximum(row, R) == per), (row == hub) | (R == hub))
        when(pair & (row > R), signal, barrier, row, C)
        greeted += one(pair & (row < R))
        if row > per:
            when(at_relay, signal, barrier, row, 0)
        if row < per - 1:
            when(at_relay, signal, barrier, row, 1)
    feeds = (C == 1) & (R < per - 1)
    greeted += one(((C == 0) & (R > per)) | feeds)
    for j in range(per):
        peer = per * C + j
        when(far(peer) & (peer > R), signal, barrier, peer, quarter)
        greeted += one(far(peer) & (peer < R))
    for row, there in beside:
        when(both(jnp.logical_not(is_relay(row, C)), there), signal, barrier, row, C)
        greeted += one(both(jnp.logical_not(at_relay), there))
    when(jnp.logical_not(is_relay(R, O)), signal, barrier, R, O)
    greeted += one(jnp.logical_not(at_relay))

    inputs = (
        (m_hbm, m_ref),
        (e_hbm, e_ref),
        (wr_hbm, wr_ref),
        (wc_hbm, wc_ref),
        (w1_hbm, w1_ref),
        (b1_hbm, b1_ref),
        (w2_hbm, w2_ref),
        (b2_hbm, b2_ref),
        (wm_hbm, wm_ref),
        (bm_hbm, bm_ref),
        (wh_hbm, wh_ref),
    )
    loads = [pltpu.make_async_copy(a, b, isem.at[i]) for i, (a, b) in enumerate(inputs)]
    for load in loads:
        load.start()

    h_at = lax.broadcasted_iota(jnp.int32, (ch, WIDE), 0)
    l_at = lax.broadcasted_iota(jnp.int32, (ch, WIDE), 1)
    in_big = l_at < LANES
    spread = jnp.where(
        jnp.where(in_big, l_at % big, big + l_at % small) == h_at, 1.0, 0.0
    )
    lanes = lax.broadcasted_iota(jnp.int32, (1, WIDE), 1)
    phase_of = jnp.where(lanes < LANES, lanes // big, (lanes % HALF) // small)
    spread4 = jnp.where(l_at % HALF == h_at, 1.0, 0.0).astype(bf)
    phase4_of = lanes // HALF
    lane = lax.broadcasted_iota(jnp.int32, (1, LANES), 1)
    lower = lane < HALF

    def remote(src, dst, s, r, row, col):
        return pltpu.make_async_remote_copy(
            src_ref=src,
            dst_ref=dst,
            send_sem=s,
            recv_sem=r,
            device_id=(group, row, col),
            device_id_type=mesh_type,
        )

    def embed(slot, row, col):
        return remote(e_hbm, eb.at[R], esend.at[slot], erecv.at[R], row, col)

    when(greeted > 0, pl.semaphore_wait, barrier, greeted)
    when((C == 1) & (R > hub + 1), signal, hcred, hub, C)
    when((C == 0) & (R > per), signal, qcred, per, 1)
    for k, (row, there) in enumerate(beside):
        when(both(is_relay(row, C), there), signal, ncred.at[k], row, C)
    when(is_relay(R, O), signal, ocred, R, O)
    embs, late = [], []
    ahead = 0
    for j in range(per):
        peer = per * C + j
        when(far(peer) & (peer < R), signal, mcred, peer, quarter)
        copy = embed(j, peer, quarter)
        wanted = far(peer) & (quarter >= C)
        embs.append((wanted, copy))
        when(wanted & (peer < R), copy.start)
        late.append((wanted & (peer > R), copy))
        ahead += one(far(peer) & (peer > R))
    ahead_hub = jnp.where((C == 1) & (R == hub), n - 2 - R, 0)
    for row in range(n):
        apart = (row - R >= 2) | (R - row >= 2)
        slot = per + 2 + jnp.where(row < R, row, row - 3)
        copy = embed(jnp.clip(slot, 0, per + 6), row, C)
        wanted = (R == hub) & apart & ((C == 1) | (row < R))
        embs.append((wanted, copy))
        when(wanted & (row < R), copy.start)
        late.append((wanted & (row > R), copy))
    to_relay = embed(per + 2, per, 1)
    embs.append((feeds, to_relay))
    when(feeds, to_relay.start)
    for k, (row, there) in enumerate(beside):
        copy = embed(per + k, row, C)
        wanted = (quarter != C) | (lax.div(row, per) == quarter)
        wanted = both(wanted & ((C == 1) | (R != per) | (row < R)), there)
        embs.append((wanted, copy))
        when(wanted & jnp.logical_not(at_relay), copy.start)

    own_at = pl.multiple_of(SIDE * C, SIDE)
    placed = [jnp.where(phase_of == p, spread, 0.0).astype(bf) for p in range(PHASES)]
    loads[0].wait()
    tile = m_ref[...].reshape(groups, PHASES, cols, ch)
    packed = mm(tile[:, 0].reshape(groups * cols, ch), placed[0])
    for p in range(1, PHASES):
        packed = packed + mm(tile[:, p].reshape(groups * cols, ch), placed[p])
    packed = packed.reshape(groups, cols, WIDE)
    for g in range(groups):
        pk[1, g, pl.ds(own_at, cols), :] = packed[g, :, :LANES].astype(bf)
    for t in range(blocks - groups):
        piece = packed[2 * t, :, LANES:]
        if 2 * t + 1 < groups:
            piece = jnp.where(lower, piece, packed[2 * t + 1, :, LANES:])
        pk[1, groups + t, pl.ds(own_at, cols), :] = piece.astype(bf)
    edge = pl.ds(pl.multiple_of(cols - SIDE - (cols - 2 * SIDE) * C, SIDE), SIDE)
    rest = pl.ds(pl.multiple_of(2 * SIDE * C, SIDE), cols - SIDE)
    side_at = pl.ds(pl.multiple_of(cols * C, SIDE), SIDE)
    halos = []
    for k, (row, there) in enumerate(beside):
        block = 2 * odd if k == 0 else 2 * (1 - odd)
        for at, part in enumerate((edge, rest)):
            slot = 2 * k + at
            halos.append(
                remote(
                    pk.at[1, :, part, :],
                    pk.at[block, :, part, :],
                    send.at[slot],
                    recv.at[slot],
                    row,
                    C,
                )
            )
    for k, (row, there) in enumerate(beside):
        when(both(at_relay, there), pl.semaphore_wait, ncred.at[k], 1)
        when(embs[k - 2][0] & at_relay, embs[k - 2][1].start)
        when(there, halos[2 * k].start)
        when(there, halos[2 * k + 1].start)
    to_side = remote(pk.at[1, :, edge, :], pk.at[1, :, side_at, :], send.at[4], recv.at[4], R, O)
    when(at_relay, pl.semaphore_wait, ocred, 1)
    to_side.start()

    def arrival(row):
        return remote(e_hbm, eb.at[row], esend.at[0], erecv.at[row], row, C)

    loads[1].wait()

    @pl.when(jnp.logical_not((C == 0) & (R == per)))
    def _():
        eb[R] = e_ref[...]

    bundles = []
    for row in range(per, n):
        whole = eb.at[pl.ds(0, per + 1)]
        bundles.append(remote(whole, whole, esend.at[per + 2 + row - per], erecv.at[0], row, 0))

    @pl.when(at_relay)
    def _():
        for row in range(per):
            arrival(row).wait_recv()
        pl.semaphore_wait(qcred, n - 1 - per)
        for copy in bundles[::-1]:
            copy.start()

    when(ahead > 0, pl.semaphore_wait, mcred, ahead)
    when(ahead_hub > 0, pl.semaphore_wait, hcred, ahead_hub)
    for waits, copy in late:
        when(waits, copy.start)

    def spread_rows(y, phases):
        top, bottom = y[:big], y[big:]
        first = [jnp.where(phases == p, top, 0.0) for p in range(PHASES)]
        second = [jnp.where(phases == p, bottom, 0.0) for p in range(PHASES)]
        return (
            jnp.concatenate(first, axis=0).astype(bf),
            jnp.concatenate(second, axis=0).astype(bf),
        )

    def pack_weight(w_ref, across, phases, dst):
        for a in range(3):
            at = a * TAPS
            for b in range(3):
                first, second = spread_rows(mm(w_ref[a, b], across), phases)
                dst[at + b * LANES : at + (b + 1) * LANES, :] = first
                low = at + 3 * LANES + (0, LANES, HALF)[b]
                dst[low : low + HALF, :] = second
            dst[at + TAPS - HALF : at + TAPS, :] = jnp.zeros((HALF, WIDE), bf)

    exact = lax.Precision.HIGHEST
    for load in loads[2:]:
        load.wait()
    pack_weight(w1_ref, spread.astype(bf), phase_of, wa)
    half_mix = mm(wm_ref[...], spread4) * 0.5
    mix = half_mix.astype(bf)
    pack_weight(w2_ref, mix, phase4_of, wb)
    first, second = spread_rows(half_mix, phase4_of)
    wb[3 * TAPS : 3 * TAPS + LANES, :] = first
    wb[3 * TAPS + LANES : 3 * TAPS + LANES + HALF, :] = second
    wb[3 * TAPS + LANES + HALF :, :] = jnp.zeros((HALF, WIDE), bf)
    bias1 = mm(b1_ref[...], spread, exact)
    bias2 = mm(b2_ref[...], half_mix, exact) + 0.5 * mm(bm_ref[...], spread4.astype(f32), exact)
    head = mm(wh_ref[...], spread4[:, :LANES].astype(f32), exact)
    wr = mm_tn(wr_ref[...], spread.astype(bf)).astype(bf)
    wc = mm_tn(wc_ref[...], spread.astype(bf)).astype(bf)

    relays = []
    for k, (row, there) in enumerate(beside):
        block = 2 * (1 - odd) if k == 0 else 2 * odd
        copy = remote(
            pk.at[block, :, edge, :],
            pk.at[block, :, side_at, :],
            send.at[5 + k],
            recv.at[5 + k],
            R,
            O,
        )
        relays.append((there, copy))
        when(there, halos[2 * k].wait_recv)
        when(there, copy.start)

    when(fed, bundles[0].wait_recv)
    for row in range(n):
        first = (per - 1) * C
        read = (row >= first) & (row <= first + per) & (row != R)
        read |= (row == R - 1) | (row == R + 1)
        read &= jnp.logical_not(fed & (row <= per))
        read &= jnp.logical_not(at_relay & (row < per))
        when(read, arrival(row).wait_recv)
    to_side.wait_recv()
    for k, (there, copy) in enumerate(relays):
        when(there, halos[2 * k + 1].wait_recv)
        when(there, copy.wait_recv)

    for k in range(n):
        ct[k * rows : (k + 1) * rows, :] = mm(eb[k], wc)
    col_terms = ct[pl.ds(pl.multiple_of((n * rows - width) * C, 8), width), :]

    def row_terms(b):
        terms = mm(eb[jnp.clip(R + b - 1, 0, n - 1)], wr)
        out = []
        for g in range(groups):
            total = terms[PHASES * g : PHASES * g + 1]
            for p in range(1, PHASES):
                total = jnp.where(phase_of == p, terms[PHASES * g + p : PHASES * g + p + 1], total)
            out.append(total)
        return out

    col_id = lax.broadcasted_iota(jnp.int32, (width, 1), 0)

    def before(v, d):
        return jnp.where(col_id < d, 0.0, pltpu.roll(v, d, axis=0))

    def after(v, d):
        return jnp.where(col_id >= width - d, 0.0, pltpu.roll(v, width - d, axis=0))

    def put_taps(dst, at, x, y, d):
        dst[at, :, :LANES] = before(x, d).astype(bf)
        dst[at, :, LANES : 2 * LANES] = x.astype(bf)
        dst[at, :, 2 * LANES : 3 * LANES] = after(x, d).astype(bf)
        dst[at, :, 3 * LANES : 4 * LANES] = jnp.where(lower, before(y, d), after(y, d)).astype(bf)
        dst[at, :, 4 * LANES :] = y.astype(bf)

    def base_block(b, valid):
        terms = row_terms(b)
        seconds = []
        for t in range(blocks - groups):
            g = 2 * t
            term = terms[g][:, LANES:]
            if g + 1 < groups:
                term = jnp.where(lower, term, terms[g + 1][:, LANES:])
            v = (pk[b, groups + t].astype(f32) + term + col_terms[:, LANES:]).astype(bf).astype(f32)
            turned = pltpu.roll(v, HALF, axis=1)
            seconds.append(jnp.where(lower, v, turned))
            seconds.append(jnp.where(lower, turned, v))
        for g in range(groups):
            x = pk[b, g].astype(f32) + terms[g][:, :LANES] + col_terms[:, :LANES]
            x, y = x.astype(bf).astype(f32), seconds[g]
            if valid is not None:
                x, y = jnp.where(valid, x, 0.0), jnp.where(valid, y, 0.0)
            at = b * groups + g
            xb[at, :, :LANES] = x.astype(bf)
            xb[at, :, LANES:] = y.astype(bf)
            put_taps(xs, at, jnp.maximum(x, 0.0), jnp.maximum(y, 0.0), FIRST_DILATION)

    step = FIRST_DILATION // PHASES
    step2 = SECOND_DILATION // PHASES
    ext = groups + 2 * step2
    skip = groups - step2 - step

    def first_layer(start, stop):
        left = jnp.concatenate(
            [
                xs[start + skip + a * step : stop + skip + a * step].reshape(-1, TAPS)
                for a in range(3)
            ],
            axis=1,
        )
        acc = mm(left, wa[...]).reshape(stop - start, width, WIDE)
        for u in range(start, stop):
            x = xb[u + skip + step].astype(f32) + acc[u - start] + bias1
            x = x.astype(bf).astype(f32)
            if u < step2:
                x = jnp.where(R > 0, x, 0.0)
            elif u >= step2 + groups:
                x = jnp.where(R < n - 1, x, 0.0)
            else:
                l1[u - step2] = x.astype(bf)
            x = jnp.maximum(x, 0.0)
            put_taps(xs2, u, x[:, :LANES], x[:, LANES:], SECOND_DILATION)

    base_block(1, None)
    base_block(0, R > 0)
    base_block(2, R < n - 1)
    cut = ext - step2
    first_layer(0, cut)
    first_layer(cut, ext)

    window = pl.ds(own_at, cols)
    left = [
        xs2[a * step2 : a * step2 + groups, window, :].reshape(groups * cols, TAPS)
        for a in range(3)
    ]
    left.append(l1[:, window, :].reshape(groups * cols, WIDE))
    mixed = (mm(jnp.concatenate(left, axis=1), wb[...]) + bias2).reshape(groups, cols, WIDE)

    def row_of(i):
        g, p = divmod(i, PHASES)
        at = p // 2 * LANES
        return mixed[g, :, at : at + LANES], p % 2

    for i in range(hr):
        (first, at), (second, _) = row_of(i), row_of(i + hr)
        if at == 0:
            second = pltpu.roll(second, HALF, axis=1)
        else:
            first = pltpu.roll(first, HALF, axis=1)
        pair = jnp.where(lower, first, second)
        yp[i] = pair
        for j in range(per):
            sf[j, i * rows : (i + 1) * rows, :] = pair[j * rows : (j + 1) * rows, :]
    used = hr * rows
    for j in range(per):
        sb[j, :used] = sf[j].astype(bf)

    for j in range(per):
        peer = per * C + j
        is_self = (peer == R) & (quarter == C)
        copy = remote(sb.at[j], gb.at[mine], msend.at[j], mrecv.at[mine], peer, quarter)
        local = pltpu.make_async_copy(sb.at[j], gb.at[j], lsem)

        @pl.when(jnp.logical_not(is_self))
        def _():
            copy.start()

        @pl.when(is_self)
        def _():
            local.start()

    early = lax.broadcasted_iota(jnp.int32, (used, 1), 0) % rows < hr
    for j in range(per):
        peer = per * C + j
        is_self = (peer == R) & (quarter == C)
        arrival = remote(sb.at[j], gb.at[j], msend.at[j], mrecv.at[j], peer, quarter)
        local = pltpu.make_async_copy(sb.at[j], gb.at[j], lsem)

        @pl.when(jnp.logical_not(is_self))
        def _():
            arrival.wait_recv()

        @pl.when(is_self)
        def _():
            local.wait()

        piece = gb[j, :used].astype(f32)
        turned = pltpu.roll(piece, HALF, axis=1)
        at = 2 * j * used
        tb[at : at + used, :] = jnp.where(early, piece, turned)
        tb[at + used : at + 2 * used, :] = jnp.where(early, turned, piece)

    halves = jnp.where(
        lax.broadcasted_iota(jnp.int32, (8, LANES), 1) // HALF
        == lax.broadcasted_iota(jnp.int32, (8, LANES), 0),
        1.0,
        0.0,
    ).astype(bf)
    for i in range(hr):
        mirror = jnp.where(
            lower, tb[pl.ds(i, cols, stride=rows), :], tb[pl.ds(i + hr, cols, stride=rows), :]
        )
        z = jnp.maximum(yp[i] + mirror, 0.0) * head
        top = z.astype(bf)
        rest = (z - top.astype(f32)).astype(bf)
        sums = mm_nt(halves, top) + mm_nt(halves, rest)
        out_ref[i : i + 1, :] = sums[0:1]
        out_ref[i + hr : i + hr + 1, :] = sums[1:2]

    to_side.wait_send()
    for k, (there, copy) in enumerate(relays):
        when(there, halos[2 * k].wait_send)
        when(there, halos[2 * k + 1].wait_send)
        when(there, copy.wait_send)

    for leaves, copy in embs:
        pl.when(leaves)(copy.wait_send)
    for copy in bundles:
        when(at_relay, copy.wait_send)

    for j in range(per):
        peer = per * C + j
        is_self = (peer == R) & (quarter == C)
        departure = remote(sb.at[j], gb.at[j], msend.at[j], mrecv.at[j], peer, quarter)

        @pl.when(jnp.logical_not(is_self))
        def _():
            departure.wait_send()


def fused(map_in, embedding, w_row, w_col, w1, b1, w2, b2, w_mix, b_mix, w_head):
    rows, cols, ch = map_in.shape
    n = lax.axis_size("row")
    width, per, hr, groups = cols + SIDE, cols // rows, rows // 2, rows // PHASES
    blocks = groups + (groups + 1) // 2
    ext = groups + 2 * SECOND_DILATION // PHASES
    used = hr * rows
    held = -(-used // 16) * 16
    bf, f32 = jnp.bfloat16, jnp.float32
    dma = pltpu.SemaphoreType.DMA
    operands = (
        map_in,
        embedding,
        w_row.T,
        w_col.T,
        w1,
        b1.reshape(1, ch),
        w2,
        b2.reshape(1, ch),
        w_mix,
        b_mix.reshape(1, ch),
        w_head.reshape(1, ch),
    )
    return pl.pallas_call(
        functools.partial(fused_kernel, n),
        out_shape=pltpu.VMEM((rows, cols), f32),
        in_specs=[pl.BlockSpec(memory_space=pl.ANY)] * 11,
        out_specs=pl.BlockSpec(memory_space=pltpu.VMEM),
        scratch_shapes=[
            pltpu.VMEM((3, blocks, width, LANES), bf),
            pltpu.VMEM((n, rows, embedding.shape[1]), bf),
            pltpu.VMEM((n * rows, WIDE), f32),
            pltpu.VMEM((3 * groups, width, WIDE), bf),
            pltpu.VMEM((3 * groups, width, TAPS), bf),
            pltpu.VMEM((groups, width, WIDE), bf),
            pltpu.VMEM((ext, width, TAPS), bf),
            pltpu.VMEM((3 * TAPS, WIDE), bf),
            pltpu.VMEM((3 * TAPS + WIDE, WIDE), bf),
            pltpu.VMEM((hr, cols, LANES), f32),
            pltpu.VMEM((per, used, LANES), f32),
            pltpu.VMEM((per, held, LANES), bf),
            pltpu.VMEM((per, held, LANES), bf),
            pltpu.VMEM((cols * rows, LANES), f32),
            dma((7,)),
            dma((7,)),
            dma((per + 7,)),
            dma((n,)),
            dma((per,)),
            dma((per,)),
            pltpu.SemaphoreType.REGULAR,
            pltpu.SemaphoreType.REGULAR,
            pltpu.SemaphoreType.REGULAR((2,)),
            pltpu.SemaphoreType.REGULAR,
            pltpu.SemaphoreType.REGULAR,
            dma,
            dma((11,)),
            *[pltpu.VMEM(x.shape, x.dtype) for x in operands],
        ],
        compiler_params=pltpu.CompilerParams(collective_id=0, has_side_effects=True),
    )(*operands)


def fits(rows, cols, channels, row_count, col_count):
    held = 2 * (cols + SIDE) * (3 * rows // PHASES) * (2 * TAPS + 2 * WIDE)
    weights = 2 * WIDE * (6 * TAPS + WIDE)
    halo = FIRST_DILATION + SECOND_DILATION
    return (
        held + weights <= FUSED_VMEM
        and rows == halo
        and col_count == 2
        and cols % SIDE == 0
        and channels == 48
        and cols * col_count == rows * row_count
    )


def on_device(
    map_in,
    embedding,
    w_row,
    w_col,
    first_kernel_weight,
    first_bias,
    second_kernel_weight,
    second_bias,
    w_mix,
    b_mix,
    w_head,
):
    patch_rows, patch_columns, channels = map_in.shape
    row_count = lax.axis_size("row")
    if fits(patch_rows, patch_columns, channels, row_count, lax.axis_size("col")):
        return fused(
            map_in,
            embedding,
            w_row,
            w_col,
            first_kernel_weight,
            first_bias,
            second_kernel_weight,
            second_bias,
            w_mix,
            b_mix,
            w_head,
        )
    row_at = lax.axis_index("row")
    col_at = lax.axis_index("col")
    all_bins = lax.all_gather(embedding, "row", axis=0, tiled=True)
    row_terms = jnp.dot(all_bins, w_row, preferred_element_type=jnp.float32)
    col_terms = jnp.dot(all_bins, w_col, preferred_element_type=jnp.float32)
    own_rows = lax.dynamic_slice_in_dim(row_terms, row_at * patch_rows, patch_rows, 0)
    own_cols = lax.dynamic_slice_in_dim(col_terms, col_at * patch_columns, patch_columns, 0)
    contact_grid = (
        map_in.astype(jnp.float32) + own_rows[:, None, :] + own_cols[None, :, :]
    ).astype(jnp.bfloat16)
    first_padded = padded(contact_grid, (("row", 0), ("col", 1)), FIRST_DILATION)
    first_layer = (
        contact_grid.astype(jnp.float32)
        + dilated_conv(
            jnp.maximum(first_padded, 0),
            first_kernel_weight,
            FIRST_DILATION,
            patch_rows,
            patch_columns,
        )
        + first_bias
    ).astype(jnp.bfloat16)
    second_padded = padded(first_layer, (("row", 0), ("col", 1)), SECOND_DILATION)
    second_layer = (
        first_layer.astype(jnp.float32)
        + dilated_conv(
            jnp.maximum(second_padded, 0),
            second_kernel_weight,
            SECOND_DILATION,
            patch_rows,
            patch_columns,
        )
        + second_bias
    ).astype(jnp.bfloat16)
    half_rows = patch_rows // 2
    blocks_per = row_count // 2
    arranged = second_layer.reshape(2, half_rows, blocks_per, patch_rows, channels)
    arranged = arranged.transpose(0, 2, 1, 3, 4).reshape(
        2 * blocks_per, half_rows, patch_rows, channels
    )
    exchanged = lax.all_to_all(
        lax.all_to_all(arranged, "row", split_axis=0, concat_axis=0, tiled=True),
        "col",
        split_axis=0,
        concat_axis=0,
        tiled=True,
    )
    exchanged = exchanged.reshape(2, blocks_per, half_rows, patch_rows, channels)
    top_half = row_at // blocks_per
    kept_part = lax.dynamic_index_in_dim(exchanged, top_half, 0, keepdims=False)
    sent_part = lax.dynamic_index_in_dim(exchanged, 1 - top_half, 0, keepdims=False)
    came_back = swapped(sent_part, "row", blocks_per.bit_length() - 1)
    stacked = jnp.where(
        top_half == 0, jnp.stack([kept_part, came_back]), jnp.stack([came_back, kept_part])
    )
    mirrored = stacked.transpose(3, 1, 0, 2, 4).reshape(patch_rows, patch_columns, channels)
    symmetric = ((second_layer.astype(jnp.float32) + mirrored.astype(jnp.float32)) * 0.5).astype(
        jnp.bfloat16
    )
    mixture = (
        jnp.einsum("rch,hk->rck", symmetric, w_mix, preferred_element_type=jnp.float32) + b_mix
    )
    mixture = jnp.maximum(mixture, 0.0)
    return jnp.sum(mixture * w_head, axis=-1)


def solution(mesh):
    placed = (
        P(("group", "row"), "col", None),
        P(("group", "row"), None),
        P(),
        P(),
        P(),
        P(),
        P(),
        P(),
        P(),
        P(),
        P(),
    )
    return jax.shard_map(
        on_device, mesh=mesh, in_specs=placed, out_specs=P(("group", "row"), "col"), check_vma=False
    )
```

```python
import functools

import jax
import jax.numpy as jnp
from jax import lax
from jax.experimental import pallas as pl
from jax.experimental.pallas import tpu as pltpu
from jax.sharding import PartitionSpec as P

FIRST_DILATION = 4
SECOND_DILATION = 8


def padded(array, sides, width):
    for axis, dim in sides:
        peers, length = (lax.axis_size(axis), array.shape[dim])
        up = [(i, (i + 1) % peers) for i in range(peers - 1)]
        down = [(j, i) for i, j in up]
        last = lax.slice_in_dim(array, length - width, length, axis=dim)
        leading = lax.slice_in_dim(array, 0, width, axis=dim)
        before = lax.ppermute(last, axis, up)
        after = lax.ppermute(leading, axis, down)
        array = jnp.concatenate([before, array, after], axis=dim)
    return array


def swapped(value, axis, bit):
    mask = 2**bit
    pairs = [(source, source ^ mask) for source in range(lax.axis_size(axis))]
    return lax.ppermute(value, axis, pairs)


def dilated_conv(active, weight, spacing, out_rows, out_cols):
    windows = []
    for tap_row in range(3):
        for tap_col in range(3):
            windows.append(
                active[
                    tap_row * spacing : tap_row * spacing + out_rows,
                    tap_col * spacing : tap_col * spacing + out_cols,
                ]
            )
    stacked = jnp.concatenate(windows, axis=-1)
    flat_weight = weight.reshape(9 * weight.shape[2], weight.shape[3])
    return jnp.einsum("rch,hk->rck", stacked, flat_weight, preferred_element_type=jnp.float32)


LANES = 128
HALF = 64
SIDE = 16
PHASES = 4
WIDE = 2 * LANES
TAPS = 5 * LANES
FUSED_VMEM = 8 * 2**20


def one_hot(rows, columns, offsets):
    r = lax.broadcasted_iota(jnp.int32, (rows, columns), 0)
    c = lax.broadcasted_iota(jnp.int32, (rows, columns), 1)
    hit = c == r + offsets[0]
    for offset in offsets[1:]:
        hit = hit | (c == r + offset)
    return jnp.where(hit, 1.0, 0.0)


def mm(a, b, precision=None):
    return jnp.dot(a, b, preferred_element_type=jnp.float32, precision=precision)


def mm_tn(a, b):
    return lax.dot_general(a, b, (((0,), (0,)), ((), ())), preferred_element_type=jnp.float32)


def mm_nt(a, b):
    return lax.dot_general(a, b, (((1,), (1,)), ((), ())), preferred_element_type=jnp.float32)


def fused_kernel(
    n,
    m_hbm,
    e_hbm,
    wr_hbm,
    wc_hbm,
    w1_hbm,
    b1_hbm,
    w2_hbm,
    b2_hbm,
    wm_hbm,
    bm_hbm,
    wh_hbm,
    out_ref,
    pk,
    eb,
    ct,
    xb,
    xs,
    l1,
    xs2,
    wa,
    wb,
    yp,
    sf,
    sb,
    gb,
    tb,
    send,
    recv,
    erecv,
    mrecv,
    mcred,
    ncred,
    m_ref,
    e_ref,
    wr_ref,
    wc_ref,
    w1_ref,
    b1_ref,
    w2_ref,
    b2_ref,
    wm_ref,
    bm_ref,
    wh_ref,
):
    bf, f32 = jnp.bfloat16, jnp.float32
    rows, cols, ch = m_ref.shape
    hr = rows // 2
    groups = rows // PHASES
    blocks = pk.shape[1]
    width = cols + SIDE
    per = cols // rows
    big = LANES // PHASES
    small = ch - big
    R = lax.axis_index("row")
    C = lax.axis_index("col")
    O = 1 - C
    group = lax.axis_index("group")
    mesh_type = pl.DeviceIdType.MESH

    relay_at, mirror_at, self_at, side_at_send, halo_at, embed_at = 0, 2, 6, 9, 11, 15
    inputs = (
        (w1_hbm, w1_ref),
        (w2_hbm, w2_ref),
        (wm_hbm, wm_ref),
        (wr_hbm, wr_ref),
        (wc_hbm, wc_ref),
        (b1_hbm, b1_ref),
        (b2_hbm, b2_ref),
        (bm_hbm, bm_ref),
        (wh_hbm, wh_ref),
        (m_hbm, m_ref),
        (e_hbm, e_ref),
    )
    loads = [pltpu.make_async_copy(a, b, send.at[i]) for i, (a, b) in enumerate(inputs)]
    load_e, load_m = loads.pop(), loads.pop()
    load_m.start()
    load_e.start()
    eb[...] = jnp.zeros_like(eb)
    quarter = lax.div(R, per)
    mine = lax.rem(R, per)
    odd = lax.rem(R, 2)
    hub = per - C
    across, slant = R + 1 - 2 * odd, R - 1 + 2 * odd
    slants = (slant >= 0) & (slant < n)
    slant = jnp.clip(slant, 0, n - 1)
    beside = ((across, None), (slant, slants))
    barrier = pltpu.get_barrier_semaphore()

    def signal(sem, row, col):
        pl.semaphore_signal(sem, inc=1, device_id=(group, row, col), device_id_type=mesh_type)

    def when(condition, act, *args):
        if condition is None:
            act(*args)
        else:
            pl.when(condition)(functools.partial(act, *args))

    def both(a, b):
        return a if b is None else a & b

    def one(condition):
        return jnp.where(condition, 1, 0)

    def far(peer):
        return (peer != R) & ((quarter != C) | (peer - R >= 2) | (R - peer >= 2))

    at_relay = (R == per) & (C == 1)
    fed = (R >= per) & (C == 0)

    def is_relay(row, col):
        return (row == per) & (col == 1)

    feeds = (C == 1) & (R < per - 1)
    spreads = (C == 1) & (R == hub)

    @pl.when(at_relay)
    def _():
        for row in range(per - 1):
            signal(barrier, row, 1)
        for row in range(per + 1, n):
            signal(barrier, row, 0)

    @pl.when(spreads)
    def _():
        for row in range(per + 1, n):
            signal(barrier, row, 1)

    when(hub - R >= 2, signal, barrier, hub, C)
    greeted = jnp.where(R == hub, R - 1, one((C == 1) & (R - hub >= 2)))
    greeted += one(((C == 0) & (R > per)) | feeds)
    for j in range(per):
        peer = per * C + j
        when(far(peer) & (peer > R), signal, barrier, peer, quarter)
        greeted += one(far(peer) & (peer < R))
    for row, there in beside:
        when(both(jnp.logical_not(is_relay(row, C)), there), signal, barrier, row, C)
        greeted += one(both(jnp.logical_not(at_relay), there))
    when(jnp.logical_not(is_relay(R, O)), signal, barrier, R, O)
    greeted += one(jnp.logical_not(at_relay))

    h_at = lax.broadcasted_iota(jnp.int32, (ch, WIDE), 0)
    l_at = lax.broadcasted_iota(jnp.int32, (ch, WIDE), 1)
    in_big = l_at < LANES
    spread = jnp.where(
        jnp.where(in_big, l_at % big, big + l_at % small) == h_at, 1.0, 0.0
    )
    lanes = lax.broadcasted_iota(jnp.int32, (1, WIDE), 1)
    phase_of = jnp.where(lanes < LANES, lanes // big, (lanes % HALF) // small)
    spread4 = jnp.where(l_at % HALF == h_at, 1.0, 0.0).astype(bf)
    phase4_of = lanes // HALF
    lane = lax.broadcasted_iota(jnp.int32, (1, LANES), 1)
    lower = lane < HALF

    def remote(src, dst, s, r, row, col):
        return pltpu.make_async_remote_copy(
            src_ref=src,
            dst_ref=dst,
            send_sem=s,
            recv_sem=r,
            device_id=(group, row, col),
            device_id_type=mesh_type,
        )

    def embed(slot, row, col):
        return remote(e_hbm, eb.at[R], send.at[embed_at + slot], erecv.at[R], row, col)

    when(greeted > 0, pl.semaphore_wait, barrier, greeted)
    to_relay = embed(per + 2, per, 1)
    when(feeds, to_relay.start)
    embs, late = [(feeds, to_relay)], []
    ahead = jnp.where(spreads | at_relay, n - 1 - per, 0)
    for j in range(per):
        peer = per * C + j
        when(far(peer) & (peer < R), signal, mcred, peer, quarter)
        copy = embed(j, peer, quarter)
        wanted = far(peer) & (quarter >= C)
        embs.append((wanted, copy))
        when(wanted & (peer < R), copy.start)
        late.append((wanted & (peer > R), copy))
        ahead += one(far(peer) & (peer > R))
    when((C == 1) & (R > hub + 1), signal, mcred, hub, C)
    when((C == 0) & (R > per), signal, mcred, per, 1)
    for row, there in beside:
        when(both(is_relay(row, C), there), signal, ncred, row, C)
    when(is_relay(R, O), signal, ncred, R, O)
    for row in range(per - 1):
        copy = embed(per + 2 + row, row, C)
        embs.append(((R == hub) & (hub - row >= 2), copy))
        when(embs[-1][0], copy.start)
    for row in range(per + 1, n):
        copy = embed(row - per - 1, row, C)
        embs.append((spreads, copy))
        late.append((spreads, copy))
    near = []
    for k, (row, there) in enumerate(beside):
        copy = embed(per + k, row, C)
        wanted = (quarter != C) | (lax.div(row, per) == quarter)
        wanted = both(wanted & ((C == 1) | (R != per) | (row < R)), there)
        near.append((wanted & at_relay, copy))
        embs.append((wanted, copy))
        when(wanted & jnp.logical_not(at_relay), copy.start)
    for load in loads:
        load.start()

    own_at = pl.multiple_of(SIDE * C, SIDE)
    placed = [jnp.where(phase_of == p, spread, 0.0).astype(bf) for p in range(PHASES)]
    load_m.wait()
    tile = m_ref[...].reshape(groups, PHASES, cols, ch)
    packed = mm(tile[:, 0].reshape(groups * cols, ch), placed[0])
    for p in range(1, PHASES):
        packed = packed + mm(tile[:, p].reshape(groups * cols, ch), placed[p])
    packed = packed.reshape(groups, cols, WIDE)
    for g in range(groups):
        pk[1, g, pl.ds(own_at, cols), :] = packed[g, :, :LANES].astype(bf)
    for t in range(blocks - groups):
        piece = packed[2 * t, :, LANES:]
        if 2 * t + 1 < groups:
            piece = jnp.where(lower, piece, packed[2 * t + 1, :, LANES:])
        pk[1, groups + t, pl.ds(own_at, cols), :] = piece.astype(bf)
    edge = pl.ds(pl.multiple_of(cols - SIDE - (cols - 2 * SIDE) * C, SIDE), SIDE)
    rest = pl.ds(pl.multiple_of(2 * SIDE * C, SIDE), cols - SIDE)
    side_at = pl.ds(pl.multiple_of(cols * C, SIDE), SIDE)
    halos = []
    for k, (row, there) in enumerate(beside):
        block = 2 * odd if k == 0 else 2 * (1 - odd)
        for at, part in enumerate((edge, rest)):
            slot = 2 * k + at
            halos.append(
                remote(
                    pk.at[1, :, part, :],
                    pk.at[block, :, part, :],
                    send.at[halo_at + slot],
                    recv.at[slot],
                    row,
                    C,
                )
            )
    when(at_relay, pl.semaphore_wait, ncred, 3)
    for k, (row, there) in enumerate(beside):
        when(near[k][0], near[k][1].start)
        when(there, halos[2 * k].start)
        when(there, halos[2 * k + 1].start)
    to_side = remote(
        pk.at[1, :, edge, :], pk.at[1, :, side_at, :], send.at[side_at_send], recv.at[4], R, O
    )
    to_side.start()

    def arrival(row):
        return remote(e_hbm, eb.at[row], send.at[embed_at], erecv.at[row], row, C)

    load_e.wait()

    @pl.when(jnp.logical_not((C == 0) & (R == per)))
    def _():
        eb[R] = e_ref[...]

    whole = eb.at[pl.ds(0, per + 1)]
    bundles = []
    for row in range(per, n):
        slot = embed_at + (0, 1, per + 2, per + 3)[row - per]
        bundles.append(remote(whole, whole, send.at[slot], erecv.at[0], row, 0))

    @pl.when(at_relay)
    def _():
        for row in range(per):
            arrival(row).wait_recv()

    when(ahead > 0, pl.semaphore_wait, mcred, ahead)

    @pl.when(at_relay)
    def _():
        for copy in bundles[::-1]:
            copy.start()

    for waits, copy in late:
        when(waits, copy.start)

    def spread_rows(y, phases):
        top, bottom = y[:big], y[big:]
        first = [jnp.where(phases == p, top, 0.0) for p in range(PHASES)]
        second = [jnp.where(phases == p, bottom, 0.0) for p in range(PHASES)]
        return (
            jnp.concatenate(first, axis=0).astype(bf),
            jnp.concatenate(second, axis=0).astype(bf),
        )

    def pack_weight(w_ref, across, phases, dst):
        for a in range(3):
            at = a * TAPS
            for b in range(3):
                first, second = spread_rows(mm(w_ref[a, b], across), phases)
                dst[at + b * LANES : at + (b + 1) * LANES, :] = first
                low = at + 3 * LANES + (0, LANES, HALF)[b]
                dst[low : low + HALF, :] = second
            dst[at + TAPS - HALF : at + TAPS, :] = jnp.zeros((HALF, WIDE), bf)

    exact = lax.Precision.HIGHEST
    for load in loads:
        load.wait()
    pack_weight(w1_ref, spread.astype(bf), phase_of, wa)
    half_mix = mm(wm_ref[...], spread4) * 0.5
    mix = half_mix.astype(bf)
    pack_weight(w2_ref, mix, phase4_of, wb)
    first, second = spread_rows(half_mix, phase4_of)
    wb[3 * TAPS : 3 * TAPS + LANES, :] = first
    wb[3 * TAPS + LANES : 3 * TAPS + LANES + HALF, :] = second
    wb[3 * TAPS + LANES + HALF :, :] = jnp.zeros((HALF, WIDE), bf)
    bias1 = mm(b1_ref[...], spread, exact)
    bias2 = mm(b2_ref[...], half_mix, exact) + 0.5 * mm(bm_ref[...], spread4.astype(f32), exact)
    head = mm(wh_ref[...], spread4[:, :LANES].astype(f32), exact)
    wr = mm_tn(wr_ref[...], spread.astype(bf)).astype(bf)
    wc = mm_tn(wc_ref[...], spread.astype(bf)).astype(bf)

    relays = []
    for k, (row, there) in enumerate(beside):
        block = 2 * (1 - odd) if k == 0 else 2 * odd
        copy = remote(
            pk.at[block, :, edge, :],
            pk.at[block, :, side_at, :],
            send.at[relay_at + k],
            recv.at[5 + k],
            R,
            O,
        )
        relays.append((there, copy))
        when(there, halos[2 * k].wait_recv)
        when(there, copy.start)

    when(fed, bundles[0].wait_recv)
    for row in range(n):
        first = (per - 1) * C
        read = (row >= first) & (row <= first + per) & (row != R)
        read |= (row == R - 1) | (row == R + 1)
        read &= jnp.logical_not(fed & (row <= per))
        read &= jnp.logical_not(at_relay & (row < per))
        when(read, arrival(row).wait_recv)
    to_side.wait_recv()
    for k, (there, copy) in enumerate(relays):
        when(there, halos[2 * k + 1].wait_recv)
        when(there, copy.wait_recv)

    for k in range(n):
        ct[k * rows : (k + 1) * rows, :] = mm(eb[k], wc)
    col_terms = ct[pl.ds(pl.multiple_of((n * rows - width) * C, 8), width), :]

    def row_terms(b):
        terms = mm(eb[jnp.clip(R + b - 1, 0, n - 1)], wr)
        out = []
        for g in range(groups):
            total = terms[PHASES * g : PHASES * g + 1]
            for p in range(1, PHASES):
                total = jnp.where(phase_of == p, terms[PHASES * g + p : PHASES * g + p + 1], total)
            out.append(total)
        return out

    col_id = lax.broadcasted_iota(jnp.int32, (width, 1), 0)

    def before(v, d):
        return jnp.where(col_id < d, 0.0, pltpu.roll(v, d, axis=0))

    def after(v, d):
        return jnp.where(col_id >= width - d, 0.0, pltpu.roll(v, width - d, axis=0))

    def put_taps(dst, at, x, y, d):
        dst[at, :, :LANES] = before(x, d).astype(bf)
        dst[at, :, LANES : 2 * LANES] = x.astype(bf)
        dst[at, :, 2 * LANES : 3 * LANES] = after(x, d).astype(bf)
        dst[at, :, 3 * LANES : 4 * LANES] = jnp.where(lower, before(y, d), after(y, d)).astype(bf)
        dst[at, :, 4 * LANES :] = y.astype(bf)

    def base_block(b, valid):
        terms = row_terms(b)
        seconds = []
        for t in range(blocks - groups):
            g = 2 * t
            term = terms[g][:, LANES:]
            if g + 1 < groups:
                term = jnp.where(lower, term, terms[g + 1][:, LANES:])
            v = (pk[b, groups + t].astype(f32) + term + col_terms[:, LANES:]).astype(bf).astype(f32)
            turned = pltpu.roll(v, HALF, axis=1)
            seconds.append(jnp.where(lower, v, turned))
            seconds.append(jnp.where(lower, turned, v))
        for g in range(groups):
            x = pk[b, g].astype(f32) + terms[g][:, :LANES] + col_terms[:, :LANES]
            x, y = x.astype(bf).astype(f32), seconds[g]
            if valid is not None:
                x, y = jnp.where(valid, x, 0.0), jnp.where(valid, y, 0.0)
            at = b * groups + g
            xb[at, :, :LANES] = x.astype(bf)
            xb[at, :, LANES:] = y.astype(bf)
            put_taps(xs, at, jnp.maximum(x, 0.0), jnp.maximum(y, 0.0), FIRST_DILATION)

    step = FIRST_DILATION // PHASES
    step2 = SECOND_DILATION // PHASES
    ext = groups + 2 * step2
    skip = groups - step2 - step

    def first_layer(start, stop):
        left = jnp.concatenate(
            [
                xs[start + skip + a * step : stop + skip + a * step].reshape(-1, TAPS)
                for a in range(3)
            ],
            axis=1,
        )
        acc = mm(left, wa[...]).reshape(stop - start, width, WIDE)
        for u in range(start, stop):
            x = xb[u + skip + step].astype(f32) + acc[u - start] + bias1
            x = x.astype(bf).astype(f32)
            if u < step2:
                x = jnp.where(R > 0, x, 0.0)
            elif u >= step2 + groups:
                x = jnp.where(R < n - 1, x, 0.0)
            else:
                l1[u - step2] = x.astype(bf)
            x = jnp.maximum(x, 0.0)
            put_taps(xs2, u, x[:, :LANES], x[:, LANES:], SECOND_DILATION)

    cut = ext - groups
    base_block(1, None)
    base_block(0, R > 0)
    first_layer(0, cut)
    base_block(2, R < n - 1)
    first_layer(cut, ext)

    window = pl.ds(own_at, cols)
    left = [
        xs2[a * step2 : a * step2 + groups, window, :].reshape(groups * cols, TAPS)
        for a in range(3)
    ]
    left.append(l1[:, window, :].reshape(groups * cols, WIDE))
    mixed = (mm(jnp.concatenate(left, axis=1), wb[...]) + bias2).reshape(groups, cols, WIDE)

    def row_of(i):
        g, p = divmod(i, PHASES)
        at = p // 2 * LANES
        return mixed[g, :, at : at + LANES], p % 2

    for i in range(hr):
        (first, at), (second, _) = row_of(i), row_of(i + hr)
        if at == 0:
            second = pltpu.roll(second, HALF, axis=1)
        else:
            first = pltpu.roll(first, HALF, axis=1)
        pair = jnp.where(lower, first, second)
        yp[i] = pair
        for j in range(per):
            sf[j, i * rows : (i + 1) * rows, :] = pair[j * rows : (j + 1) * rows, :]
    used = hr * rows
    for j in range(per):
        sb[j, :used] = sf[j].astype(bf)

    for j in range(per):
        peer = per * C + j
        is_self = (peer == R) & (quarter == C)
        copy = remote(sb.at[j], gb.at[mine], send.at[mirror_at + j], mrecv.at[mine], peer, quarter)
        local = pltpu.make_async_copy(sb.at[j], gb.at[j], send.at[self_at])

        @pl.when(jnp.logical_not(is_self))
        def _():
            copy.start()

        @pl.when(is_self)
        def _():
            local.start()

    to_side.wait_send()
    for k, (there, copy) in enumerate(relays):
        when(there, halos[2 * k].wait_send)
        when(there, halos[2 * k + 1].wait_send)
        when(there, copy.wait_send)

    for leaves, copy in embs:
        pl.when(leaves)(copy.wait_send)
    for copy in bundles:
        when(at_relay, copy.wait_send)

    early = lax.broadcasted_iota(jnp.int32, (used, 1), 0) % rows < hr
    for j in range(per):
        peer = per * C + j
        is_self = (peer == R) & (quarter == C)
        arrival = remote(sb.at[j], gb.at[j], send.at[mirror_at + j], mrecv.at[j], peer, quarter)
        local = pltpu.make_async_copy(sb.at[j], gb.at[j], send.at[self_at])

        @pl.when(jnp.logical_not(is_self))
        def _():
            arrival.wait_recv()

        @pl.when(is_self)
        def _():
            local.wait()

        piece = gb[j, :used].astype(f32)
        turned = pltpu.roll(piece, HALF, axis=1)
        at = 2 * j * used
        tb[at : at + used, :] = jnp.where(early, piece, turned)
        tb[at + used : at + 2 * used, :] = jnp.where(early, turned, piece)

    halves = jnp.where(
        lax.broadcasted_iota(jnp.int32, (8, LANES), 1) // HALF
        == lax.broadcasted_iota(jnp.int32, (8, LANES), 0),
        1.0,
        0.0,
    ).astype(bf)
    for i in range(hr):
        mirror = jnp.where(
            lower, tb[pl.ds(i, cols, stride=rows), :], tb[pl.ds(i + hr, cols, stride=rows), :]
        )
        z = jnp.maximum(yp[i] + mirror, 0.0) * head
        top = z.astype(bf)
        rest = (z - top.astype(f32)).astype(bf)
        sums = mm_nt(halves, top) + mm_nt(halves, rest)
        out_ref[i : i + 1, :] = sums[0:1]
        out_ref[i + hr : i + hr + 1, :] = sums[1:2]

    for j in range(per):
        peer = per * C + j
        is_self = (peer == R) & (quarter == C)
        departure = remote(sb.at[j], gb.at[j], send.at[mirror_at + j], mrecv.at[j], peer, quarter)

        @pl.when(jnp.logical_not(is_self))
        def _():
            departure.wait_send()


def fused(map_in, embedding, w_row, w_col, w1, b1, w2, b2, w_mix, b_mix, w_head):
    rows, cols, ch = map_in.shape
    n = lax.axis_size("row")
    width, per, hr, groups = cols + SIDE, cols // rows, rows // 2, rows // PHASES
    blocks = groups + (groups + 1) // 2
    ext = groups + 2 * SECOND_DILATION // PHASES
    used = hr * rows
    held = -(-used // 16) * 16
    bf, f32 = jnp.bfloat16, jnp.float32
    dma = pltpu.SemaphoreType.DMA
    operands = (
        map_in,
        embedding,
        w_row.T,
        w_col.T,
        w1,
        b1.reshape(1, ch),
        w2,
        b2.reshape(1, ch),
        w_mix,
        b_mix.reshape(1, ch),
        w_head.reshape(1, ch),
    )
    return pl.pallas_call(
        functools.partial(fused_kernel, n),
        out_shape=pltpu.VMEM((rows, cols), f32),
        in_specs=[pl.BlockSpec(memory_space=pl.ANY)] * 11,
        out_specs=pl.BlockSpec(memory_space=pltpu.VMEM),
        scratch_shapes=[
            pltpu.VMEM((3, blocks, width, LANES), bf),
            pltpu.VMEM((n, rows, embedding.shape[1]), bf),
            pltpu.VMEM((n * rows, WIDE), f32),
            pltpu.VMEM((3 * groups, width, WIDE), bf),
            pltpu.VMEM((3 * groups, width, TAPS), bf),
            pltpu.VMEM((groups, width, WIDE), bf),
            pltpu.VMEM((ext, width, TAPS), bf),
            pltpu.VMEM((3 * TAPS, WIDE), bf),
            pltpu.VMEM((3 * TAPS + WIDE, WIDE), bf),
            pltpu.VMEM((hr, cols, LANES), f32),
            pltpu.VMEM((per, used, LANES), f32),
            pltpu.VMEM((per, held, LANES), bf),
            pltpu.VMEM((per, held, LANES), bf),
            pltpu.VMEM((cols * rows, LANES), f32),
            dma((24,)),
            dma((7,)),
            dma((n,)),
            dma((per,)),
            pltpu.SemaphoreType.REGULAR,
            pltpu.SemaphoreType.REGULAR,
            *[pltpu.VMEM(x.shape, x.dtype) for x in operands],
        ],
        compiler_params=pltpu.CompilerParams(collective_id=0, has_side_effects=True),
    )(*operands)


def fits(rows, cols, channels, row_count, col_count):
    held = 2 * (cols + SIDE) * (3 * rows // PHASES) * (2 * TAPS + 2 * WIDE)
    weights = 2 * WIDE * (6 * TAPS + WIDE)
    halo = FIRST_DILATION + SECOND_DILATION
    return (
        held + weights <= FUSED_VMEM
        and rows == halo
        and row_count == 8
        and col_count == 2
        and cols % SIDE == 0
        and channels == 48
        and cols * col_count == rows * row_count
    )


def on_device(
    map_in,
    embedding,
    w_row,
    w_col,
    first_kernel_weight,
    first_bias,
    second_kernel_weight,
    second_bias,
    w_mix,
    b_mix,
    w_head,
):
    patch_rows, patch_columns, channels = map_in.shape
    row_count = lax.axis_size("row")
    if fits(patch_rows, patch_columns, channels, row_count, lax.axis_size("col")):
        return fused(
            map_in,
            embedding,
            w_row,
            w_col,
            first_kernel_weight,
            first_bias,
            second_kernel_weight,
            second_bias,
            w_mix,
            b_mix,
            w_head,
        )
    row_at = lax.axis_index("row")
    col_at = lax.axis_index("col")
    all_bins = lax.all_gather(embedding, "row", axis=0, tiled=True)
    row_terms = jnp.dot(all_bins, w_row, preferred_element_type=jnp.float32)
    col_terms = jnp.dot(all_bins, w_col, preferred_element_type=jnp.float32)
    own_rows = lax.dynamic_slice_in_dim(row_terms, row_at * patch_rows, patch_rows, 0)
    own_cols = lax.dynamic_slice_in_dim(col_terms, col_at * patch_columns, patch_columns, 0)
    contact_grid = (
        map_in.astype(jnp.float32) + own_rows[:, None, :] + own_cols[None, :, :]
    ).astype(jnp.bfloat16)
    first_padded = padded(contact_grid, (("row", 0), ("col", 1)), FIRST_DILATION)
    first_layer = (
        contact_grid.astype(jnp.float32)
        + dilated_conv(
            jnp.maximum(first_padded, 0),
            first_kernel_weight,
            FIRST_DILATION,
            patch_rows,
            patch_columns,
        )
        + first_bias
    ).astype(jnp.bfloat16)
    second_padded = padded(first_layer, (("row", 0), ("col", 1)), SECOND_DILATION)
    second_layer = (
        first_layer.astype(jnp.float32)
        + dilated_conv(
            jnp.maximum(second_padded, 0),
            second_kernel_weight,
            SECOND_DILATION,
            patch_rows,
            patch_columns,
        )
        + second_bias
    ).astype(jnp.bfloat16)
    half_rows = patch_rows // 2
    blocks_per = row_count // 2
    arranged = second_layer.reshape(2, half_rows, blocks_per, patch_rows, channels)
    arranged = arranged.transpose(0, 2, 1, 3, 4).reshape(
        2 * blocks_per, half_rows, patch_rows, channels
    )
    exchanged = lax.all_to_all(
        lax.all_to_all(arranged, "row", split_axis=0, concat_axis=0, tiled=True),
        "col",
        split_axis=0,
        concat_axis=0,
        tiled=True,
    )
    exchanged = exchanged.reshape(2, blocks_per, half_rows, patch_rows, channels)
    top_half = row_at // blocks_per
    kept_part = lax.dynamic_index_in_dim(exchanged, top_half, 0, keepdims=False)
    sent_part = lax.dynamic_index_in_dim(exchanged, 1 - top_half, 0, keepdims=False)
    came_back = swapped(sent_part, "row", blocks_per.bit_length() - 1)
    stacked = jnp.where(
        top_half == 0, jnp.stack([kept_part, came_back]), jnp.stack([came_back, kept_part])
    )
    mirrored = stacked.transpose(3, 1, 0, 2, 4).reshape(patch_rows, patch_columns, channels)
    symmetric = ((second_layer.astype(jnp.float32) + mirrored.astype(jnp.float32)) * 0.5).astype(
        jnp.bfloat16
    )
    mixture = (
        jnp.einsum("rch,hk->rck", symmetric, w_mix, preferred_element_type=jnp.float32) + b_mix
    )
    mixture = jnp.maximum(mixture, 0.0)
    return jnp.sum(mixture * w_head, axis=-1)


def solution(mesh):
    placed = (
        P(("group", "row"), "col", None),
        P(("group", "row"), None),
        P(),
        P(),
        P(),
        P(),
        P(),
        P(),
        P(),
        P(),
        P(),
    )
    return jax.shard_map(
        on_device, mesh=mesh, in_specs=placed, out_specs=P(("group", "row"), "col"), check_vma=False
    )
```

```python
import functools

import jax
import jax.numpy as jnp
from jax import lax
from jax.experimental import pallas as pl
from jax.experimental.pallas import tpu as pltpu
from jax.sharding import PartitionSpec as P

FIRST_DILATION = 4
SECOND_DILATION = 8


def padded(array, sides, width):
    for axis, dim in sides:
        peers, length = (lax.axis_size(axis), array.shape[dim])
        up = [(i, (i + 1) % peers) for i in range(peers - 1)]
        down = [(j, i) for i, j in up]
        last = lax.slice_in_dim(array, length - width, length, axis=dim)
        leading = lax.slice_in_dim(array, 0, width, axis=dim)
        before = lax.ppermute(last, axis, up)
        after = lax.ppermute(leading, axis, down)
        array = jnp.concatenate([before, array, after], axis=dim)
    return array


def swapped(value, axis, bit):
    mask = 2**bit
    pairs = [(source, source ^ mask) for source in range(lax.axis_size(axis))]
    return lax.ppermute(value, axis, pairs)


def dilated_conv(active, weight, spacing, out_rows, out_cols):
    windows = []
    for tap_row in range(3):
        for tap_col in range(3):
            windows.append(
                active[
                    tap_row * spacing : tap_row * spacing + out_rows,
                    tap_col * spacing : tap_col * spacing + out_cols,
                ]
            )
    stacked = jnp.concatenate(windows, axis=-1)
    flat_weight = weight.reshape(9 * weight.shape[2], weight.shape[3])
    return jnp.einsum("rch,hk->rck", stacked, flat_weight, preferred_element_type=jnp.float32)


LANES = 128
HALF = 64
SIDE = 16
PHASES = 4
WIDE = 2 * LANES
TAPS = 5 * LANES
FUSED_VMEM = 8 * 2**20


def one_hot(rows, columns, offsets):
    r = lax.broadcasted_iota(jnp.int32, (rows, columns), 0)
    c = lax.broadcasted_iota(jnp.int32, (rows, columns), 1)
    hit = c == r + offsets[0]
    for offset in offsets[1:]:
        hit = hit | (c == r + offset)
    return jnp.where(hit, 1.0, 0.0)


def mm(a, b, precision=None):
    return jnp.dot(a, b, preferred_element_type=jnp.float32, precision=precision)


def mm_tn(a, b):
    return lax.dot_general(a, b, (((0,), (0,)), ((), ())), preferred_element_type=jnp.float32)


def mm_nt(a, b):
    return lax.dot_general(a, b, (((1,), (1,)), ((), ())), preferred_element_type=jnp.float32)


def fused_kernel(
    n,
    m_hbm,
    e_hbm,
    wr_hbm,
    wc_hbm,
    w1_hbm,
    b1_hbm,
    w2_hbm,
    b2_hbm,
    wm_hbm,
    bm_hbm,
    wh_hbm,
    out_ref,
    pk,
    eb,
    ct,
    xb,
    xs,
    l1,
    xs2,
    wa,
    wb,
    yp,
    sf,
    sb,
    gb,
    tb,
    send,
    recv,
    erecv,
    mrecv,
    mcred,
    ncred,
    m_ref,
    e_ref,
    wr_ref,
    wc_ref,
    w1_ref,
    b1_ref,
    w2_ref,
    b2_ref,
    wm_ref,
    bm_ref,
    wh_ref,
):
    bf, f32 = jnp.bfloat16, jnp.float32
    rows, cols, ch = m_ref.shape
    hr = rows // 2
    groups = rows // PHASES
    blocks = pk.shape[1]
    width = cols + SIDE
    per = cols // rows
    big = LANES // PHASES
    small = ch - big
    R = lax.axis_index("row")
    C = lax.axis_index("col")
    O = 1 - C
    group = lax.axis_index("group")
    mesh_type = pl.DeviceIdType.MESH

    relay_at, mirror_at, self_at, side_at_send, halo_at, embed_at = 0, 2, 6, 9, 11, 15
    inputs = (
        (w1_hbm, w1_ref),
        (w2_hbm, w2_ref),
        (wm_hbm, wm_ref),
        (wr_hbm, wr_ref),
        (wc_hbm, wc_ref),
        (b1_hbm, b1_ref),
        (b2_hbm, b2_ref),
        (bm_hbm, bm_ref),
        (wh_hbm, wh_ref),
        (m_hbm, m_ref),
        (e_hbm, e_ref),
    )
    loads = [pltpu.make_async_copy(a, b, send.at[i]) for i, (a, b) in enumerate(inputs)]
    load_e, load_m = loads.pop(), loads.pop()
    load_m.start()
    load_e.start()
    eb[...] = jnp.zeros_like(eb)
    quarter = lax.div(R, per)
    mine = lax.rem(R, per)
    odd = lax.rem(R, 2)
    hub = per - C
    across, slant = R + 1 - 2 * odd, R - 1 + 2 * odd
    slants = (slant >= 0) & (slant < n)
    slant = jnp.clip(slant, 0, n - 1)
    beside = ((across, None), (slant, slants))
    barrier = pltpu.get_barrier_semaphore()

    def signal(sem, row, col):
        pl.semaphore_signal(sem, inc=1, device_id=(group, row, col), device_id_type=mesh_type)

    def when(condition, act, *args):
        if condition is None:
            act(*args)
        else:
            pl.when(condition)(functools.partial(act, *args))

    def both(a, b):
        return a if b is None else a & b

    def one(condition):
        return jnp.where(condition, 1, 0)

    def far(peer):
        return (peer != R) & ((quarter != C) | (peer - R >= 2) | (R - peer >= 2))

    at_relay = (R == per) & (C == 1)
    fed = (R >= per) & (C == 0)

    def is_relay(row, col):
        return (row == per) & (col == 1)

    feeds = (C == 1) & (R < per - 1)
    spreads = (C == 1) & (R == hub)

    @pl.when(at_relay)
    def _():
        for row in range(per - 1):
            signal(barrier, row, 1)
        for row in range(per + 1, n):
            signal(barrier, row, 0)

    @pl.when(spreads)
    def _():
        for row in range(per + 1, n):
            signal(barrier, row, 1)

    when(hub - R >= 2, signal, barrier, hub, C)
    greeted = jnp.where(R == hub, R - 1, one((C == 1) & (R - hub >= 2)))
    greeted += one(((C == 0) & (R > per)) | feeds)
    for j in range(per):
        peer = per * C + j
        when(far(peer) & (peer > R), signal, barrier, peer, quarter)
        greeted += one(far(peer) & (peer < R))
    for row, there in beside:
        when(both(jnp.logical_not(is_relay(row, C)), there), signal, barrier, row, C)
        greeted += one(both(jnp.logical_not(at_relay), there))
    when(jnp.logical_not(is_relay(R, O)), signal, barrier, R, O)
    greeted += one(jnp.logical_not(at_relay))

    h_at = lax.broadcasted_iota(jnp.int32, (ch, WIDE), 0)
    l_at = lax.broadcasted_iota(jnp.int32, (ch, WIDE), 1)
    in_big = l_at < LANES
    spread = jnp.where(
        jnp.where(in_big, l_at % big, big + l_at % small) == h_at, 1.0, 0.0
    )
    lanes = lax.broadcasted_iota(jnp.int32, (1, WIDE), 1)
    phase_of = jnp.where(lanes < LANES, lanes // big, (lanes % HALF) // small)
    spread4 = jnp.where(l_at % HALF == h_at, 1.0, 0.0).astype(bf)
    phase4_of = lanes // HALF
    lane = lax.broadcasted_iota(jnp.int32, (1, LANES), 1)
    lower = lane < HALF

    def remote(src, dst, s, r, row, col):
        return pltpu.make_async_remote_copy(
            src_ref=src,
            dst_ref=dst,
            send_sem=s,
            recv_sem=r,
            device_id=(group, row, col),
            device_id_type=mesh_type,
        )

    def embed(slot, row, col):
        return remote(e_hbm, eb.at[R], send.at[embed_at + slot], erecv.at[R], row, col)

    when(greeted > 0, pl.semaphore_wait, barrier, greeted)
    to_relay = embed(per + 2, per, 1)
    when(feeds, to_relay.start)
    embs, soon_sent, late = [(feeds, to_relay)], [], []
    ahead = jnp.where(at_relay, n - 1 - per, 0)
    for j in range(per):
        peer = per * C + j
        when(far(peer) & (peer < R), signal, mcred, peer, quarter)
        copy = embed(j, peer, quarter)
        wanted = far(peer) & (quarter >= C)
        embs.append((wanted, copy))
        soon_sent.append((wanted & (peer < R), copy))
        late.append((wanted & (peer > R), copy))
        ahead += one(far(peer) & (peer > R))
    when((C == 1) & (R > hub + 1), signal, ncred, hub, C)
    when((C == 0) & (R > per), signal, mcred, per, 1)
    for row, there in beside:
        when(both(is_relay(row, C), there), signal, ncred, row, C)
    when(is_relay(R, O), signal, ncred, R, O)
    for row in range(per - 1):
        copy = embed(per + 2 + row, row, C)
        embs.append(((R == hub) & (hub - row >= 2), copy))
        soon_sent.append(embs[-1])
    for row in range(per + 1, n):
        copy = embed(row - per - 1, row, C)
        embs.append((spreads, copy))
        late.append((spreads, copy))
    near = []
    for k, (row, there) in enumerate(beside):
        copy = embed(per + k, row, C)
        wanted = (quarter != C) | (lax.div(row, per) == quarter)
        wanted = both(wanted & ((C == 1) | (R != per) | (row < R)), there)
        near.append((wanted & at_relay, copy))
        embs.append((wanted, copy))
        when(wanted & jnp.logical_not(at_relay), copy.start)
    for load in loads:
        load.start()

    own_at = pl.multiple_of(SIDE * C, SIDE)
    placed = [jnp.where(phase_of == p, spread, 0.0).astype(bf) for p in range(PHASES)]
    load_m.wait()
    tile = m_ref[...].reshape(groups, PHASES, cols, ch)
    packed = mm(tile[:, 0].reshape(groups * cols, ch), placed[0])
    for p in range(1, PHASES):
        packed = packed + mm(tile[:, p].reshape(groups * cols, ch), placed[p])
    packed = packed.reshape(groups, cols, WIDE)
    for g in range(groups):
        pk[1, g, pl.ds(own_at, cols), :] = packed[g, :, :LANES].astype(bf)
    for t in range(blocks - groups):
        piece = packed[2 * t, :, LANES:]
        if 2 * t + 1 < groups:
            piece = jnp.where(lower, piece, packed[2 * t + 1, :, LANES:])
        pk[1, groups + t, pl.ds(own_at, cols), :] = piece.astype(bf)
    edge = pl.ds(pl.multiple_of(cols - SIDE - (cols - 2 * SIDE) * C, SIDE), SIDE)
    rest = pl.ds(pl.multiple_of(2 * SIDE * C, SIDE), cols - SIDE)
    side_at = pl.ds(pl.multiple_of(cols * C, SIDE), SIDE)
    halos = []
    for k, (row, there) in enumerate(beside):
        block = 2 * odd if k == 0 else 2 * (1 - odd)
        for at, part in enumerate((edge, rest)):
            slot = 2 * k + at
            halos.append(
                remote(
                    pk.at[1, :, part, :],
                    pk.at[block, :, part, :],
                    send.at[halo_at + slot],
                    recv.at[slot],
                    row,
                    C,
                )
            )
    when(at_relay, pl.semaphore_wait, ncred, 3)
    when(slants, halos[2].start)
    halos[0].start()
    when(slants & (C == 0), halos[3].start)
    when(C == 0, halos[1].start)
    to_side = remote(
        pk.at[1, :, edge, :], pk.at[1, :, side_at, :], send.at[side_at_send], recv.at[4], R, O
    )
    to_side.start()
    for wanted, copy in near + soon_sent:
        when(wanted, copy.start)

    def arrival(row):
        return remote(e_hbm, eb.at[row], send.at[embed_at], erecv.at[row], row, C)

    load_e.wait()

    @pl.when(jnp.logical_not((C == 0) & (R == per)))
    def _():
        eb[R] = e_ref[...]

    whole = eb.at[pl.ds(0, per + 1)]
    bundles = []
    for row in range(per, n):
        slot = embed_at + (0, 1, per + 2, per + 3)[row - per]
        bundles.append(remote(whole, whole, send.at[slot], erecv.at[0], row, 0))

    @pl.when(at_relay)
    def _():
        for row in range(per):
            arrival(row).wait_recv()

    soon = quarter >= C
    when(soon & (ahead > 0), pl.semaphore_wait, mcred, ahead)
    when(spreads, pl.semaphore_wait, ncred, n - 1 - per)

    @pl.when(at_relay)
    def _():
        for copy in bundles[::-1]:
            copy.start()

    for waits, copy in late:
        when(waits, copy.start)

    def spread_rows(y, phases):
        top, bottom = y[:big], y[big:]
        first = [jnp.where(phases == p, top, 0.0) for p in range(PHASES)]
        second = [jnp.where(phases == p, bottom, 0.0) for p in range(PHASES)]
        return (
            jnp.concatenate(first, axis=0).astype(bf),
            jnp.concatenate(second, axis=0).astype(bf),
        )

    def pack_weight(w_ref, across, phases, dst):
        for a in range(3):
            at = a * TAPS
            for b in range(3):
                first, second = spread_rows(mm(w_ref[a, b], across), phases)
                dst[at + b * LANES : at + (b + 1) * LANES, :] = first
                low = at + 3 * LANES + (0, LANES, HALF)[b]
                dst[low : low + HALF, :] = second
            dst[at + TAPS - HALF : at + TAPS, :] = jnp.zeros((HALF, WIDE), bf)

    exact = lax.Precision.HIGHEST
    for load in loads:
        load.wait()
    pack_weight(w1_ref, spread.astype(bf), phase_of, wa)
    half_mix = mm(wm_ref[...], spread4) * 0.5
    mix = half_mix.astype(bf)
    pack_weight(w2_ref, mix, phase4_of, wb)
    first, second = spread_rows(half_mix, phase4_of)
    wb[3 * TAPS : 3 * TAPS + LANES, :] = first
    wb[3 * TAPS + LANES : 3 * TAPS + LANES + HALF, :] = second
    wb[3 * TAPS + LANES + HALF :, :] = jnp.zeros((HALF, WIDE), bf)
    bias1 = mm(b1_ref[...], spread, exact)
    bias2 = mm(b2_ref[...], half_mix, exact) + 0.5 * mm(bm_ref[...], spread4.astype(f32), exact)
    head = mm(wh_ref[...], spread4[:, :LANES].astype(f32), exact)
    wr = mm_tn(wr_ref[...], spread.astype(bf)).astype(bf)
    wc = mm_tn(wc_ref[...], spread.astype(bf)).astype(bf)

    relays = []
    for k, (row, there) in enumerate(beside):
        block = 2 * (1 - odd) if k == 0 else 2 * odd
        copy = remote(
            pk.at[block, :, edge, :],
            pk.at[block, :, side_at, :],
            send.at[relay_at + k],
            recv.at[5 + k],
            R,
            O,
        )
        relays.append((there, copy))
    halos[0].wait_recv()
    relays[0][1].start()
    when(slants & (C == 1), halos[3].start)
    when(C == 1, halos[1].start)
    when(slants, halos[2].wait_recv)
    when(slants, relays[1][1].start)

    when(fed, bundles[0].wait_recv)
    for row in range(n):
        first = (per - 1) * C
        read = (row >= first) & (row <= first + per) & (row != R)
        read |= (row == R - 1) | (row == R + 1)
        read &= jnp.logical_not(fed & (row <= per))
        read &= jnp.logical_not(at_relay & (row < per))
        when(read, arrival(row).wait_recv)
    held = -(-width // rows)
    for k in range(held):
        ct[k * rows : (k + 1) * rows, :] = mm(eb[(n - held) * C + k], wc)
    def row_terms_of(b):
        terms = mm(eb[jnp.clip(R + b - 1, 0, n - 1)], wr)
        out = []
        for g in range(groups):
            total = terms[PHASES * g : PHASES * g + 1]
            for p in range(1, PHASES):
                total = jnp.where(phase_of == p, terms[PHASES * g + p : PHASES * g + p + 1], total)
            out.append(total)
        return out

    row_terms = [row_terms_of(b) for b in range(3)]

    to_side.wait_recv()
    halos[1].wait_recv()
    when(slants, halos[3].wait_recv)
    for there, copy in relays:
        when(there, copy.wait_recv)

    col_id = lax.broadcasted_iota(jnp.int32, (width, 1), 0)

    def before(v, d):
        return jnp.where(col_id < d, 0.0, pltpu.roll(v, d, axis=0))

    def after(v, d):
        return jnp.where(col_id >= width - d, 0.0, pltpu.roll(v, width - d, axis=0))

    def put_taps(dst, at, x, y, d):
        dst[at, :, :LANES] = before(x, d).astype(bf)
        dst[at, :, LANES : 2 * LANES] = x.astype(bf)
        dst[at, :, 2 * LANES : 3 * LANES] = after(x, d).astype(bf)
        dst[at, :, 3 * LANES : 4 * LANES] = jnp.where(lower, before(y, d), after(y, d)).astype(bf)
        dst[at, :, 4 * LANES :] = y.astype(bf)

    def base_block(b, valid):
        terms = row_terms[b]
        seconds = []
        for t in range(blocks - groups):
            g = 2 * t
            term = terms[g][:, LANES:]
            if g + 1 < groups:
                term = jnp.where(lower, term, terms[g + 1][:, LANES:])
            v = (pk[b, groups + t].astype(f32) + term + col_terms[:, LANES:]).astype(bf).astype(f32)
            turned = pltpu.roll(v, HALF, axis=1)
            seconds.append(jnp.where(lower, v, turned))
            seconds.append(jnp.where(lower, turned, v))
        for g in range(groups):
            x = pk[b, g].astype(f32) + terms[g][:, :LANES] + col_terms[:, :LANES]
            x, y = x.astype(bf).astype(f32), seconds[g]
            if valid is not None:
                x, y = jnp.where(valid, x, 0.0), jnp.where(valid, y, 0.0)
            at = b * groups + g
            xb[at, :, :LANES] = x.astype(bf)
            xb[at, :, LANES:] = y.astype(bf)
            put_taps(xs, at, jnp.maximum(x, 0.0), jnp.maximum(y, 0.0), FIRST_DILATION)

    step = FIRST_DILATION // PHASES
    step2 = SECOND_DILATION // PHASES
    ext = groups + 2 * step2
    skip = groups - step2 - step

    def first_layer(start, stop):
        left = jnp.concatenate(
            [
                xs[start + skip + a * step : stop + skip + a * step].reshape(-1, TAPS)
                for a in range(3)
            ],
            axis=1,
        )
        acc = mm(left, wa[...]).reshape(stop - start, width, WIDE)
        for u in range(start, stop):
            x = xb[u + skip + step].astype(f32) + acc[u - start] + bias1
            x = x.astype(bf).astype(f32)
            if u < step2:
                x = jnp.where(R > 0, x, 0.0)
            elif u >= step2 + groups:
                x = jnp.where(R < n - 1, x, 0.0)
            else:
                l1[u - step2] = x.astype(bf)
            x = jnp.maximum(x, 0.0)
            put_taps(xs2, u, x[:, :LANES], x[:, LANES:], SECOND_DILATION)

    cut = 5
    col_terms = ct[pl.ds(pl.multiple_of((held * rows - width) * C, 8), width), :]
    base_block(1, None)
    base_block(0, R > 0)
    first_layer(0, 2)
    base_block(2, R < n - 1)
    first_layer(2, 5)
    first_layer(cut, ext)

    when(jnp.logical_not(soon) & (ahead > 0), pl.semaphore_wait, mcred, ahead)
    window = pl.ds(own_at, cols)
    left = [
        xs2[a * step2 : a * step2 + groups, window, :].reshape(groups * cols, TAPS)
        for a in range(3)
    ]
    left.append(l1[:, window, :].reshape(groups * cols, WIDE))
    mixed = (mm(jnp.concatenate(left, axis=1), wb[...]) + bias2).reshape(groups, cols, WIDE)

    def row_of(i):
        g, p = divmod(i, PHASES)
        at = p // 2 * LANES
        return mixed[g, :, at : at + LANES], p % 2

    for i in range(hr):
        (first, at), (second, _) = row_of(i), row_of(i + hr)
        if at == 0:
            second = pltpu.roll(second, HALF, axis=1)
        else:
            first = pltpu.roll(first, HALF, axis=1)
        pair = jnp.where(lower, first, second)
        yp[i] = pair
        for j in range(per):
            sf[j, i * rows : (i + 1) * rows, :] = pair[j * rows : (j + 1) * rows, :]
    used = hr * rows
    for j in range(per):
        sb[j, :used] = sf[j].astype(bf)

    for j in range(per):
        peer = per * C + j
        is_self = (peer == R) & (quarter == C)
        copy = remote(sb.at[j], gb.at[mine], send.at[mirror_at + j], mrecv.at[mine], peer, quarter)
        local = pltpu.make_async_copy(sb.at[j], gb.at[j], send.at[self_at])

        @pl.when(jnp.logical_not(is_self))
        def _():
            copy.start()

        @pl.when(is_self)
        def _():
            local.start()

    to_side.wait_send()
    for at in range(2):
        halos[at].wait_send()
        when(slants, halos[2 + at].wait_send)
    for there, copy in relays:
        when(there, copy.wait_send)

    for leaves, copy in embs:
        pl.when(leaves)(copy.wait_send)
    for copy in bundles:
        when(at_relay, copy.wait_send)

    early = lax.broadcasted_iota(jnp.int32, (used, 1), 0) % rows < hr
    for j in range(per):
        peer = per * C + j
        is_self = (peer == R) & (quarter == C)
        arrival = remote(sb.at[j], gb.at[j], send.at[mirror_at + j], mrecv.at[j], peer, quarter)
        local = pltpu.make_async_copy(sb.at[j], gb.at[j], send.at[self_at])

        @pl.when(jnp.logical_not(is_self))
        def _():
            arrival.wait_recv()

        @pl.when(is_self)
        def _():
            local.wait()

        piece = gb[j, :used].astype(f32)
        turned = pltpu.roll(piece, HALF, axis=1)
        at = 2 * j * used
        tb[at : at + used, :] = jnp.where(early, piece, turned)
        tb[at + used : at + 2 * used, :] = jnp.where(early, turned, piece)

    halves = jnp.where(
        lax.broadcasted_iota(jnp.int32, (8, WIDE), 1) % LANES // HALF
        == lax.broadcasted_iota(jnp.int32, (8, WIDE), 0),
        1.0,
        0.0,
    ).astype(bf)
    for i in range(hr):
        mirror = jnp.where(
            lower, tb[pl.ds(i, cols, stride=rows), :], tb[pl.ds(i + hr, cols, stride=rows), :]
        )
        z = jnp.maximum(yp[i] + mirror, 0.0) * head
        top = z.astype(bf)
        rest = (z - top.astype(f32)).astype(bf)
        sums = mm_nt(halves, jnp.concatenate([top, rest], axis=1))
        out_ref[i : i + 1, :] = sums[0:1]
        out_ref[i + hr : i + hr + 1, :] = sums[1:2]

    for j in range(per):
        peer = per * C + j
        is_self = (peer == R) & (quarter == C)
        departure = remote(sb.at[j], gb.at[j], send.at[mirror_at + j], mrecv.at[j], peer, quarter)

        @pl.when(jnp.logical_not(is_self))
        def _():
            departure.wait_send()


def fused(map_in, embedding, w_row, w_col, w1, b1, w2, b2, w_mix, b_mix, w_head):
    rows, cols, ch = map_in.shape
    n = lax.axis_size("row")
    width, per, hr, groups = cols + SIDE, cols // rows, rows // 2, rows // PHASES
    blocks = groups + (groups + 1) // 2
    ext = groups + 2 * SECOND_DILATION // PHASES
    used = hr * rows
    held = -(-used // 16) * 16
    bf, f32 = jnp.bfloat16, jnp.float32
    dma = pltpu.SemaphoreType.DMA
    operands = (
        map_in,
        embedding,
        w_row.T,
        w_col.T,
        w1,
        b1.reshape(1, ch),
        w2,
        b2.reshape(1, ch),
        w_mix,
        b_mix.reshape(1, ch),
        w_head.reshape(1, ch),
    )
    return pl.pallas_call(
        functools.partial(fused_kernel, n),
        out_shape=pltpu.VMEM((rows, cols), f32),
        in_specs=[pl.BlockSpec(memory_space=pl.ANY)] * 11,
        out_specs=pl.BlockSpec(memory_space=pltpu.VMEM),
        scratch_shapes=[
            pltpu.VMEM((3, blocks, width, LANES), bf),
            pltpu.VMEM((n, rows, embedding.shape[1]), bf),
            pltpu.VMEM((-(-width // rows) * rows, WIDE), f32),
            pltpu.VMEM((3 * groups, width, WIDE), bf),
            pltpu.VMEM((3 * groups, width, TAPS), bf),
            pltpu.VMEM((groups, width, WIDE), bf),
            pltpu.VMEM((ext, width, TAPS), bf),
            pltpu.VMEM((3 * TAPS, WIDE), bf),
            pltpu.VMEM((3 * TAPS + WIDE, WIDE), bf),
            pltpu.VMEM((hr, cols, LANES), f32),
            pltpu.VMEM((per, used, LANES), f32),
            pltpu.VMEM((per, held, LANES), bf),
            pltpu.VMEM((per, held, LANES), bf),
            pltpu.VMEM((cols * rows, LANES), f32),
            dma((24,)),
            dma((7,)),
            dma((n,)),
            dma((per,)),
            pltpu.SemaphoreType.REGULAR,
            pltpu.SemaphoreType.REGULAR,
            *[pltpu.VMEM(x.shape, x.dtype) for x in operands],
        ],
        compiler_params=pltpu.CompilerParams(collective_id=0, has_side_effects=True),
    )(*operands)


def fits(rows, cols, channels, row_count, col_count):
    held = 2 * (cols + SIDE) * (3 * rows // PHASES) * (2 * TAPS + 2 * WIDE)
    weights = 2 * WIDE * (6 * TAPS + WIDE)
    halo = FIRST_DILATION + SECOND_DILATION
    return (
        held + weights <= FUSED_VMEM
        and rows == halo
        and row_count == 8
        and col_count == 2
        and cols % SIDE == 0
        and channels == 48
        and cols * col_count == rows * row_count
    )


def on_device(
    map_in,
    embedding,
    w_row,
    w_col,
    first_kernel_weight,
    first_bias,
    second_kernel_weight,
    second_bias,
    w_mix,
    b_mix,
    w_head,
):
    patch_rows, patch_columns, channels = map_in.shape
    row_count = lax.axis_size("row")
    if fits(patch_rows, patch_columns, channels, row_count, lax.axis_size("col")):
        return fused(
            map_in,
            embedding,
            w_row,
            w_col,
            first_kernel_weight,
            first_bias,
            second_kernel_weight,
            second_bias,
            w_mix,
            b_mix,
            w_head,
        )
    row_at = lax.axis_index("row")
    col_at = lax.axis_index("col")
    all_bins = lax.all_gather(embedding, "row", axis=0, tiled=True)
    row_terms = jnp.dot(all_bins, w_row, preferred_element_type=jnp.float32)
    col_terms = jnp.dot(all_bins, w_col, preferred_element_type=jnp.float32)
    own_rows = lax.dynamic_slice_in_dim(row_terms, row_at * patch_rows, patch_rows, 0)
    own_cols = lax.dynamic_slice_in_dim(col_terms, col_at * patch_columns, patch_columns, 0)
    contact_grid = (
        map_in.astype(jnp.float32) + own_rows[:, None, :] + own_cols[None, :, :]
    ).astype(jnp.bfloat16)
    first_padded = padded(contact_grid, (("row", 0), ("col", 1)), FIRST_DILATION)
    first_layer = (
        contact_grid.astype(jnp.float32)
        + dilated_conv(
            jnp.maximum(first_padded, 0),
            first_kernel_weight,
            FIRST_DILATION,
            patch_rows,
            patch_columns,
        )
        + first_bias
    ).astype(jnp.bfloat16)
    second_padded = padded(first_layer, (("row", 0), ("col", 1)), SECOND_DILATION)
    second_layer = (
        first_layer.astype(jnp.float32)
        + dilated_conv(
            jnp.maximum(second_padded, 0),
            second_kernel_weight,
            SECOND_DILATION,
            patch_rows,
            patch_columns,
        )
        + second_bias
    ).astype(jnp.bfloat16)
    half_rows = patch_rows // 2
    blocks_per = row_count // 2
    arranged = second_layer.reshape(2, half_rows, blocks_per, patch_rows, channels)
    arranged = arranged.transpose(0, 2, 1, 3, 4).reshape(
        2 * blocks_per, half_rows, patch_rows, channels
    )
    exchanged = lax.all_to_all(
        lax.all_to_all(arranged, "row", split_axis=0, concat_axis=0, tiled=True),
        "col",
        split_axis=0,
        concat_axis=0,
        tiled=True,
    )
    exchanged = exchanged.reshape(2, blocks_per, half_rows, patch_rows, channels)
    top_half = row_at // blocks_per
    kept_part = lax.dynamic_index_in_dim(exchanged, top_half, 0, keepdims=False)
    sent_part = lax.dynamic_index_in_dim(exchanged, 1 - top_half, 0, keepdims=False)
    came_back = swapped(sent_part, "row", blocks_per.bit_length() - 1)
    stacked = jnp.where(
        top_half == 0, jnp.stack([kept_part, came_back]), jnp.stack([came_back, kept_part])
    )
    mirrored = stacked.transpose(3, 1, 0, 2, 4).reshape(patch_rows, patch_columns, channels)
    symmetric = ((second_layer.astype(jnp.float32) + mirrored.astype(jnp.float32)) * 0.5).astype(
        jnp.bfloat16
    )
    mixture = (
        jnp.einsum("rch,hk->rck", symmetric, w_mix, preferred_element_type=jnp.float32) + b_mix
    )
    mixture = jnp.maximum(mixture, 0.0)
    return jnp.sum(mixture * w_head, axis=-1)


def solution(mesh):
    placed = (
        P(("group", "row"), "col", None),
        P(("group", "row"), None),
        P(),
        P(),
        P(),
        P(),
        P(),
        P(),
        P(),
        P(),
        P(),
    )
    return jax.shard_map(
        on_device, mesh=mesh, in_specs=placed, out_specs=P(("group", "row"), "col"), check_vma=False
    )
```

```python
import functools

import jax
import jax.numpy as jnp
from jax import lax
from jax.experimental import pallas as pl
from jax.experimental.pallas import tpu as pltpu
from jax.sharding import PartitionSpec as P

FIRST_DILATION = 4
SECOND_DILATION = 8


def padded(array, sides, width):
    for axis, dim in sides:
        peers, length = (lax.axis_size(axis), array.shape[dim])
        up = [(i, (i + 1) % peers) for i in range(peers - 1)]
        down = [(j, i) for i, j in up]
        last = lax.slice_in_dim(array, length - width, length, axis=dim)
        leading = lax.slice_in_dim(array, 0, width, axis=dim)
        before = lax.ppermute(last, axis, up)
        after = lax.ppermute(leading, axis, down)
        array = jnp.concatenate([before, array, after], axis=dim)
    return array


def swapped(value, axis, bit):
    mask = 2**bit
    pairs = [(source, source ^ mask) for source in range(lax.axis_size(axis))]
    return lax.ppermute(value, axis, pairs)


def dilated_conv(active, weight, spacing, out_rows, out_cols):
    windows = []
    for tap_row in range(3):
        for tap_col in range(3):
            windows.append(
                active[
                    tap_row * spacing : tap_row * spacing + out_rows,
                    tap_col * spacing : tap_col * spacing + out_cols,
                ]
            )
    stacked = jnp.concatenate(windows, axis=-1)
    flat_weight = weight.reshape(9 * weight.shape[2], weight.shape[3])
    return jnp.einsum("rch,hk->rck", stacked, flat_weight, preferred_element_type=jnp.float32)


LANES = 128
HALF = 64
SIDE = 16
PHASES = 4
WIDE = 2 * LANES
TAPS = 5 * LANES
FUSED_VMEM = 8 * 2**20


def one_hot(rows, columns, offsets):
    r = lax.broadcasted_iota(jnp.int32, (rows, columns), 0)
    c = lax.broadcasted_iota(jnp.int32, (rows, columns), 1)
    hit = c == r + offsets[0]
    for offset in offsets[1:]:
        hit = hit | (c == r + offset)
    return jnp.where(hit, 1.0, 0.0)


def mm(a, b, precision=None):
    return jnp.dot(a, b, preferred_element_type=jnp.float32, precision=precision)


def mm_tn(a, b):
    return lax.dot_general(a, b, (((0,), (0,)), ((), ())), preferred_element_type=jnp.float32)


def mm_nt(a, b):
    return lax.dot_general(a, b, (((1,), (1,)), ((), ())), preferred_element_type=jnp.float32)


def fused_kernel(
    n,
    m_hbm,
    e_hbm,
    wr_hbm,
    wc_hbm,
    w1_hbm,
    b1_hbm,
    w2_hbm,
    b2_hbm,
    wm_hbm,
    bm_hbm,
    wh_hbm,
    out_ref,
    pk,
    eb,
    ct,
    xb,
    xs,
    l1,
    xs2,
    wa,
    wb,
    yp,
    sf,
    sb,
    gb,
    tb,
    send,
    recv,
    erecv,
    mrecv,
    mcred,
    ncred,
    m_ref,
    e_ref,
    wr_ref,
    wc_ref,
    w1_ref,
    b1_ref,
    w2_ref,
    b2_ref,
    wm_ref,
    bm_ref,
    wh_ref,
):
    bf, f32 = jnp.bfloat16, jnp.float32
    rows, cols, ch = m_ref.shape
    hr = rows // 2
    groups = rows // PHASES
    blocks = pk.shape[1]
    width = cols + SIDE
    per = cols // rows
    big = LANES // PHASES
    small = ch - big
    R = lax.axis_index("row")
    C = lax.axis_index("col")
    O = 1 - C
    group = lax.axis_index("group")
    mesh_type = pl.DeviceIdType.MESH

    relay_at, mirror_at, self_at, side_at_send, halo_at, embed_at = 0, 2, 6, 9, 11, 15
    inputs = (
        (w1_hbm, w1_ref),
        (w2_hbm, w2_ref),
        (wm_hbm, wm_ref),
        (wr_hbm, wr_ref),
        (wc_hbm, wc_ref),
        (b1_hbm, b1_ref),
        (b2_hbm, b2_ref),
        (bm_hbm, bm_ref),
        (wh_hbm, wh_ref),
        (m_hbm, m_ref),
        (e_hbm, e_ref),
    )
    loads = [pltpu.make_async_copy(a, b, send.at[i]) for i, (a, b) in enumerate(inputs)]
    load_e, load_m = loads.pop(), loads.pop()
    load_m.start()
    load_e.start()
    eb[...] = jnp.zeros_like(eb)
    quarter = lax.div(R, per)
    mine = lax.rem(R, per)
    odd = lax.rem(R, 2)
    hub = per - C
    across, slant = R + 1 - 2 * odd, R - 1 + 2 * odd
    slants = (slant >= 0) & (slant < n)
    slant = jnp.clip(slant, 0, n - 1)
    beside = ((across, None), (slant, slants))
    barrier = pltpu.get_barrier_semaphore()

    def signal(sem, row, col):
        pl.semaphore_signal(sem, inc=1, device_id=(group, row, col), device_id_type=mesh_type)

    def when(condition, act, *args):
        if condition is None:
            act(*args)
        else:
            pl.when(condition)(functools.partial(act, *args))

    def both(a, b):
        return a if b is None else a & b

    def one(condition):
        return jnp.where(condition, 1, 0)

    def far(peer):
        return (peer != R) & ((quarter != C) | (peer - R >= 2) | (R - peer >= 2))

    collects = (R == per - 2) & (C == 1)
    fed = (R >= per) & (C == 0)
    gives = (R == per) & (C == 1)
    feeds = (C == 1) & (R == 0)
    spreads = (C == 1) & (R == hub)

    @pl.when(gives)
    def _():
        for row in range(per + 1, n):
            signal(barrier, row, 0)

    when(collects, signal, barrier, 0, 1)
    @pl.when(spreads)
    def _():
        for row in range(per + 1, n):
            signal(barrier, row, 1)

    when(hub - R >= 2, signal, barrier, hub, C)
    greeted = jnp.where(R == hub, R - 1, one((C == 1) & (R - hub >= 2)))
    greeted += one(((C == 0) & (R > per)) | feeds)
    for j in range(per):
        peer = per * C + j
        when(far(peer) & (peer > R), signal, barrier, peer, quarter)
        greeted += one(far(peer) & (peer < R))
    for row, there in beside:
        when(there, signal, barrier, row, C)
        greeted += 1 if there is None else one(there)
    signal(barrier, R, O)
    greeted += 1

    h_at = lax.broadcasted_iota(jnp.int32, (ch, WIDE), 0)
    l_at = lax.broadcasted_iota(jnp.int32, (ch, WIDE), 1)
    in_big = l_at < LANES
    spread = jnp.where(
        jnp.where(in_big, l_at % big, big + l_at % small) == h_at, 1.0, 0.0
    )
    lanes = lax.broadcasted_iota(jnp.int32, (1, WIDE), 1)
    phase_of = jnp.where(lanes < LANES, lanes // big, (lanes % HALF) // small)
    spread4 = jnp.where(l_at % HALF == h_at, 1.0, 0.0).astype(bf)
    phase4_of = lanes // HALF
    lane = lax.broadcasted_iota(jnp.int32, (1, LANES), 1)
    lower = lane < HALF

    def remote(src, dst, s, r, row, col):
        return pltpu.make_async_remote_copy(
            src_ref=src,
            dst_ref=dst,
            send_sem=s,
            recv_sem=r,
            device_id=(group, row, col),
            device_id_type=mesh_type,
        )

    def embed(slot, row, col):
        return remote(e_hbm, eb.at[R], send.at[embed_at + slot], erecv.at[R], row, col)

    pl.semaphore_wait(barrier, greeted)
    to_collector = embed(per + 2, per - 2, 1)
    when(feeds, to_collector.start)
    embs, soon_sent, late = [(feeds, to_collector)], [], []
    ahead = jnp.where(gives, n - 1 - per, 0)
    for j in range(per):
        peer = per * C + j
        when(far(peer) & (peer < R), signal, mcred, peer, quarter)
        copy = embed(j, peer, quarter)
        wanted = far(peer) & (quarter >= C)
        embs.append((wanted, copy))
        soon_sent.append((wanted & (peer < R), copy))
        late.append((wanted & (peer > R), copy))
        ahead += one(far(peer) & (peer > R))
    when((C == 1) & (R > hub + 1), signal, ncred, hub, C)
    when((C == 0) & (R > per), signal, mcred, per, 1)
    for row in range(per - 1):
        copy = embed(per + 2 + row, row, C)
        embs.append(((R == hub) & (hub - row >= 2), copy))
        soon_sent.append(embs[-1])
    for row in range(per + 1, n):
        copy = embed(row - per - 1, row, C)
        embs.append((spreads, copy))
        late.append((spreads, copy))
        copy = embed((0, 1, per + 2)[row - per - 1], row, 0)
        embs.append((gives, copy))
        late.append((gives, copy))
    for k, (row, there) in enumerate(beside):
        copy = embed(per + k, row, C)
        wanted = (quarter != C) | (lax.div(row, per) == quarter)
        wanted = both(wanted & ((C == 1) | (R != per) | (row < R)), there)
        embs.append((wanted, copy))
        when(wanted, copy.start)
    for load in loads:
        load.start()

    own_at = pl.multiple_of(SIDE * C, SIDE)
    placed = [jnp.where(phase_of == p, spread, 0.0).astype(bf) for p in range(PHASES)]
    load_m.wait()
    tile = m_ref[...].reshape(groups, PHASES, cols, ch)
    packed = mm(tile[:, 0].reshape(groups * cols, ch), placed[0])
    for p in range(1, PHASES):
        packed = packed + mm(tile[:, p].reshape(groups * cols, ch), placed[p])
    packed = packed.reshape(groups, cols, WIDE)
    for g in range(groups):
        pk[1, g, pl.ds(own_at, cols), :] = packed[g, :, :LANES].astype(bf)
    for t in range(blocks - groups):
        piece = packed[2 * t, :, LANES:]
        if 2 * t + 1 < groups:
            piece = jnp.where(lower, piece, packed[2 * t + 1, :, LANES:])
        pk[1, groups + t, pl.ds(own_at, cols), :] = piece.astype(bf)
    edge = pl.ds(pl.multiple_of(cols - SIDE - (cols - 2 * SIDE) * C, SIDE), SIDE)
    rest = pl.ds(pl.multiple_of(2 * SIDE * C, SIDE), cols - SIDE)
    side_at = pl.ds(pl.multiple_of(cols * C, SIDE), SIDE)
    halos = []
    for k, (row, there) in enumerate(beside):
        block = 2 * odd if k == 0 else 2 * (1 - odd)
        for at, part in enumerate((edge, rest)):
            slot = 2 * k + at
            halos.append(
                remote(
                    pk.at[1, :, part, :],
                    pk.at[block, :, part, :],
                    send.at[halo_at + slot],
                    recv.at[slot],
                    row,
                    C,
                )
            )
    when(slants, halos[2].start)
    halos[0].start()
    when(slants & (C == 0), halos[3].start)
    when(C == 0, halos[1].start)
    to_side = remote(
        pk.at[1, :, edge, :], pk.at[1, :, side_at, :], send.at[side_at_send], recv.at[4], R, O
    )
    to_side.start()
    for wanted, copy in soon_sent:
        when(wanted, copy.start)

    def arrival(row):
        return remote(e_hbm, eb.at[row], send.at[embed_at], erecv.at[row], row, C)

    load_e.wait()

    eb[R] = e_ref[...]

    soon = quarter >= C
    when(soon & (ahead > 0), pl.semaphore_wait, mcred, ahead)
    when(spreads, pl.semaphore_wait, ncred, n - 1 - per)
    for waits, copy in late:
        when(waits, copy.start)

    def spread_rows(y, phases):
        top, bottom = y[:big], y[big:]
        first = [jnp.where(phases == p, top, 0.0) for p in range(PHASES)]
        second = [jnp.where(phases == p, bottom, 0.0) for p in range(PHASES)]
        return (
            jnp.concatenate(first, axis=0).astype(bf),
            jnp.concatenate(second, axis=0).astype(bf),
        )

    def pack_weight(w_ref, across, phases, dst, places):
        for a, at in enumerate(places):
            for b in range(3):
                first, second = spread_rows(mm(w_ref[a, b], across), phases)
                dst[at + b * LANES : at + (b + 1) * LANES, :] = first
                low = at + 3 * LANES + (0, LANES, HALF)[b]
                dst[low : low + HALF, :] = second
            dst[at + TAPS - HALF : at + TAPS, :] = jnp.zeros((HALF, WIDE), bf)

    exact = lax.Precision.HIGHEST
    for load in loads:
        load.wait()
    pack_weight(w1_ref, spread.astype(bf), phase_of, wa, (0, TAPS, 2 * TAPS))
    half_mix = mm(wm_ref[...], spread4) * 0.5
    mix = half_mix.astype(bf)
    pack_weight(w2_ref, mix, phase4_of, wb, (0, TAPS, 2 * TAPS + WIDE))
    first, second = spread_rows(half_mix, phase4_of)
    at = 2 * TAPS
    wb[at : at + LANES, :] = first
    wb[at + LANES : at + LANES + HALF, :] = second
    wb[at + LANES + HALF : at + WIDE, :] = jnp.zeros((HALF, WIDE), bf)
    bias1 = mm(b1_ref[...], spread, exact)
    bias2 = mm(b2_ref[...], half_mix, exact) + 0.5 * mm(bm_ref[...], spread4.astype(f32), exact)
    head = mm(wh_ref[...], spread4[:, :LANES].astype(f32), exact)
    wr = mm_tn(wr_ref[...], spread.astype(bf)).astype(bf)
    wc = mm_tn(wc_ref[...], spread.astype(bf)).astype(bf)

    whole = eb.at[pl.ds(0, per)]
    bundles = [
        remote(whole, whole, send.at[embed_at + row], erecv.at[0], per + row, 0)
        for row in range(per)
    ]

    @pl.when(collects)
    def _():
        for row in range(per):
            if row != per - 2:
                arrival(row).wait_recv()
        pl.semaphore_wait(mcred, ahead)
        for copy in bundles[::-1]:
            copy.start()

    relays = []
    for k, (row, there) in enumerate(beside):
        block = 2 * (1 - odd) if k == 0 else 2 * odd
        copy = remote(
            pk.at[block, :, edge, :],
            pk.at[block, :, side_at, :],
            send.at[relay_at + k],
            recv.at[5 + k],
            R,
            O,
        )
        relays.append((there, copy))
    halos[0].wait_recv()
    relays[0][1].start()
    when(slants, halos[2].wait_recv)
    when(slants, relays[1][1].start)

    when(slants & (C == 1), halos[3].start)
    when(C == 1, halos[1].start)
    when(fed, bundles[0].wait_recv)
    for row in range(n):
        first = (per - 1) * C
        read = (row >= first) & (row <= first + per) & (row != R)
        read |= (row == R - 1) | (row == R + 1)
        if row < per:
            read &= jnp.logical_not(fed | collects)
        when(read, arrival(row).wait_recv)
    held = -(-width // rows)
    for k in range(held):
        ct[k * rows : (k + 1) * rows, :] = mm(eb[(n - held) * C + k], wc)
    def row_terms_of(b):
        terms = mm(eb[jnp.clip(R + b - 1, 0, n - 1)], wr)
        out = []
        for g in range(groups):
            total = terms[PHASES * g : PHASES * g + 1]
            for p in range(1, PHASES):
                total = jnp.where(phase_of == p, terms[PHASES * g + p : PHASES * g + p + 1], total)
            out.append(total)
        return out

    row_terms = [row_terms_of(b) for b in range(3)]

    to_side.wait_recv()
    halos[1].wait_recv()
    when(slants, halos[3].wait_recv)
    for there, copy in relays:
        when(there, copy.wait_recv)

    col_id = lax.broadcasted_iota(jnp.int32, (width, 1), 0)

    def before(v, d):
        if d % 8 == 0:
            return jnp.concatenate([jnp.zeros((d, LANES), f32), v[: width - d]], axis=0)
        return jnp.where(col_id < d, 0.0, pltpu.roll(v, d, axis=0))

    def after(v, d):
        if d % 8 == 0:
            return jnp.concatenate([v[d:], jnp.zeros((d, LANES), f32)], axis=0)
        return jnp.where(col_id >= width - d, 0.0, pltpu.roll(v, width - d, axis=0))

    def put_taps(dst, at, x, y, d):
        dst[at, :, :LANES] = before(x, d).astype(bf)
        dst[at, :, LANES : 2 * LANES] = x.astype(bf)
        dst[at, :, 2 * LANES : 3 * LANES] = after(x, d).astype(bf)
        dst[at, :, 3 * LANES : 4 * LANES] = jnp.where(lower, before(y, d), after(y, d)).astype(bf)
        dst[at, :, 4 * LANES :] = y.astype(bf)

    def base_block(b, valid):
        terms = row_terms[b]
        seconds = []
        for t in range(blocks - groups):
            g = 2 * t
            term = terms[g][:, LANES:]
            if g + 1 < groups:
                term = jnp.where(lower, term, terms[g + 1][:, LANES:])
            v = (pk[b, groups + t].astype(f32) + term + col_terms[:, LANES:]).astype(bf).astype(f32)
            turned = pltpu.roll(v, HALF, axis=1)
            seconds.append(jnp.where(lower, v, turned))
            seconds.append(jnp.where(lower, turned, v))
        for g in range(groups):
            x = pk[b, g].astype(f32) + terms[g][:, :LANES] + col_terms[:, :LANES]
            x, y = x.astype(bf).astype(f32), seconds[g]
            if valid is not None:
                x, y = jnp.where(valid, x, 0.0), jnp.where(valid, y, 0.0)
            at = b * groups + g
            xb[at, :, :LANES] = x.astype(bf)
            xb[at, :, LANES:] = y.astype(bf)
            put_taps(xs, at, jnp.maximum(x, 0.0), jnp.maximum(y, 0.0), FIRST_DILATION)

    step = FIRST_DILATION // PHASES
    step2 = SECOND_DILATION // PHASES
    ext = groups + 2 * step2
    skip = groups - step2 - step

    def first_layer(start, stop):
        left = jnp.concatenate(
            [
                xs[start + skip + a * step : stop + skip + a * step].reshape(-1, TAPS)
                for a in range(3)
            ],
            axis=1,
        )
        acc = mm(left, wa[...]).reshape(stop - start, width, WIDE)
        for u in range(start, stop):
            x = xb[u + skip + step].astype(f32) + acc[u - start] + bias1
            x = x.astype(bf).astype(f32)
            if u < step2:
                x = jnp.where(R > 0, x, 0.0)
            elif u >= step2 + groups:
                x = jnp.where(R < n - 1, x, 0.0)
            else:
                l1[u - step2] = x.astype(bf)
            x = jnp.maximum(x, 0.0)
            put_taps(xs2, u, x[:, :LANES], x[:, LANES:], SECOND_DILATION)

    col_terms = ct[pl.ds(pl.multiple_of((held * rows - width) * C, 8), width), :]
    base_block(1, None)
    base_block(0, R > 0)
    window = pl.ds(own_at, cols)

    def second_taps(a):
        return xs2[a * step2 : a * step2 + groups, window, :].reshape(groups * cols, TAPS)

    known = 2 * step2 + groups - step2
    first_layer(0, 4)
    base_block(2, R < n - 1)
    first_layer(4, known)
    left = [second_taps(0), second_taps(1), l1[:, window, :].reshape(groups * cols, WIDE)]
    mixed = mm(jnp.concatenate(left, axis=1), wb[: 2 * TAPS + WIDE])
    first_layer(known, ext)
    mixed = mixed + mm(second_taps(2), wb[2 * TAPS + WIDE :]) + bias2
    mixed = mixed.reshape(groups, cols, WIDE)

    def row_of(i):
        g, p = divmod(i, PHASES)
        at = p // 2 * LANES
        return mixed[g, :, at : at + LANES], p % 2

    for i in range(hr):
        (first, at), (second, _) = row_of(i), row_of(i + hr)
        if at == 0:
            second = pltpu.roll(second, HALF, axis=1)
        else:
            first = pltpu.roll(first, HALF, axis=1)
        pair = jnp.where(lower, first, second)
        yp[i] = pair
        for j in range(per):
            sf[j, i * rows : (i + 1) * rows, :] = pair[j * rows : (j + 1) * rows, :]
    used = hr * rows
    for j in range(per):
        sb[j, :used] = sf[j].astype(bf)

    when(jnp.logical_not(soon | collects) & (ahead > 0), pl.semaphore_wait, mcred, ahead)
    for j in range(per):
        peer = per * C + j
        is_self = (peer == R) & (quarter == C)
        copy = remote(sb.at[j], gb.at[mine], send.at[mirror_at + j], mrecv.at[mine], peer, quarter)
        local = pltpu.make_async_copy(sb.at[j], gb.at[j], send.at[self_at])

        @pl.when(jnp.logical_not(is_self))
        def _():
            copy.start()

        @pl.when(is_self)
        def _():
            local.start()

    to_side.wait_send()
    for at in range(2):
        halos[at].wait_send()
        when(slants, halos[2 + at].wait_send)
    for there, copy in relays:
        when(there, copy.wait_send)

    for leaves, copy in embs:
        pl.when(leaves)(copy.wait_send)
    for copy in bundles:
        when(collects, copy.wait_send)

    early = lax.broadcasted_iota(jnp.int32, (used, 1), 0) % rows < hr
    for j in range(per):
        peer = per * C + j
        is_self = (peer == R) & (quarter == C)
        arrival = remote(sb.at[j], gb.at[j], send.at[mirror_at + j], mrecv.at[j], peer, quarter)
        local = pltpu.make_async_copy(sb.at[j], gb.at[j], send.at[self_at])

        @pl.when(jnp.logical_not(is_self))
        def _():
            arrival.wait_recv()

        @pl.when(is_self)
        def _():
            local.wait()

        piece = gb[j, :used].astype(f32)
        turned = pltpu.roll(piece, HALF, axis=1)
        at = 2 * j * used
        tb[at : at + used, :] = jnp.where(early, piece, turned)
        tb[at + used : at + 2 * used, :] = jnp.where(early, turned, piece)

    halves = jnp.where(
        lax.broadcasted_iota(jnp.int32, (8, WIDE), 1) % LANES // HALF
        == lax.broadcasted_iota(jnp.int32, (8, WIDE), 0),
        1.0,
        0.0,
    ).astype(bf)
    for i in range(hr):
        mirror = jnp.where(
            lower, tb[pl.ds(i, cols, stride=rows), :], tb[pl.ds(i + hr, cols, stride=rows), :]
        )
        z = jnp.maximum(yp[i] + mirror, 0.0) * head
        top = z.astype(bf)
        rest = (z - top.astype(f32)).astype(bf)
        sums = mm_nt(halves, jnp.concatenate([top, rest], axis=1))
        out_ref[i : i + 1, :] = sums[0:1]
        out_ref[i + hr : i + hr + 1, :] = sums[1:2]

    for j in range(per):
        peer = per * C + j
        is_self = (peer == R) & (quarter == C)
        departure = remote(sb.at[j], gb.at[j], send.at[mirror_at + j], mrecv.at[j], peer, quarter)

        @pl.when(jnp.logical_not(is_self))
        def _():
            departure.wait_send()


def fused(map_in, embedding, w_row, w_col, w1, b1, w2, b2, w_mix, b_mix, w_head):
    rows, cols, ch = map_in.shape
    n = lax.axis_size("row")
    width, per, hr, groups = cols + SIDE, cols // rows, rows // 2, rows // PHASES
    blocks = groups + (groups + 1) // 2
    ext = groups + 2 * SECOND_DILATION // PHASES
    used = hr * rows
    held = -(-used // 16) * 16
    bf, f32 = jnp.bfloat16, jnp.float32
    dma = pltpu.SemaphoreType.DMA
    operands = (
        map_in,
        embedding,
        w_row.T,
        w_col.T,
        w1,
        b1.reshape(1, ch),
        w2,
        b2.reshape(1, ch),
        w_mix,
        b_mix.reshape(1, ch),
        w_head.reshape(1, ch),
    )
    return pl.pallas_call(
        functools.partial(fused_kernel, n),
        out_shape=pltpu.VMEM((rows, cols), f32),
        in_specs=[pl.BlockSpec(memory_space=pl.ANY)] * 11,
        out_specs=pl.BlockSpec(memory_space=pltpu.VMEM),
        scratch_shapes=[
            pltpu.VMEM((3, blocks, width, LANES), bf),
            pltpu.VMEM((n, rows, embedding.shape[1]), bf),
            pltpu.VMEM((-(-width // rows) * rows, WIDE), f32),
            pltpu.VMEM((3 * groups, width, WIDE), bf),
            pltpu.VMEM((3 * groups, width, TAPS), bf),
            pltpu.VMEM((groups, width, WIDE), bf),
            pltpu.VMEM((ext, width, TAPS), bf),
            pltpu.VMEM((3 * TAPS, WIDE), bf),
            pltpu.VMEM((3 * TAPS + WIDE, WIDE), bf),
            pltpu.VMEM((hr, cols, LANES), f32),
            pltpu.VMEM((per, used, LANES), f32),
            pltpu.VMEM((per, held, LANES), bf),
            pltpu.VMEM((per, held, LANES), bf),
            pltpu.VMEM((cols * rows, LANES), f32),
            dma((24,)),
            dma((7,)),
            dma((n,)),
            dma((per,)),
            pltpu.SemaphoreType.REGULAR,
            pltpu.SemaphoreType.REGULAR,
            *[pltpu.VMEM(x.shape, x.dtype) for x in operands],
        ],
        compiler_params=pltpu.CompilerParams(collective_id=0, has_side_effects=True),
    )(*operands)


def fits(rows, cols, channels, row_count, col_count):
    held = 2 * (cols + SIDE) * (3 * rows // PHASES) * (2 * TAPS + 2 * WIDE)
    weights = 2 * WIDE * (6 * TAPS + WIDE)
    halo = FIRST_DILATION + SECOND_DILATION
    return (
        held + weights <= FUSED_VMEM
        and rows == halo
        and row_count == 8
        and col_count == 2
        and cols % SIDE == 0
        and channels == 48
        and cols * col_count == rows * row_count
    )


def on_device(
    map_in,
    embedding,
    w_row,
    w_col,
    first_kernel_weight,
    first_bias,
    second_kernel_weight,
    second_bias,
    w_mix,
    b_mix,
    w_head,
):
    patch_rows, patch_columns, channels = map_in.shape
    row_count = lax.axis_size("row")
    if fits(patch_rows, patch_columns, channels, row_count, lax.axis_size("col")):
        return fused(
            map_in,
            embedding,
            w_row,
            w_col,
            first_kernel_weight,
            first_bias,
            second_kernel_weight,
            second_bias,
            w_mix,
            b_mix,
            w_head,
        )
    row_at = lax.axis_index("row")
    col_at = lax.axis_index("col")
    all_bins = lax.all_gather(embedding, "row", axis=0, tiled=True)
    row_terms = jnp.dot(all_bins, w_row, preferred_element_type=jnp.float32)
    col_terms = jnp.dot(all_bins, w_col, preferred_element_type=jnp.float32)
    own_rows = lax.dynamic_slice_in_dim(row_terms, row_at * patch_rows, patch_rows, 0)
    own_cols = lax.dynamic_slice_in_dim(col_terms, col_at * patch_columns, patch_columns, 0)
    contact_grid = (
        map_in.astype(jnp.float32) + own_rows[:, None, :] + own_cols[None, :, :]
    ).astype(jnp.bfloat16)
    first_padded = padded(contact_grid, (("row", 0), ("col", 1)), FIRST_DILATION)
    first_layer = (
        contact_grid.astype(jnp.float32)
        + dilated_conv(
            jnp.maximum(first_padded, 0),
            first_kernel_weight,
            FIRST_DILATION,
            patch_rows,
            patch_columns,
        )
        + first_bias
    ).astype(jnp.bfloat16)
    second_padded = padded(first_layer, (("row", 0), ("col", 1)), SECOND_DILATION)
    second_layer = (
        first_layer.astype(jnp.float32)
        + dilated_conv(
            jnp.maximum(second_padded, 0),
            second_kernel_weight,
            SECOND_DILATION,
            patch_rows,
            patch_columns,
        )
        + second_bias
    ).astype(jnp.bfloat16)
    half_rows = patch_rows // 2
    blocks_per = row_count // 2
    arranged = second_layer.reshape(2, half_rows, blocks_per, patch_rows, channels)
    arranged = arranged.transpose(0, 2, 1, 3, 4).reshape(
        2 * blocks_per, half_rows, patch_rows, channels
    )
    exchanged = lax.all_to_all(
        lax.all_to_all(arranged, "row", split_axis=0, concat_axis=0, tiled=True),
        "col",
        split_axis=0,
        concat_axis=0,
        tiled=True,
    )
    exchanged = exchanged.reshape(2, blocks_per, half_rows, patch_rows, channels)
    top_half = row_at // blocks_per
    kept_part = lax.dynamic_index_in_dim(exchanged, top_half, 0, keepdims=False)
    sent_part = lax.dynamic_index_in_dim(exchanged, 1 - top_half, 0, keepdims=False)
    came_back = swapped(sent_part, "row", blocks_per.bit_length() - 1)
    stacked = jnp.where(
        top_half == 0, jnp.stack([kept_part, came_back]), jnp.stack([came_back, kept_part])
    )
    mirrored = stacked.transpose(3, 1, 0, 2, 4).reshape(patch_rows, patch_columns, channels)
    symmetric = ((second_layer.astype(jnp.float32) + mirrored.astype(jnp.float32)) * 0.5).astype(
        jnp.bfloat16
    )
    mixture = (
        jnp.einsum("rch,hk->rck", symmetric, w_mix, preferred_element_type=jnp.float32) + b_mix
    )
    mixture = jnp.maximum(mixture, 0.0)
    return jnp.sum(mixture * w_head, axis=-1)


def solution(mesh):
    placed = (
        P(("group", "row"), "col", None),
        P(("group", "row"), None),
        P(),
        P(),
        P(),
        P(),
        P(),
        P(),
        P(),
        P(),
        P(),
    )
    return jax.shard_map(
        on_device, mesh=mesh, in_specs=placed, out_specs=P(("group", "row"), "col"), check_vma=False
    )
```

```python
import functools

import jax
import jax.numpy as jnp
from jax import lax
from jax.experimental import pallas as pl
from jax.experimental.pallas import tpu as pltpu
from jax.sharding import PartitionSpec as P

FIRST_DILATION = 4
SECOND_DILATION = 8


def padded(array, sides, width):
    for axis, dim in sides:
        peers, length = (lax.axis_size(axis), array.shape[dim])
        up = [(i, (i + 1) % peers) for i in range(peers - 1)]
        down = [(j, i) for i, j in up]
        last = lax.slice_in_dim(array, length - width, length, axis=dim)
        leading = lax.slice_in_dim(array, 0, width, axis=dim)
        before = lax.ppermute(last, axis, up)
        after = lax.ppermute(leading, axis, down)
        array = jnp.concatenate([before, array, after], axis=dim)
    return array


def swapped(value, axis, bit):
    mask = 2**bit
    pairs = [(source, source ^ mask) for source in range(lax.axis_size(axis))]
    return lax.ppermute(value, axis, pairs)


def dilated_conv(active, weight, spacing, out_rows, out_cols):
    windows = []
    for tap_row in range(3):
        for tap_col in range(3):
            windows.append(
                active[
                    tap_row * spacing : tap_row * spacing + out_rows,
                    tap_col * spacing : tap_col * spacing + out_cols,
                ]
            )
    stacked = jnp.concatenate(windows, axis=-1)
    flat_weight = weight.reshape(9 * weight.shape[2], weight.shape[3])
    return jnp.einsum("rch,hk->rck", stacked, flat_weight, preferred_element_type=jnp.float32)


LANES = 128
HALF = 64
SIDE = 16
PHASES = 4
WIDE = 2 * LANES
TAPS = 5 * LANES
FUSED_VMEM = 8 * 2**20


def one_hot(rows, columns, offsets):
    r = lax.broadcasted_iota(jnp.int32, (rows, columns), 0)
    c = lax.broadcasted_iota(jnp.int32, (rows, columns), 1)
    hit = c == r + offsets[0]
    for offset in offsets[1:]:
        hit = hit | (c == r + offset)
    return jnp.where(hit, 1.0, 0.0)


def mm(a, b, precision=None):
    return jnp.dot(a, b, preferred_element_type=jnp.float32, precision=precision)


def mm_tn(a, b):
    return lax.dot_general(a, b, (((0,), (0,)), ((), ())), preferred_element_type=jnp.float32)


def mm_nt(a, b):
    return lax.dot_general(a, b, (((1,), (1,)), ((), ())), preferred_element_type=jnp.float32)


def fused_kernel(
    n,
    m_hbm,
    e_hbm,
    wr_hbm,
    wc_hbm,
    w1_hbm,
    b1_hbm,
    w2_hbm,
    b2_hbm,
    wm_hbm,
    bm_hbm,
    wh_hbm,
    out_ref,
    pk,
    eb,
    ct,
    xb,
    xs,
    l1,
    xs2,
    wa,
    wb,
    yp,
    sf,
    sb,
    gb,
    tb,
    send,
    recv,
    erecv,
    mrecv,
    mcred,
    ncred,
    m_ref,
    e_ref,
    wrc_ref,
    w12_ref,
    wm_ref,
    row_ref,
):
    bf, f32 = jnp.bfloat16, jnp.float32
    rows, cols, ch = m_ref.shape
    hr = rows // 2
    groups = rows // PHASES
    blocks = pk.shape[1]
    width = cols + SIDE
    per = cols // rows
    big = LANES // PHASES
    small = ch - big
    R = lax.axis_index("row")
    C = lax.axis_index("col")
    O = 1 - C
    group = lax.axis_index("group")
    mesh_type = pl.DeviceIdType.MESH

    at_side, at_mirror, at_halo, at_embed = 4, 5, 6, 7
    wr_ref, wc_ref = wrc_ref.at[0], wrc_ref.at[1]
    w1_ref, w2_ref = w12_ref.at[0], w12_ref.at[1]
    b1_ref, b2_ref, bm_ref, wh_ref = (row_ref.at[i] for i in range(4))
    groups_of = (
        ((w1_hbm, w1_ref), (w2_hbm, w2_ref)),
        ((wm_hbm, wm_ref),),
        ((wr_hbm, wr_ref), (wc_hbm, wc_ref)),
        ((b1_hbm, b1_ref), (b2_hbm, b2_ref), (bm_hbm, bm_ref), (wh_hbm, wh_ref)),
    )
    loads = [
        pltpu.make_async_copy(a, b, send.at[i]) for i, pairs in enumerate(groups_of) for a, b in pairs
    ]
    load_m = pltpu.make_async_copy(m_hbm, m_ref, send.at[at_side])
    load_e = pltpu.make_async_copy(e_hbm, e_ref, send.at[at_mirror])
    load_m.start()
    load_e.start()
    eb[...] = jnp.zeros_like(eb)
    quarter = lax.div(R, per)
    mine = lax.rem(R, per)
    odd = lax.rem(R, 2)
    hub = per - C
    across, slant = R + 1 - 2 * odd, R - 1 + 2 * odd
    slants = (slant >= 0) & (slant < n)
    slant = jnp.clip(slant, 0, n - 1)
    beside = ((across, None), (slant, slants))
    barrier = pltpu.get_barrier_semaphore()

    def signal(sem, row, col):
        pl.semaphore_signal(sem, inc=1, device_id=(group, row, col), device_id_type=mesh_type)

    def when(condition, act, *args):
        if condition is None:
            act(*args)
        else:
            pl.when(condition)(functools.partial(act, *args))

    def both(a, b):
        return a if b is None else a & b

    def one(condition):
        return jnp.where(condition, 1, 0)

    def far(peer):
        return (peer != R) & ((quarter != C) | (peer - R >= 2) | (R - peer >= 2))

    collects = (R == per - 2) & (C == 1)
    fed = (R >= per) & (C == 0)
    gives = (R == per) & (C == 1)
    feeds = (C == 1) & (R == 0)
    spreads = (C == 1) & (R == hub)

    @pl.when(gives)
    def _():
        for row in range(per + 1, n):
            signal(barrier, row, 0)

    when(collects, signal, barrier, 0, 1)
    @pl.when(spreads)
    def _():
        for row in range(per + 1, n):
            signal(barrier, row, 1)

    when(hub - R >= 2, signal, barrier, hub, C)
    greeted = jnp.where(R == hub, R - 1, one((C == 1) & (R - hub >= 2)))
    greeted += one(((C == 0) & (R > per)) | feeds)
    for j in range(per):
        peer = per * C + j
        when(far(peer) & (peer > R), signal, barrier, peer, quarter)
        greeted += one(far(peer) & (peer < R))
    for row, there in beside:
        when(there, signal, barrier, row, C)
        greeted += 1 if there is None else one(there)
    signal(barrier, R, O)
    greeted += 1

    h_at = lax.broadcasted_iota(jnp.int32, (ch, WIDE), 0)
    l_at = lax.broadcasted_iota(jnp.int32, (ch, WIDE), 1)
    in_big = l_at < LANES
    spread = jnp.where(
        jnp.where(in_big, l_at % big, big + l_at % small) == h_at, 1.0, 0.0
    )
    lanes = lax.broadcasted_iota(jnp.int32, (1, WIDE), 1)
    phase_of = jnp.where(lanes < LANES, lanes // big, (lanes % HALF) // small)
    spread4 = jnp.where(l_at % HALF == h_at, 1.0, 0.0).astype(bf)
    phase4_of = lanes // HALF
    lane = lax.broadcasted_iota(jnp.int32, (1, LANES), 1)
    lower = lane < HALF

    def remote(src, dst, s, r, row, col):
        return pltpu.make_async_remote_copy(
            src_ref=src,
            dst_ref=dst,
            send_sem=s,
            recv_sem=r,
            device_id=(group, row, col),
            device_id_type=mesh_type,
        )

    def embed(row, col):
        collected = one((row == per - 2) & (col == 1) & (R < per))
        return remote(e_hbm, eb.at[R], send.at[at_embed], erecv.at[collected], row, col)

    pl.semaphore_wait(barrier, greeted)
    to_collector = embed(per - 2, 1)
    when(feeds, to_collector.start)
    embs, soon_sent, late = [(feeds, to_collector)], [], []
    ahead = jnp.where(gives, n - 1 - per, 0)
    for j in range(per):
        peer = per * C + j
        when(far(peer) & (peer < R), signal, mcred, peer, quarter)
        copy = embed(peer, quarter)
        wanted = far(peer) & (quarter >= C)
        embs.append((wanted, copy))
        soon_sent.append((wanted & (peer < R), copy))
        late.append((wanted & (peer > R), copy))
        ahead += one(far(peer) & (peer > R))
    when((C == 1) & (R > hub + 1), signal, ncred, hub, C)
    when((C == 0) & (R > per), signal, mcred, per, 1)
    for row in range(per - 1):
        copy = embed(row, C)
        embs.append(((R == hub) & (hub - row >= 2), copy))
        soon_sent.append(embs[-1])
    for row in range(per + 1, n):
        copy = embed(row, C)
        embs.append((spreads, copy))
        late.append((spreads, copy))
        copy = embed(row, 0)
        embs.append((gives, copy))
        late.append((gives, copy))
    for k, (row, there) in enumerate(beside):
        copy = embed(row, C)
        wanted = (quarter != C) | (lax.div(row, per) == quarter)
        wanted = both(wanted & ((C == 1) | (R != per) | (row < R)), there)
        embs.append((wanted, copy))
        when(wanted, copy.start)
    for load in loads:
        load.start()

    own_at = pl.multiple_of(SIDE * C, SIDE)
    placed = [jnp.where(phase_of == p, spread, 0.0).astype(bf) for p in range(PHASES)]
    load_m.wait()
    tile = m_ref[...].reshape(groups, PHASES, cols, ch)
    packed = mm(tile[:, 0].reshape(groups * cols, ch), placed[0])
    for p in range(1, PHASES):
        packed = packed + mm(tile[:, p].reshape(groups * cols, ch), placed[p])
    packed = packed.reshape(groups, cols, WIDE)
    for g in range(groups):
        pk[1, g, pl.ds(own_at, cols), :] = packed[g, :, :LANES].astype(bf)
    for t in range(blocks - groups):
        piece = packed[2 * t, :, LANES:]
        if 2 * t + 1 < groups:
            piece = jnp.where(lower, piece, packed[2 * t + 1, :, LANES:])
        pk[1, groups + t, pl.ds(own_at, cols), :] = piece.astype(bf)
    edge = pl.ds(pl.multiple_of(cols - SIDE - (cols - 2 * SIDE) * C, SIDE), SIDE)
    rest = pl.ds(pl.multiple_of(2 * SIDE * C, SIDE), cols - SIDE)
    side_at = pl.ds(pl.multiple_of(cols * C, SIDE), SIDE)
    halos = []
    for k, (row, there) in enumerate(beside):
        block = 2 * odd if k == 0 else 2 * (1 - odd)
        for at, part in enumerate((edge, rest)):
            halos.append(
                remote(
                    pk.at[1, :, part, :],
                    pk.at[block, :, part, :],
                    send.at[at_halo],
                    recv.at[k if at == 0 else 2],
                    row,
                    C,
                )
            )
    when(slants, halos[2].start)
    halos[0].start()
    when(slants & (C == 0), halos[3].start)
    when(C == 0, halos[1].start)
    to_side = remote(
        pk.at[1, :, edge, :], pk.at[1, :, side_at, :], send.at[at_side], recv.at[3], R, O
    )
    to_side.start()
    for wanted, copy in soon_sent:
        when(wanted, copy.start)

    def block_of(ref, s, r):
        return remote(ref, ref, s, r, R, O)

    def embeds(count, r):
        return block_of(eb.at[pl.ds(0, count)], send.at[at_embed], erecv.at[r])

    load_e.wait()

    eb[R] = e_ref[...]

    soon = quarter >= C
    when(soon & (ahead > 0), pl.semaphore_wait, mcred, ahead)
    when(spreads, pl.semaphore_wait, ncred, n - 1 - per)
    for waits, copy in late:
        when(waits, copy.start)

    def spread_rows(y, phases):
        top, bottom = y[:big], y[big:]
        first = [jnp.where(phases == p, top, 0.0) for p in range(PHASES)]
        second = [jnp.where(phases == p, bottom, 0.0) for p in range(PHASES)]
        return (
            jnp.concatenate(first, axis=0).astype(bf),
            jnp.concatenate(second, axis=0).astype(bf),
        )

    def pack_weight(w_ref, across, phases, dst, places):
        for a, at in enumerate(places):
            for b in range(3):
                first, second = spread_rows(mm(w_ref[a, b], across), phases)
                dst[at + b * LANES : at + (b + 1) * LANES, :] = first
                low = at + 3 * LANES + (0, LANES, HALF)[b]
                dst[low : low + HALF, :] = second
            dst[at + TAPS - HALF : at + TAPS, :] = jnp.zeros((HALF, WIDE), bf)

    exact = lax.Precision.HIGHEST
    for i, held in enumerate((w12_ref, wm_ref, wrc_ref, row_ref)):
        pltpu.make_async_copy(held, held, send.at[i]).wait()
    pack_weight(w1_ref, spread.astype(bf), phase_of, wa, (0, TAPS, 2 * TAPS))
    half_mix = mm(wm_ref[...], spread4) * 0.5
    mix = half_mix.astype(bf)
    pack_weight(w2_ref, mix, phase4_of, wb, (0, TAPS, 2 * TAPS + WIDE))
    first, second = spread_rows(half_mix, phase4_of)
    at = 2 * TAPS
    wb[at : at + LANES, :] = first
    wb[at + LANES : at + LANES + HALF, :] = second
    wb[at + LANES + HALF : at + WIDE, :] = jnp.zeros((HALF, WIDE), bf)
    bias1 = mm(b1_ref[...], spread, exact)
    bias2 = mm(b2_ref[...], half_mix, exact) + 0.5 * mm(bm_ref[...], spread4.astype(f32), exact)
    head = mm(wh_ref[...], spread4[:, :LANES].astype(f32), exact)
    wr = mm_tn(wr_ref[...], spread.astype(bf)).astype(bf)
    wc = mm_tn(wc_ref[...], spread.astype(bf)).astype(bf)

    whole = eb.at[pl.ds(0, per)]
    bundles = [
        remote(whole, whole, send.at[row], erecv.at[0], per + row, 0)
        for row in range(per)
    ]

    @pl.when(collects)
    def _():
        embeds(per - 1, 1).wait_recv()
        pl.semaphore_wait(mcred, ahead)
        for copy in bundles[::-1]:
            copy.start()

    relays = []
    for k, (row, there) in enumerate(beside):
        block = 2 * (1 - odd) if k == 0 else 2 * odd
        copy = remote(
            pk.at[block, :, edge, :],
            pk.at[block, :, side_at, :],
            send.at[at_side],
            recv.at[3],
            R,
            O,
        )
        relays.append((there, copy))
    halos[0].wait_recv()
    relays[0][1].start()
    when(slants, halos[2].wait_recv)
    when(slants, relays[1][1].start)

    when(slants & (C == 1), halos[3].start)
    when(C == 1, halos[1].start)
    awaited = jnp.where(fed, per, 0)
    for row in range(n):
        first = (per - 1) * C
        read = (row >= first) & (row <= first + per) & (row != R)
        read |= (row == R - 1) | (row == R + 1)
        if row < per:
            read &= jnp.logical_not(fed | collects)
        awaited += one(read)
    for count in range(1, n + 1):
        when(awaited == count, embeds(count, 0).wait_recv)
    held = -(-width // rows)
    for k in range(held):
        ct[k * rows : (k + 1) * rows, :] = mm(eb[(n - held) * C + k], wc)
    def row_terms_of(b):
        terms = mm(eb[jnp.clip(R + b - 1, 0, n - 1)], wr)
        out = []
        for g in range(groups):
            total = terms[PHASES * g : PHASES * g + 1]
            for p in range(1, PHASES):
                total = jnp.where(phase_of == p, terms[PHASES * g + p : PHASES * g + p + 1], total)
            out.append(total)
        return out

    row_terms = [row_terms_of(b) for b in range(3)]

    for count, there in ((3, slants), (2, jnp.logical_not(slants))):
        edges = block_of(pk.at[pl.ds(0, count), :, edge, :], send.at[at_side], recv.at[3])
        rests = block_of(pk.at[pl.ds(0, count - 1), :, rest, :], send.at[at_halo], recv.at[2])
        when(there, edges.wait_recv)
        when(there, rests.wait_recv)

    col_id = lax.broadcasted_iota(jnp.int32, (width, 1), 0)

    def before(v, d):
        if d % 8 == 0:
            return jnp.concatenate([jnp.zeros((d, LANES), f32), v[: width - d]], axis=0)
        return jnp.where(col_id < d, 0.0, pltpu.roll(v, d, axis=0))

    def after(v, d):
        if d % 8 == 0:
            return jnp.concatenate([v[d:], jnp.zeros((d, LANES), f32)], axis=0)
        return jnp.where(col_id >= width - d, 0.0, pltpu.roll(v, width - d, axis=0))

    def put_taps(dst, at, x, y, d):
        dst[at, :, :LANES] = before(x, d).astype(bf)
        dst[at, :, LANES : 2 * LANES] = x.astype(bf)
        dst[at, :, 2 * LANES : 3 * LANES] = after(x, d).astype(bf)
        dst[at, :, 3 * LANES : 4 * LANES] = jnp.where(lower, before(y, d), after(y, d)).astype(bf)
        dst[at, :, 4 * LANES :] = y.astype(bf)

    def base_block(b, valid):
        terms = row_terms[b]
        seconds = []
        for t in range(blocks - groups):
            g = 2 * t
            term = terms[g][:, LANES:]
            if g + 1 < groups:
                term = jnp.where(lower, term, terms[g + 1][:, LANES:])
            v = (pk[b, groups + t].astype(f32) + term + col_terms[:, LANES:]).astype(bf).astype(f32)
            turned = pltpu.roll(v, HALF, axis=1)
            seconds.append(jnp.where(lower, v, turned))
            seconds.append(jnp.where(lower, turned, v))
        for g in range(groups):
            x = pk[b, g].astype(f32) + terms[g][:, :LANES] + col_terms[:, :LANES]
            x, y = x.astype(bf).astype(f32), seconds[g]
            if valid is not None:
                x, y = jnp.where(valid, x, 0.0), jnp.where(valid, y, 0.0)
            at = b * groups + g
            xb[at, :, :LANES] = x.astype(bf)
            xb[at, :, LANES:] = y.astype(bf)
            put_taps(xs, at, jnp.maximum(x, 0.0), jnp.maximum(y, 0.0), FIRST_DILATION)

    step = FIRST_DILATION // PHASES
    step2 = SECOND_DILATION // PHASES
    ext = groups + 2 * step2
    skip = groups - step2 - step

    def first_layer(start, stop):
        left = jnp.concatenate(
            [
                xs[start + skip + a * step : stop + skip + a * step].reshape(-1, TAPS)
                for a in range(3)
            ],
            axis=1,
        )
        acc = mm(left, wa[...]).reshape(stop - start, width, WIDE)
        for u in range(start, stop):
            x = xb[u + skip + step].astype(f32) + acc[u - start] + bias1
            x = x.astype(bf).astype(f32)
            if u < step2:
                x = jnp.where(R > 0, x, 0.0)
            elif u >= step2 + groups:
                x = jnp.where(R < n - 1, x, 0.0)
            else:
                l1[u - step2] = x.astype(bf)
            x = jnp.maximum(x, 0.0)
            put_taps(xs2, u, x[:, :LANES], x[:, LANES:], SECOND_DILATION)

    col_terms = ct[pl.ds(pl.multiple_of((held * rows - width) * C, 8), width), :]
    base_block(1, None)
    base_block(0, R > 0)
    window = pl.ds(own_at, cols)

    def second_taps(a):
        return xs2[a * step2 : a * step2 + groups, window, :].reshape(groups * cols, TAPS)

    known = 2 * step2 + groups - step2
    first_layer(0, 4)
    base_block(2, R < n - 1)
    first_layer(4, known)
    left = [second_taps(0), second_taps(1), l1[:, window, :].reshape(groups * cols, WIDE)]
    mixed = mm(jnp.concatenate(left, axis=1), wb[: 2 * TAPS + WIDE])
    first_layer(known, ext)
    mixed = mixed + mm(second_taps(2), wb[2 * TAPS + WIDE :]) + bias2
    mixed = mixed.reshape(groups, cols, WIDE)

    def row_of(i):
        g, p = divmod(i, PHASES)
        at = p // 2 * LANES
        return mixed[g, :, at : at + LANES], p % 2

    for i in range(hr):
        (first, at), (second, _) = row_of(i), row_of(i + hr)
        if at == 0:
            second = pltpu.roll(second, HALF, axis=1)
        else:
            first = pltpu.roll(first, HALF, axis=1)
        pair = jnp.where(lower, first, second)
        yp[i] = pair
        for j in range(per):
            sf[j, i * rows : (i + 1) * rows, :] = pair[j * rows : (j + 1) * rows, :]
    used = hr * rows
    for j in range(per):
        sb[j, :used] = sf[j].astype(bf)

    when(jnp.logical_not(soon | collects) & (ahead > 0), pl.semaphore_wait, mcred, ahead)
    for j in range(per):
        peer = per * C + j
        is_self = (peer == R) & (quarter == C)
        copy = remote(sb.at[j], gb.at[mine], send.at[at_mirror], mrecv.at[mine], peer, quarter)
        local = pltpu.make_async_copy(sb.at[j], gb.at[j], send.at[0])

        @pl.when(jnp.logical_not(is_self))
        def _():
            copy.start()

        @pl.when(is_self)
        def _():
            local.start()

    for count, there in ((3, slants), (2, jnp.logical_not(slants))):
        edges = block_of(pk.at[pl.ds(0, count), :, edge, :], send.at[at_side], recv.at[3])
        tiles = pk.at[pl.ds(0, count - 1), :, pl.ds(own_at, cols), :]
        when(there, edges.wait_send)
        when(there, block_of(tiles, send.at[at_halo], recv.at[2]).wait_send)
    sent = 0
    for leaves, _ in embs:
        sent += one(leaves)
    for count in range(1, n + 1):
        when(sent == count, embeds(count, 0).wait_send)
    for copy in bundles:
        when(collects, copy.wait_send)

    early = lax.broadcasted_iota(jnp.int32, (used, 1), 0) % rows < hr
    for j in range(per):
        peer = per * C + j
        is_self = (peer == R) & (quarter == C)
        arrival = remote(sb.at[j], gb.at[j], send.at[at_mirror], mrecv.at[j], peer, quarter)
        local = pltpu.make_async_copy(sb.at[j], gb.at[j], send.at[0])

        @pl.when(jnp.logical_not(is_self))
        def _():
            arrival.wait_recv()

        @pl.when(is_self)
        def _():
            local.wait()

        piece = gb[j, :used].astype(f32)
        turned = pltpu.roll(piece, HALF, axis=1)
        at = 2 * j * used
        tb[at : at + used, :] = jnp.where(early, piece, turned)
        tb[at + used : at + 2 * used, :] = jnp.where(early, turned, piece)

    halves = jnp.where(
        lax.broadcasted_iota(jnp.int32, (8, WIDE), 1) % LANES // HALF
        == lax.broadcasted_iota(jnp.int32, (8, WIDE), 0),
        1.0,
        0.0,
    ).astype(bf)
    for i in range(hr):
        mirror = jnp.where(
            lower, tb[pl.ds(i, cols, stride=rows), :], tb[pl.ds(i + hr, cols, stride=rows), :]
        )
        z = jnp.maximum(yp[i] + mirror, 0.0) * head
        top = z.astype(bf)
        rest = (z - top.astype(f32)).astype(bf)
        sums = mm_nt(halves, jnp.concatenate([top, rest], axis=1))
        out_ref[i : i + 1, :] = sums[0:1]
        out_ref[i + hr : i + hr + 1, :] = sums[1:2]

    for count, there in ((per - 1, quarter == C), (per, quarter != C)):
        pieces = block_of(sb.at[pl.ds(0, count)], send.at[at_mirror], mrecv.at[0])
        when(there, pieces.wait_send)


def fused(map_in, embedding, w_row, w_col, w1, b1, w2, b2, w_mix, b_mix, w_head):
    rows, cols, ch = map_in.shape
    n = lax.axis_size("row")
    width, per, hr, groups = cols + SIDE, cols // rows, rows // 2, rows // PHASES
    blocks = groups + (groups + 1) // 2
    ext = groups + 2 * SECOND_DILATION // PHASES
    used = hr * rows
    held = -(-used // 16) * 16
    bf, f32 = jnp.bfloat16, jnp.float32
    dma = pltpu.SemaphoreType.DMA
    operands = (
        map_in,
        embedding,
        w_row.T,
        w_col.T,
        w1,
        b1.reshape(1, ch),
        w2,
        b2.reshape(1, ch),
        w_mix,
        b_mix.reshape(1, ch),
        w_head.reshape(1, ch),
    )
    return pl.pallas_call(
        functools.partial(fused_kernel, n),
        out_shape=pltpu.VMEM((rows, cols), f32),
        in_specs=[pl.BlockSpec(memory_space=pl.ANY)] * 11,
        out_specs=pl.BlockSpec(memory_space=pltpu.VMEM),
        scratch_shapes=[
            pltpu.VMEM((3, blocks, width, LANES), bf),
            pltpu.VMEM((n, rows, embedding.shape[1]), bf),
            pltpu.VMEM((-(-width // rows) * rows, WIDE), f32),
            pltpu.VMEM((3 * groups, width, WIDE), bf),
            pltpu.VMEM((3 * groups, width, TAPS), bf),
            pltpu.VMEM((groups, width, WIDE), bf),
            pltpu.VMEM((ext, width, TAPS), bf),
            pltpu.VMEM((3 * TAPS, WIDE), bf),
            pltpu.VMEM((3 * TAPS + WIDE, WIDE), bf),
            pltpu.VMEM((hr, cols, LANES), f32),
            pltpu.VMEM((per, used, LANES), f32),
            pltpu.VMEM((per, held, LANES), bf),
            pltpu.VMEM((per, held, LANES), bf),
            pltpu.VMEM((cols * rows, LANES), f32),
            dma((8,)),
            dma((4,)),
            dma((2,)),
            dma((per,)),
            pltpu.SemaphoreType.REGULAR,
            pltpu.SemaphoreType.REGULAR,
            pltpu.VMEM(map_in.shape, bf),
            pltpu.VMEM(embedding.shape, bf),
            pltpu.VMEM((2, *w_row.T.shape), bf),
            pltpu.VMEM((2, *w1.shape), bf),
            pltpu.VMEM(w_mix.shape, bf),
            pltpu.VMEM((4, 1, ch), f32),
        ],
        compiler_params=pltpu.CompilerParams(collective_id=0, has_side_effects=True),
    )(*operands)


def fits(rows, cols, channels, row_count, col_count):
    held = 2 * (cols + SIDE) * (3 * rows // PHASES) * (2 * TAPS + 2 * WIDE)
    weights = 2 * WIDE * (6 * TAPS + WIDE)
    halo = FIRST_DILATION + SECOND_DILATION
    return (
        held + weights <= FUSED_VMEM
        and rows == halo
        and row_count == 8
        and col_count == 2
        and cols % SIDE == 0
        and channels == 48
        and cols * col_count == rows * row_count
    )


def on_device(
    map_in,
    embedding,
    w_row,
    w_col,
    first_kernel_weight,
    first_bias,
    second_kernel_weight,
    second_bias,
    w_mix,
    b_mix,
    w_head,
):
    patch_rows, patch_columns, channels = map_in.shape
    row_count = lax.axis_size("row")
    if fits(patch_rows, patch_columns, channels, row_count, lax.axis_size("col")):
        return fused(
            map_in,
            embedding,
            w_row,
            w_col,
            first_kernel_weight,
            first_bias,
            second_kernel_weight,
            second_bias,
            w_mix,
            b_mix,
            w_head,
        )
    row_at = lax.axis_index("row")
    col_at = lax.axis_index("col")
    all_bins = lax.all_gather(embedding, "row", axis=0, tiled=True)
    row_terms = jnp.dot(all_bins, w_row, preferred_element_type=jnp.float32)
    col_terms = jnp.dot(all_bins, w_col, preferred_element_type=jnp.float32)
    own_rows = lax.dynamic_slice_in_dim(row_terms, row_at * patch_rows, patch_rows, 0)
    own_cols = lax.dynamic_slice_in_dim(col_terms, col_at * patch_columns, patch_columns, 0)
    contact_grid = (
        map_in.astype(jnp.float32) + own_rows[:, None, :] + own_cols[None, :, :]
    ).astype(jnp.bfloat16)
    first_padded = padded(contact_grid, (("row", 0), ("col", 1)), FIRST_DILATION)
    first_layer = (
        contact_grid.astype(jnp.float32)
        + dilated_conv(
            jnp.maximum(first_padded, 0),
            first_kernel_weight,
            FIRST_DILATION,
            patch_rows,
            patch_columns,
        )
        + first_bias
    ).astype(jnp.bfloat16)
    second_padded = padded(first_layer, (("row", 0), ("col", 1)), SECOND_DILATION)
    second_layer = (
        first_layer.astype(jnp.float32)
        + dilated_conv(
            jnp.maximum(second_padded, 0),
            second_kernel_weight,
            SECOND_DILATION,
            patch_rows,
            patch_columns,
        )
        + second_bias
    ).astype(jnp.bfloat16)
    half_rows = patch_rows // 2
    blocks_per = row_count // 2
    arranged = second_layer.reshape(2, half_rows, blocks_per, patch_rows, channels)
    arranged = arranged.transpose(0, 2, 1, 3, 4).reshape(
        2 * blocks_per, half_rows, patch_rows, channels
    )
    exchanged = lax.all_to_all(
        lax.all_to_all(arranged, "row", split_axis=0, concat_axis=0, tiled=True),
        "col",
        split_axis=0,
        concat_axis=0,
        tiled=True,
    )
    exchanged = exchanged.reshape(2, blocks_per, half_rows, patch_rows, channels)
    top_half = row_at // blocks_per
    kept_part = lax.dynamic_index_in_dim(exchanged, top_half, 0, keepdims=False)
    sent_part = lax.dynamic_index_in_dim(exchanged, 1 - top_half, 0, keepdims=False)
    came_back = swapped(sent_part, "row", blocks_per.bit_length() - 1)
    stacked = jnp.where(
        top_half == 0, jnp.stack([kept_part, came_back]), jnp.stack([came_back, kept_part])
    )
    mirrored = stacked.transpose(3, 1, 0, 2, 4).reshape(patch_rows, patch_columns, channels)
    symmetric = ((second_layer.astype(jnp.float32) + mirrored.astype(jnp.float32)) * 0.5).astype(
        jnp.bfloat16
    )
    mixture = (
        jnp.einsum("rch,hk->rck", symmetric, w_mix, preferred_element_type=jnp.float32) + b_mix
    )
    mixture = jnp.maximum(mixture, 0.0)
    return jnp.sum(mixture * w_head, axis=-1)


def solution(mesh):
    placed = (
        P(("group", "row"), "col", None),
        P(("group", "row"), None),
        P(),
        P(),
        P(),
        P(),
        P(),
        P(),
        P(),
        P(),
        P(),
    )
    return jax.shard_map(
        on_device, mesh=mesh, in_specs=placed, out_specs=P(("group", "row"), "col"), check_vma=False
    )
```

```python
import functools

import jax
import jax.numpy as jnp
from jax import lax
from jax.experimental import pallas as pl
from jax.experimental.pallas import tpu as pltpu
from jax.sharding import PartitionSpec as P

FIRST_DILATION = 4
SECOND_DILATION = 8


def padded(array, sides, width):
    for axis, dim in sides:
        peers, length = (lax.axis_size(axis), array.shape[dim])
        up = [(i, (i + 1) % peers) for i in range(peers - 1)]
        down = [(j, i) for i, j in up]
        last = lax.slice_in_dim(array, length - width, length, axis=dim)
        leading = lax.slice_in_dim(array, 0, width, axis=dim)
        before = lax.ppermute(last, axis, up)
        after = lax.ppermute(leading, axis, down)
        array = jnp.concatenate([before, array, after], axis=dim)
    return array


def swapped(value, axis, bit):
    mask = 2**bit
    pairs = [(source, source ^ mask) for source in range(lax.axis_size(axis))]
    return lax.ppermute(value, axis, pairs)


def dilated_conv(active, weight, spacing, out_rows, out_cols):
    windows = []
    for tap_row in range(3):
        for tap_col in range(3):
            windows.append(
                active[
                    tap_row * spacing : tap_row * spacing + out_rows,
                    tap_col * spacing : tap_col * spacing + out_cols,
                ]
            )
    stacked = jnp.concatenate(windows, axis=-1)
    flat_weight = weight.reshape(9 * weight.shape[2], weight.shape[3])
    return jnp.einsum("rch,hk->rck", stacked, flat_weight, preferred_element_type=jnp.float32)


LANES = 128
HALF = 64
SIDE = 16
PHASES = 4
WIDE = 2 * LANES
TAPS = 5 * LANES
FUSED_VMEM = 8 * 2**20


def one_hot(rows, columns, offsets):
    r = lax.broadcasted_iota(jnp.int32, (rows, columns), 0)
    c = lax.broadcasted_iota(jnp.int32, (rows, columns), 1)
    hit = c == r + offsets[0]
    for offset in offsets[1:]:
        hit = hit | (c == r + offset)
    return jnp.where(hit, 1.0, 0.0)


def mm(a, b, precision=None):
    return jnp.dot(a, b, preferred_element_type=jnp.float32, precision=precision)


def mm_tn(a, b):
    return lax.dot_general(a, b, (((0,), (0,)), ((), ())), preferred_element_type=jnp.float32)


def mm_nt(a, b):
    return lax.dot_general(a, b, (((1,), (1,)), ((), ())), preferred_element_type=jnp.float32)


def fused_kernel(
    n,
    m_hbm,
    e_hbm,
    wr_hbm,
    wc_hbm,
    w1_hbm,
    b1_hbm,
    w2_hbm,
    b2_hbm,
    wm_hbm,
    bm_hbm,
    wh_hbm,
    out_ref,
    pk,
    eb,
    ct,
    xb,
    xs,
    l1,
    xs2,
    wa,
    wb,
    yp,
    sf,
    sb,
    gb,
    tb,
    send,
    recv,
    erecv,
    mrecv,
    mcred,
    ncred,
    m_ref,
    e_ref,
    wrc_ref,
    w12_ref,
    wm_ref,
    row_ref,
):
    bf, f32 = jnp.bfloat16, jnp.float32
    rows, cols, ch = m_ref.shape
    hr = rows // 2
    groups = rows // PHASES
    blocks = pk.shape[1]
    width = cols + SIDE
    per = cols // rows
    big = LANES // PHASES
    small = ch - big
    R = lax.axis_index("row")
    C = lax.axis_index("col")
    O = 1 - C
    group = lax.axis_index("group")
    mesh_type = pl.DeviceIdType.MESH

    at_side, at_mirror, at_halo, at_embed = 4, 5, 6, 7
    wr_ref, wc_ref = wrc_ref.at[0], wrc_ref.at[1]
    w1_ref, w2_ref = w12_ref.at[0], w12_ref.at[1]
    b1_ref, b2_ref, bm_ref, wh_ref = (row_ref.at[i] for i in range(4))
    groups_of = (
        ((w1_hbm, w1_ref), (w2_hbm, w2_ref)),
        ((wm_hbm, wm_ref),),
        ((wr_hbm, wr_ref), (wc_hbm, wc_ref)),
        ((b1_hbm, b1_ref), (b2_hbm, b2_ref), (bm_hbm, bm_ref), (wh_hbm, wh_ref)),
    )
    loads = [
        pltpu.make_async_copy(a, b, send.at[i]) for i, pairs in enumerate(groups_of) for a, b in pairs
    ]
    load_m = pltpu.make_async_copy(m_hbm, m_ref, send.at[at_side])
    load_e = pltpu.make_async_copy(e_hbm, e_ref, send.at[at_mirror])
    load_m.start()
    load_e.start()
    eb[...] = jnp.zeros_like(eb)
    quarter = lax.div(R, per)
    mine = lax.rem(R, per)
    odd = lax.rem(R, 2)
    hub = per - C
    across, slant = R + 1 - 2 * odd, R - 1 + 2 * odd
    slants = (slant >= 0) & (slant < n)
    slant = jnp.clip(slant, 0, n - 1)
    beside = ((across, None), (slant, slants))
    barrier = pltpu.get_barrier_semaphore()

    def signal(sem, row, col):
        pl.semaphore_signal(sem, inc=1, device_id=(group, row, col), device_id_type=mesh_type)

    def when(condition, act, *args):
        if condition is None:
            act(*args)
        else:
            pl.when(condition)(functools.partial(act, *args))

    def both(a, b):
        return a if b is None else a & b

    def one(condition):
        return jnp.where(condition, 1, 0)

    def far(peer):
        return (peer != R) & ((quarter != C) | (peer - R >= 2) | (R - peer >= 2))

    collects = (R == per - 2) & (C == 1)
    fed = (R >= per) & (C == 0)
    gives = (R == per) & (C == 1)
    feeds = (C == 1) & (R == 0)
    spreads = (C == 1) & (R == hub)

    @pl.when(gives)
    def _():
        for row in range(per + 1, n):
            signal(barrier, row, 0)

    when(collects, signal, barrier, 0, 1)
    @pl.when(spreads)
    def _():
        for row in range(per + 1, n):
            signal(barrier, row, 1)

    when(hub - R >= 2, signal, barrier, hub, C)
    greeted = jnp.where(R == hub, R - 1, one((C == 1) & (R - hub >= 2)))
    greeted += one(((C == 0) & (R > per)) | feeds)
    for j in range(per):
        peer = per * C + j
        when(far(peer) & (peer > R), signal, barrier, peer, quarter)
        greeted += one(far(peer) & (peer < R))
    for row, there in beside:
        when(there, signal, barrier, row, C)
        greeted += 1 if there is None else one(there)
    signal(barrier, R, O)
    greeted += 1

    h_at = lax.broadcasted_iota(jnp.int32, (ch, WIDE), 0)
    l_at = lax.broadcasted_iota(jnp.int32, (ch, WIDE), 1)
    in_big = l_at < LANES
    spread = jnp.where(
        jnp.where(in_big, l_at % big, big + l_at % small) == h_at, 1.0, 0.0
    )
    lanes = lax.broadcasted_iota(jnp.int32, (1, WIDE), 1)
    phase_of = jnp.where(lanes < LANES, lanes // big, (lanes % HALF) // small)
    spread4 = jnp.where(l_at % HALF == h_at, 1.0, 0.0).astype(bf)
    phase4_of = lanes // HALF
    lane = lax.broadcasted_iota(jnp.int32, (1, LANES), 1)
    lower = lane < HALF

    def remote(src, dst, s, r, row, col):
        return pltpu.make_async_remote_copy(
            src_ref=src,
            dst_ref=dst,
            send_sem=s,
            recv_sem=r,
            device_id=(group, row, col),
            device_id_type=mesh_type,
        )

    def embed(row, col):
        collected = one((row == per - 2) & (col == 1) & (R < per))
        return remote(e_hbm, eb.at[R], send.at[at_embed], erecv.at[collected], row, col)

    pl.semaphore_wait(barrier, greeted)
    to_collector = embed(per - 2, 1)
    when(feeds, to_collector.start)
    embs, soon_sent, late = [(feeds, to_collector)], [], []
    ahead = jnp.where(gives, n - 1 - per, 0)
    for j in range(per):
        peer = per * C + j
        when(far(peer) & (peer < R), signal, mcred, peer, quarter)
        copy = embed(peer, quarter)
        wanted = far(peer) & (quarter >= C)
        embs.append((wanted, copy))
        soon_sent.append((wanted & (peer < R), copy))
        late.append((wanted & (peer > R), copy))
        ahead += one(far(peer) & (peer > R))
    when((C == 1) & (R > hub + 1), signal, ncred, hub, C)
    when((C == 0) & (R > per), signal, mcred, per, 1)
    for row in range(per - 1):
        copy = embed(row, C)
        embs.append(((R == hub) & (hub - row >= 2), copy))
        soon_sent.append(embs[-1])
    for row in range(per + 1, n):
        copy = embed(row, C)
        embs.append((spreads, copy))
        late.append((spreads, copy))
        copy = embed(row, 0)
        embs.append((gives, copy))
        late.append((gives, copy))
    for k, (row, there) in enumerate(beside):
        copy = embed(row, C)
        wanted = (quarter != C) | (lax.div(row, per) == quarter)
        wanted = both(wanted & ((C == 1) | (R != per) | (row < R)), there)
        embs.append((wanted, copy))
        when(wanted, copy.start)
    for load in loads:
        load.start()

    own_at = pl.multiple_of(SIDE * C, SIDE)
    placed = [jnp.where(phase_of == p, spread, 0.0).astype(bf) for p in range(PHASES)]
    load_m.wait()
    tile = m_ref[...].reshape(groups, PHASES, cols, ch)
    packed = mm(tile[:, 0].reshape(groups * cols, ch), placed[0])
    for p in range(1, PHASES):
        packed = packed + mm(tile[:, p].reshape(groups * cols, ch), placed[p])
    packed = packed.reshape(groups, cols, WIDE)
    for g in range(groups):
        pk[1, g, pl.ds(own_at, cols), :] = packed[g, :, :LANES].astype(bf)
    for t in range(blocks - groups):
        piece = packed[2 * t, :, LANES:]
        if 2 * t + 1 < groups:
            piece = jnp.where(lower, piece, packed[2 * t + 1, :, LANES:])
        pk[1, groups + t, pl.ds(own_at, cols), :] = piece.astype(bf)
    edge = pl.ds(pl.multiple_of(cols - SIDE - (cols - 2 * SIDE) * C, SIDE), SIDE)
    rest = pl.ds(pl.multiple_of(2 * SIDE * C, SIDE), cols - SIDE)
    side_at = pl.ds(pl.multiple_of(cols * C, SIDE), SIDE)
    halos = []
    for k, (row, there) in enumerate(beside):
        block = 2 * odd if k == 0 else 2 * (1 - odd)
        for at, part in enumerate((edge, rest)):
            halos.append(
                remote(
                    pk.at[1, :, part, :],
                    pk.at[block, :, part, :],
                    send.at[at_halo],
                    recv.at[k if at == 0 else 2],
                    row,
                    C,
                )
            )
    when(slants, halos[2].start)
    halos[0].start()
    when(slants & (C == 0), halos[3].start)
    when(C == 0, halos[1].start)
    to_side = remote(
        pk.at[1, :, edge, :], pk.at[1, :, side_at, :], send.at[at_side], recv.at[3], R, O
    )
    to_side.start()
    for wanted, copy in soon_sent:
        when(wanted, copy.start)

    def block_of(ref, s, r):
        return remote(ref, ref, s, r, R, O)

    def embeds(count, r):
        return block_of(eb.at[pl.ds(0, count)], send.at[at_embed], erecv.at[r])

    load_e.wait()

    eb[R] = e_ref[...]

    soon = quarter >= C
    when(soon & (ahead > 0), pl.semaphore_wait, mcred, ahead)
    when(spreads, pl.semaphore_wait, ncred, n - 1 - per)
    for waits, copy in late:
        when(waits, copy.start)

    def spread_rows(y, phases):
        top, bottom = y[:big], y[big:]
        first = [jnp.where(phases == p, top, 0.0) for p in range(PHASES)]
        second = [jnp.where(phases == p, bottom, 0.0) for p in range(PHASES)]
        return (
            jnp.concatenate(first, axis=0).astype(bf),
            jnp.concatenate(second, axis=0).astype(bf),
        )

    def pack_weight(w_ref, across, phases, dst, places):
        for a, at in enumerate(places):
            for b in range(3):
                first, second = spread_rows(mm(w_ref[a, b], across), phases)
                dst[at + b * LANES : at + (b + 1) * LANES, :] = first
                low = at + 3 * LANES + (0, LANES, HALF)[b]
                dst[low : low + HALF, :] = second
            dst[at + TAPS - HALF : at + TAPS, :] = jnp.zeros((HALF, WIDE), bf)

    exact = lax.Precision.HIGHEST
    for i, held in enumerate((w12_ref, wm_ref, wrc_ref, row_ref)):
        pltpu.make_async_copy(held, held, send.at[i]).wait()
    pack_weight(w1_ref, spread.astype(bf), phase_of, wa, (0, TAPS, 2 * TAPS))
    half_mix = mm(wm_ref[...], spread4) * 0.5
    mix = half_mix.astype(bf)
    pack_weight(w2_ref, mix, phase4_of, wb, (0, TAPS, 2 * TAPS + WIDE))
    first, second = spread_rows(half_mix, phase4_of)
    at = 2 * TAPS
    wb[at : at + LANES, :] = first
    wb[at + LANES : at + LANES + HALF, :] = second
    wb[at + LANES + HALF : at + WIDE, :] = jnp.zeros((HALF, WIDE), bf)
    bias1 = mm(b1_ref[...], spread, exact)
    bias2 = mm(b2_ref[...], half_mix, exact) + 0.5 * mm(bm_ref[...], spread4.astype(f32), exact)
    head = mm(wh_ref[...], spread4[:, :LANES].astype(f32), exact)
    wr = mm_tn(wr_ref[...], spread.astype(bf)).astype(bf)
    wc = mm_tn(wc_ref[...], spread.astype(bf)).astype(bf)

    whole = eb.at[pl.ds(0, per)]
    bundles = [
        remote(whole, whole, send.at[row], erecv.at[0], per + row, 0)
        for row in range(per)
    ]

    @pl.when(collects)
    def _():
        embeds(per - 1, 1).wait_recv()
        pl.semaphore_wait(mcred, ahead)
        for copy in bundles[::-1]:
            copy.start()

    relays = []
    for k, (row, there) in enumerate(beside):
        block = 2 * (1 - odd) if k == 0 else 2 * odd
        copy = remote(
            pk.at[block, :, edge, :],
            pk.at[block, :, side_at, :],
            send.at[at_side],
            recv.at[3],
            R,
            O,
        )
        relays.append((there, copy))
    halos[0].wait_recv()
    relays[0][1].start()
    when(slants, halos[2].wait_recv)
    when(slants, relays[1][1].start)

    when(slants & (C == 1), halos[3].start)
    when(C == 1, halos[1].start)
    awaited = jnp.where(fed, per, 0)
    for row in range(n):
        first = (per - 1) * C
        read = (row >= first) & (row <= first + per) & (row != R)
        read |= (row == R - 1) | (row == R + 1)
        if row < per:
            read &= jnp.logical_not(fed | collects)
        awaited += one(read)
    for count in range(1, n + 1):
        when(awaited == count, embeds(count, 0).wait_recv)
    held = -(-width // rows)
    for k in range(held):
        ct[k * rows : (k + 1) * rows, :] = mm(eb[(n - held) * C + k], wc)
    def row_terms_of(b):
        terms = mm(eb[jnp.clip(R + b - 1, 0, n - 1)], wr)
        out = []
        for g in range(groups):
            total = terms[PHASES * g : PHASES * g + 1]
            for p in range(1, PHASES):
                total = jnp.where(phase_of == p, terms[PHASES * g + p : PHASES * g + p + 1], total)
            out.append(total)
        return out

    row_terms = [row_terms_of(b) for b in range(3)]

    for count, there in ((3, slants), (2, jnp.logical_not(slants))):
        edges = block_of(pk.at[pl.ds(0, count), :, edge, :], send.at[at_side], recv.at[3])
        rests = block_of(pk.at[pl.ds(0, count - 1), :, rest, :], send.at[at_halo], recv.at[2])
        when(there, edges.wait_recv)
        when(there, rests.wait_recv)

    col_id = lax.broadcasted_iota(jnp.int32, (width, 1), 0)

    def before(v, d):
        if d % 8 == 0:
            return jnp.concatenate([jnp.zeros((d, LANES), f32), v[: width - d]], axis=0)
        return jnp.where(col_id < d, 0.0, pltpu.roll(v, d, axis=0))

    def after(v, d):
        if d % 8 == 0:
            return jnp.concatenate([v[d:], jnp.zeros((d, LANES), f32)], axis=0)
        return jnp.where(col_id >= width - d, 0.0, pltpu.roll(v, width - d, axis=0))

    def put_taps(dst, at, x, y, d):
        dst[at, :, :LANES] = before(x, d).astype(bf)
        dst[at, :, LANES : 2 * LANES] = x.astype(bf)
        dst[at, :, 2 * LANES : 3 * LANES] = after(x, d).astype(bf)
        dst[at, :, 3 * LANES : 4 * LANES] = jnp.where(lower, before(y, d), after(y, d)).astype(bf)
        dst[at, :, 4 * LANES :] = y.astype(bf)

    def base_block(b, valid):
        terms = row_terms[b]
        seconds = []
        for t in range(blocks - groups):
            g = 2 * t
            term = terms[g][:, LANES:]
            if g + 1 < groups:
                term = jnp.where(lower, term, terms[g + 1][:, LANES:])
            v = (pk[b, groups + t].astype(f32) + term + col_terms[:, LANES:]).astype(bf).astype(f32)
            turned = pltpu.roll(v, HALF, axis=1)
            seconds.append(jnp.where(lower, v, turned))
            seconds.append(jnp.where(lower, turned, v))
        for g in range(groups):
            x = pk[b, g].astype(f32) + terms[g][:, :LANES] + col_terms[:, :LANES]
            x, y = x.astype(bf).astype(f32), seconds[g]
            if valid is not None:
                x, y = jnp.where(valid, x, 0.0), jnp.where(valid, y, 0.0)
            at = b * groups + g
            xb[at, :, :LANES] = x.astype(bf)
            xb[at, :, LANES:] = y.astype(bf)
            put_taps(xs, at, jnp.maximum(x, 0.0), jnp.maximum(y, 0.0), FIRST_DILATION)

    step = FIRST_DILATION // PHASES
    step2 = SECOND_DILATION // PHASES
    ext = groups + 2 * step2
    skip = groups - step2 - step

    def first_layer(start, stop):
        left = jnp.concatenate(
            [
                xs[start + skip + a * step : stop + skip + a * step].reshape(-1, TAPS)
                for a in range(3)
            ],
            axis=1,
        )
        acc = mm(left, wa[...]).reshape(stop - start, width, WIDE)
        for u in range(start, stop):
            x = xb[u + skip + step].astype(f32) + acc[u - start] + bias1
            x = x.astype(bf).astype(f32)
            if u < step2:
                x = jnp.where(R > 0, x, 0.0)
            elif u >= step2 + groups:
                x = jnp.where(R < n - 1, x, 0.0)
            else:
                l1[u - step2] = x.astype(bf)
            x = jnp.maximum(x, 0.0)
            put_taps(xs2, u, x[:, :LANES], x[:, LANES:], SECOND_DILATION)

    col_terms = ct[pl.ds(pl.multiple_of((held * rows - width) * C, 8), width), :]
    base_block(1, None)
    base_block(0, R > 0)
    window = pl.ds(own_at, cols)

    def second_taps(a):
        return xs2[a * step2 : a * step2 + groups, window, :].reshape(groups * cols, TAPS)

    known = 2 * step2 + groups - step2
    first_layer(0, 4)
    base_block(2, R < n - 1)
    first_layer(4, known)
    left = [second_taps(0), second_taps(1), l1[:, window, :].reshape(groups * cols, WIDE)]
    mixed = mm(jnp.concatenate(left, axis=1), wb[: 2 * TAPS + WIDE])
    first_layer(known, ext)
    mixed = mixed + mm(second_taps(2), wb[2 * TAPS + WIDE :]) + bias2
    mixed = mixed.reshape(groups, cols, WIDE)

    def row_of(i):
        g, p = divmod(i, PHASES)
        at = p // 2 * LANES
        return mixed[g, :, at : at + LANES], p % 2

    for i in range(hr):
        (first, at), (second, _) = row_of(i), row_of(i + hr)
        if at == 0:
            second = pltpu.roll(second, HALF, axis=1)
        else:
            first = pltpu.roll(first, HALF, axis=1)
        pair = jnp.where(lower, first, second)
        yp[i] = pair
        for j in range(per):
            sb[j, i * rows : (i + 1) * rows, :] = pair[j * rows : (j + 1) * rows, :].astype(bf)
    used = hr * rows

    when(jnp.logical_not(soon | collects) & (ahead > 0), pl.semaphore_wait, mcred, ahead)
    for j in range(per):
        peer = per * C + j
        is_self = (peer == R) & (quarter == C)
        copy = remote(sb.at[j], gb.at[mine], send.at[at_mirror], mrecv.at[mine], peer, quarter)
        local = pltpu.make_async_copy(sb.at[j], gb.at[j], send.at[0])

        @pl.when(jnp.logical_not(is_self))
        def _():
            copy.start()

        @pl.when(is_self)
        def _():
            local.start()

    for count, there in ((3, slants), (2, jnp.logical_not(slants))):
        edges = block_of(pk.at[pl.ds(0, count), :, edge, :], send.at[at_side], recv.at[3])
        tiles = pk.at[pl.ds(0, count - 1), :, pl.ds(own_at, cols), :]
        when(there, edges.wait_send)
        when(there, block_of(tiles, send.at[at_halo], recv.at[2]).wait_send)
    sent = 0
    for leaves, _ in embs:
        sent += one(leaves)
    for count in range(1, n + 1):
        when(sent == count, embeds(count, 0).wait_send)
    for copy in bundles:
        when(collects, copy.wait_send)

    early = lax.broadcasted_iota(jnp.int32, (used, 1), 0) % rows < hr
    for j in range(per):
        peer = per * C + j
        is_self = (peer == R) & (quarter == C)
        arrival = remote(sb.at[j], gb.at[j], send.at[at_mirror], mrecv.at[j], peer, quarter)
        local = pltpu.make_async_copy(sb.at[j], gb.at[j], send.at[0])

        @pl.when(jnp.logical_not(is_self))
        def _():
            arrival.wait_recv()

        @pl.when(is_self)
        def _():
            local.wait()

        piece = gb[j, :used].astype(f32)
        turned = pltpu.roll(piece, HALF, axis=1)
        at = 2 * j * used
        tb[at : at + used, :] = jnp.where(early, piece, turned)
        tb[at + used : at + 2 * used, :] = jnp.where(early, turned, piece)

    halves = jnp.where(
        lax.broadcasted_iota(jnp.int32, (8, WIDE), 1) % LANES // HALF
        == lax.broadcasted_iota(jnp.int32, (8, WIDE), 0),
        1.0,
        0.0,
    ).astype(bf)
    for i in range(hr):
        mirror = jnp.where(
            lower, tb[pl.ds(i, cols, stride=rows), :], tb[pl.ds(i + hr, cols, stride=rows), :]
        )
        z = jnp.maximum(yp[i] + mirror, 0.0) * head
        top = z.astype(bf)
        rest = (z - top.astype(f32)).astype(bf)
        sums = mm_nt(halves, jnp.concatenate([top, rest], axis=1))
        out_ref[i : i + 1, :] = sums[0:1]
        out_ref[i + hr : i + hr + 1, :] = sums[1:2]

    for count, there in ((per - 1, quarter == C), (per, quarter != C)):
        pieces = block_of(sb.at[pl.ds(0, count)], send.at[at_mirror], mrecv.at[0])
        when(there, pieces.wait_send)


def fused(map_in, embedding, w_row, w_col, w1, b1, w2, b2, w_mix, b_mix, w_head):
    rows, cols, ch = map_in.shape
    n = lax.axis_size("row")
    width, per, hr, groups = cols + SIDE, cols // rows, rows // 2, rows // PHASES
    blocks = groups + (groups + 1) // 2
    ext = groups + 2 * SECOND_DILATION // PHASES
    used = hr * rows
    held = used
    bf, f32 = jnp.bfloat16, jnp.float32
    dma = pltpu.SemaphoreType.DMA
    operands = (
        map_in,
        embedding,
        w_row.T,
        w_col.T,
        w1,
        b1.reshape(1, ch),
        w2,
        b2.reshape(1, ch),
        w_mix,
        b_mix.reshape(1, ch),
        w_head.reshape(1, ch),
    )
    return pl.pallas_call(
        functools.partial(fused_kernel, n),
        out_shape=pltpu.VMEM((rows, cols), f32),
        in_specs=[pl.BlockSpec(memory_space=pl.ANY)] * 11,
        out_specs=pl.BlockSpec(memory_space=pltpu.VMEM),
        scratch_shapes=[
            pltpu.VMEM((3, blocks, width, LANES), bf),
            pltpu.VMEM((n, rows, embedding.shape[1]), bf),
            pltpu.VMEM((-(-width // rows) * rows, WIDE), f32),
            pltpu.VMEM((3 * groups, width, WIDE), bf),
            pltpu.VMEM((3 * groups, width, TAPS), bf),
            pltpu.VMEM((groups, width, WIDE), bf),
            pltpu.VMEM((ext, width, TAPS), bf),
            pltpu.VMEM((3 * TAPS, WIDE), bf),
            pltpu.VMEM((3 * TAPS + WIDE, WIDE), bf),
            pltpu.VMEM((hr, cols, LANES), f32),
            pltpu.VMEM((per, used, LANES), f32),
            pltpu.VMEM((per, held, LANES), bf),
            pltpu.VMEM((per, held, LANES), bf),
            pltpu.VMEM((cols * rows, LANES), f32),
            dma((8,)),
            dma((4,)),
            dma((2,)),
            dma((per,)),
            pltpu.SemaphoreType.REGULAR,
            pltpu.SemaphoreType.REGULAR,
            pltpu.VMEM(map_in.shape, bf),
            pltpu.VMEM(embedding.shape, bf),
            pltpu.VMEM((2, *w_row.T.shape), bf),
            pltpu.VMEM((2, *w1.shape), bf),
            pltpu.VMEM(w_mix.shape, bf),
            pltpu.VMEM((4, 1, ch), f32),
        ],
        compiler_params=pltpu.CompilerParams(collective_id=0, has_side_effects=True),
    )(*operands)


def fits(rows, cols, channels, row_count, col_count):
    held = 2 * (cols + SIDE) * (3 * rows // PHASES) * (2 * TAPS + 2 * WIDE)
    weights = 2 * WIDE * (6 * TAPS + WIDE)
    halo = FIRST_DILATION + SECOND_DILATION
    return (
        held + weights <= FUSED_VMEM
        and rows == halo
        and row_count == 8
        and col_count == 2
        and cols % SIDE == 0
        and channels == 48
        and cols * col_count == rows * row_count
    )


def on_device(
    map_in,
    embedding,
    w_row,
    w_col,
    first_kernel_weight,
    first_bias,
    second_kernel_weight,
    second_bias,
    w_mix,
    b_mix,
    w_head,
):
    patch_rows, patch_columns, channels = map_in.shape
    row_count = lax.axis_size("row")
    if fits(patch_rows, patch_columns, channels, row_count, lax.axis_size("col")):
        return fused(
            map_in,
            embedding,
            w_row,
            w_col,
            first_kernel_weight,
            first_bias,
            second_kernel_weight,
            second_bias,
            w_mix,
            b_mix,
            w_head,
        )
    row_at = lax.axis_index("row")
    col_at = lax.axis_index("col")
    all_bins = lax.all_gather(embedding, "row", axis=0, tiled=True)
    row_terms = jnp.dot(all_bins, w_row, preferred_element_type=jnp.float32)
    col_terms = jnp.dot(all_bins, w_col, preferred_element_type=jnp.float32)
    own_rows = lax.dynamic_slice_in_dim(row_terms, row_at * patch_rows, patch_rows, 0)
    own_cols = lax.dynamic_slice_in_dim(col_terms, col_at * patch_columns, patch_columns, 0)
    contact_grid = (
        map_in.astype(jnp.float32) + own_rows[:, None, :] + own_cols[None, :, :]
    ).astype(jnp.bfloat16)
    first_padded = padded(contact_grid, (("row", 0), ("col", 1)), FIRST_DILATION)
    first_layer = (
        contact_grid.astype(jnp.float32)
        + dilated_conv(
            jnp.maximum(first_padded, 0),
            first_kernel_weight,
            FIRST_DILATION,
            patch_rows,
            patch_columns,
        )
        + first_bias
    ).astype(jnp.bfloat16)
    second_padded = padded(first_layer, (("row", 0), ("col", 1)), SECOND_DILATION)
    second_layer = (
        first_layer.astype(jnp.float32)
        + dilated_conv(
            jnp.maximum(second_padded, 0),
            second_kernel_weight,
            SECOND_DILATION,
            patch_rows,
            patch_columns,
        )
        + second_bias
    ).astype(jnp.bfloat16)
    half_rows = patch_rows // 2
    blocks_per = row_count // 2
    arranged = second_layer.reshape(2, half_rows, blocks_per, patch_rows, channels)
    arranged = arranged.transpose(0, 2, 1, 3, 4).reshape(
        2 * blocks_per, half_rows, patch_rows, channels
    )
    exchanged = lax.all_to_all(
        lax.all_to_all(arranged, "row", split_axis=0, concat_axis=0, tiled=True),
        "col",
        split_axis=0,
        concat_axis=0,
        tiled=True,
    )
    exchanged = exchanged.reshape(2, blocks_per, half_rows, patch_rows, channels)
    top_half = row_at // blocks_per
    kept_part = lax.dynamic_index_in_dim(exchanged, top_half, 0, keepdims=False)
    sent_part = lax.dynamic_index_in_dim(exchanged, 1 - top_half, 0, keepdims=False)
    came_back = swapped(sent_part, "row", blocks_per.bit_length() - 1)
    stacked = jnp.where(
        top_half == 0, jnp.stack([kept_part, came_back]), jnp.stack([came_back, kept_part])
    )
    mirrored = stacked.transpose(3, 1, 0, 2, 4).reshape(patch_rows, patch_columns, channels)
    symmetric = ((second_layer.astype(jnp.float32) + mirrored.astype(jnp.float32)) * 0.5).astype(
        jnp.bfloat16
    )
    mixture = (
        jnp.einsum("rch,hk->rck", symmetric, w_mix, preferred_element_type=jnp.float32) + b_mix
    )
    mixture = jnp.maximum(mixture, 0.0)
    return jnp.sum(mixture * w_head, axis=-1)


def solution(mesh):
    placed = (
        P(("group", "row"), "col", None),
        P(("group", "row"), None),
        P(),
        P(),
        P(),
        P(),
        P(),
        P(),
        P(),
        P(),
        P(),
    )
    return jax.shard_map(
        on_device, mesh=mesh, in_specs=placed, out_specs=P(("group", "row"), "col"), check_vma=False
    )
```

```python
import functools

import jax
import jax.numpy as jnp
from jax import lax
from jax.experimental import pallas as pl
from jax.experimental.pallas import tpu as pltpu
from jax.sharding import PartitionSpec as P

FIRST_DILATION = 4
SECOND_DILATION = 8


def padded(array, sides, width):
    for axis, dim in sides:
        peers, length = (lax.axis_size(axis), array.shape[dim])
        up = [(i, (i + 1) % peers) for i in range(peers - 1)]
        down = [(j, i) for i, j in up]
        last = lax.slice_in_dim(array, length - width, length, axis=dim)
        leading = lax.slice_in_dim(array, 0, width, axis=dim)
        before = lax.ppermute(last, axis, up)
        after = lax.ppermute(leading, axis, down)
        array = jnp.concatenate([before, array, after], axis=dim)
    return array


def swapped(value, axis, bit):
    mask = 2**bit
    pairs = [(source, source ^ mask) for source in range(lax.axis_size(axis))]
    return lax.ppermute(value, axis, pairs)


def dilated_conv(active, weight, spacing, out_rows, out_cols):
    windows = []
    for tap_row in range(3):
        for tap_col in range(3):
            windows.append(
                active[
                    tap_row * spacing : tap_row * spacing + out_rows,
                    tap_col * spacing : tap_col * spacing + out_cols,
                ]
            )
    stacked = jnp.concatenate(windows, axis=-1)
    flat_weight = weight.reshape(9 * weight.shape[2], weight.shape[3])
    return jnp.einsum("rch,hk->rck", stacked, flat_weight, preferred_element_type=jnp.float32)


LANES = 128
HALF = 64
SIDE = 16
PHASES = 4
WIDE = 2 * LANES
TAPS = 5 * LANES
FUSED_VMEM = 8 * 2**20


def one_hot(rows, columns, offsets):
    r = lax.broadcasted_iota(jnp.int32, (rows, columns), 0)
    c = lax.broadcasted_iota(jnp.int32, (rows, columns), 1)
    hit = c == r + offsets[0]
    for offset in offsets[1:]:
        hit = hit | (c == r + offset)
    return jnp.where(hit, 1.0, 0.0)


def mm(a, b, precision=None):
    return jnp.dot(a, b, preferred_element_type=jnp.float32, precision=precision)


def mm_tn(a, b):
    return lax.dot_general(a, b, (((0,), (0,)), ((), ())), preferred_element_type=jnp.float32)


def mm_nt(a, b):
    return lax.dot_general(a, b, (((1,), (1,)), ((), ())), preferred_element_type=jnp.float32)


def fused_kernel(
    n,
    m_hbm,
    e_hbm,
    wr_hbm,
    wc_hbm,
    w1_hbm,
    b1_hbm,
    w2_hbm,
    b2_hbm,
    wm_hbm,
    bm_hbm,
    wh_hbm,
    out_ref,
    pk,
    eb,
    ct,
    xb,
    xs,
    l1,
    xs2,
    wa,
    wb,
    yp,
    sf,
    sb,
    gb,
    tb,
    send,
    recv,
    erecv,
    mrecv,
    mcred,
    ncred,
    m_ref,
    e_ref,
    wrc_ref,
    w12_ref,
    wm_ref,
    row_ref,
):
    bf, f32 = jnp.bfloat16, jnp.float32
    rows, cols, ch = m_ref.shape
    hr = rows // 2
    groups = rows // PHASES
    blocks = pk.shape[1]
    width = cols + SIDE
    per = cols // rows
    big = LANES // PHASES
    small = ch - big
    R = lax.axis_index("row")
    C = lax.axis_index("col")
    O = 1 - C
    group = lax.axis_index("group")
    mesh_type = pl.DeviceIdType.MESH

    at_side, at_mirror, at_halo, at_embed = 4, 5, 6, 7
    wr_ref, wc_ref = wrc_ref.at[0], wrc_ref.at[1]
    w1_ref, w2_ref = w12_ref.at[0], w12_ref.at[1]
    b1_ref, b2_ref, bm_ref, wh_ref = (row_ref.at[i] for i in range(4))
    groups_of = (
        ((w1_hbm, w1_ref), (w2_hbm, w2_ref)),
        ((wm_hbm, wm_ref),),
        ((wr_hbm, wr_ref), (wc_hbm, wc_ref)),
        ((b1_hbm, b1_ref), (b2_hbm, b2_ref), (bm_hbm, bm_ref), (wh_hbm, wh_ref)),
    )
    loads = [
        pltpu.make_async_copy(a, b, send.at[i]) for i, pairs in enumerate(groups_of) for a, b in pairs
    ]
    load_m = pltpu.make_async_copy(m_hbm, m_ref, send.at[at_side])
    load_e = pltpu.make_async_copy(e_hbm, e_ref, send.at[at_mirror])
    load_m.start()
    load_e.start()
    eb[...] = jnp.zeros_like(eb)
    quarter = lax.div(R, per)
    mine = lax.rem(R, per)
    odd = lax.rem(R, 2)
    hub = per - C
    across, slant = R + 1 - 2 * odd, R - 1 + 2 * odd
    slants = (slant >= 0) & (slant < n)
    slant = jnp.clip(slant, 0, n - 1)
    beside = ((across, None), (slant, slants))
    barrier = pltpu.get_barrier_semaphore()

    def signal(sem, row, col):
        pl.semaphore_signal(sem, inc=1, device_id=(group, row, col), device_id_type=mesh_type)

    def when(condition, act, *args):
        if condition is None:
            act(*args)
        else:
            pl.when(condition)(functools.partial(act, *args))

    def both(a, b):
        return a if b is None else a & b

    def one(condition):
        return jnp.where(condition, 1, 0)

    def far(peer):
        return (peer != R) & ((quarter != C) | (peer - R >= 2) | (R - peer >= 2))

    collects = (R == per - 2) & (C == 1)
    fed = (R >= per) & (C == 0)
    gives = (R == per) & (C == 1)
    feeds = (C == 1) & (R == 0)
    spreads = (C == 1) & (R == hub)

    @pl.when(gives)
    def _():
        for row in range(per + 1, n):
            signal(barrier, row, 0)

    when(collects, signal, barrier, 0, 1)
    @pl.when(spreads)
    def _():
        for row in range(per + 1, n):
            signal(barrier, row, 1)

    when(hub - R >= 2, signal, barrier, hub, C)
    greeted = jnp.where(R == hub, R - 1, one((C == 1) & (R - hub >= 2)))
    greeted += one(((C == 0) & (R > per)) | feeds)
    for j in range(per):
        peer = per * C + j
        when(far(peer) & (peer > R), signal, barrier, peer, quarter)
        greeted += one(far(peer) & (peer < R))
    for row, there in beside:
        when(there, signal, barrier, row, C)
        greeted += 1 if there is None else one(there)
    signal(barrier, R, O)
    greeted += 1

    h_at = lax.broadcasted_iota(jnp.int32, (ch, WIDE), 0)
    l_at = lax.broadcasted_iota(jnp.int32, (ch, WIDE), 1)
    in_big = l_at < LANES
    spread = jnp.where(
        jnp.where(in_big, l_at % big, big + l_at % small) == h_at, 1.0, 0.0
    )
    lanes = lax.broadcasted_iota(jnp.int32, (1, WIDE), 1)
    phase_of = jnp.where(lanes < LANES, lanes // big, (lanes % HALF) // small)
    spread4 = jnp.where(l_at % HALF == h_at, 1.0, 0.0).astype(bf)
    phase4_of = lanes // HALF
    lane = lax.broadcasted_iota(jnp.int32, (1, LANES), 1)
    lower = lane < HALF

    def remote(src, dst, s, r, row, col):
        return pltpu.make_async_remote_copy(
            src_ref=src,
            dst_ref=dst,
            send_sem=s,
            recv_sem=r,
            device_id=(group, row, col),
            device_id_type=mesh_type,
        )

    def embed(row, col):
        collected = one((row == per - 2) & (col == 1) & (R < per))
        return remote(e_hbm, eb.at[R], send.at[at_embed], erecv.at[collected], row, col)

    pl.semaphore_wait(barrier, greeted)
    to_collector = embed(per - 2, 1)
    when(feeds, to_collector.start)
    embs, soon_sent, late = [(feeds, to_collector)], [], []
    ahead = jnp.where(gives, n - 1 - per, 0)
    for j in range(per):
        peer = per * C + j
        answers = far(peer) & (peer < R)
        if j == per - 2:
            when(fed, signal, ncred.at[mine], peer, quarter)
            answers &= jnp.logical_not(fed)
        when(answers, signal, mcred, peer, quarter)
        copy = embed(peer, quarter)
        wanted = far(peer) & (quarter >= C)
        embs.append((wanted, copy))
        soon_sent.append((wanted & (peer < R), copy))
        late.append((wanted & (peer > R), copy))
        ahead += one(far(peer) & (peer > R))
    when((C == 1) & (R > hub + 1), signal, ncred.at[0], hub, C)
    when((C == 0) & (R > per), signal, mcred, per, 1)
    for row in range(per - 1):
        copy = embed(row, C)
        embs.append(((R == hub) & (hub - row >= 2), copy))
        soon_sent.append(embs[-1])
    for row in range(per + 1, n):
        copy = embed(row, C)
        embs.append((spreads, copy))
        late.append((spreads, copy))
        copy = embed(row, 0)
        embs.append((gives, copy))
        late.append((gives, copy))
    for k, (row, there) in enumerate(beside):
        copy = embed(row, C)
        wanted = (quarter != C) | (lax.div(row, per) == quarter)
        wanted = both(wanted & ((C == 1) | (R != per) | (row < R)), there)
        embs.append((wanted, copy))
        when(wanted, copy.start)
    for load in loads:
        load.start()

    own_at = pl.multiple_of(SIDE * C, SIDE)
    placed = [jnp.where(phase_of == p, spread, 0.0).astype(bf) for p in range(PHASES)]
    load_m.wait()
    tile = m_ref[...].reshape(groups, PHASES, cols, ch)
    packed = mm(tile[:, 0].reshape(groups * cols, ch), placed[0])
    for p in range(1, PHASES):
        packed = packed + mm(tile[:, p].reshape(groups * cols, ch), placed[p])
    packed = packed.reshape(groups, cols, WIDE)
    for g in range(groups):
        pk[1, g, pl.ds(own_at, cols), :] = packed[g, :, :LANES].astype(bf)
    for t in range(blocks - groups):
        piece = packed[2 * t, :, LANES:]
        if 2 * t + 1 < groups:
            piece = jnp.where(lower, piece, packed[2 * t + 1, :, LANES:])
        pk[1, groups + t, pl.ds(own_at, cols), :] = piece.astype(bf)
    edge = pl.ds(pl.multiple_of(cols - SIDE - (cols - 2 * SIDE) * C, SIDE), SIDE)
    rest = pl.ds(pl.multiple_of(2 * SIDE * C, SIDE), cols - SIDE)
    side_at = pl.ds(pl.multiple_of(cols * C, SIDE), SIDE)
    halos = []
    for k, (row, there) in enumerate(beside):
        block = 2 * odd if k == 0 else 2 * (1 - odd)
        for at, part in enumerate((edge, rest)):
            halos.append(
                remote(
                    pk.at[1, :, part, :],
                    pk.at[block, :, part, :],
                    send.at[at_halo],
                    recv.at[k if at == 0 else 2],
                    row,
                    C,
                )
            )
    when(slants, halos[2].start)
    halos[0].start()
    when(slants & (C == 0), halos[3].start)
    when(C == 0, halos[1].start)
    to_side = remote(
        pk.at[1, :, edge, :], pk.at[1, :, side_at, :], send.at[at_side], recv.at[3], R, O
    )
    to_side.start()
    for wanted, copy in soon_sent:
        when(wanted, copy.start)

    def block_of(ref, s, r):
        return remote(ref, ref, s, r, R, O)

    def embeds(count, r):
        return block_of(eb.at[pl.ds(0, count)], send.at[at_embed], erecv.at[r])

    load_e.wait()

    eb[R] = e_ref[...]

    soon = quarter >= C
    when(soon & (ahead > 0), pl.semaphore_wait, mcred, ahead)
    when(spreads, pl.semaphore_wait, ncred.at[0], n - 1 - per)
    for waits, copy in late:
        when(waits, copy.start)

    def spread_rows(y, phases):
        top, bottom = y[:big], y[big:]
        first = [jnp.where(phases == p, top, 0.0) for p in range(PHASES)]
        second = [jnp.where(phases == p, bottom, 0.0) for p in range(PHASES)]
        return (
            jnp.concatenate(first, axis=0).astype(bf),
            jnp.concatenate(second, axis=0).astype(bf),
        )

    def pack_weight(w_ref, across, phases, dst, places):
        for a, at in enumerate(places):
            for b in range(3):
                first, second = spread_rows(mm(w_ref[a, b], across), phases)
                dst[at + b * LANES : at + (b + 1) * LANES, :] = first
                low = at + 3 * LANES + (0, LANES, HALF)[b]
                dst[low : low + HALF, :] = second
            dst[at + TAPS - HALF : at + TAPS, :] = jnp.zeros((HALF, WIDE), bf)

    exact = lax.Precision.HIGHEST
    for i, held in enumerate((w12_ref, wm_ref, wrc_ref, row_ref)):
        pltpu.make_async_copy(held, held, send.at[i]).wait()
    pack_weight(w1_ref, spread.astype(bf), phase_of, wa, (0, TAPS, 2 * TAPS))
    half_mix = mm(wm_ref[...], spread4) * 0.5
    mix = half_mix.astype(bf)
    pack_weight(w2_ref, mix, phase4_of, wb, (0, TAPS, 2 * TAPS + WIDE))
    first, second = spread_rows(half_mix, phase4_of)
    at = 2 * TAPS
    wb[at : at + LANES, :] = first
    wb[at + LANES : at + LANES + HALF, :] = second
    wb[at + LANES + HALF : at + WIDE, :] = jnp.zeros((HALF, WIDE), bf)
    bias1 = mm(b1_ref[...], spread, exact)
    bias2 = mm(b2_ref[...], half_mix, exact) + 0.5 * mm(bm_ref[...], spread4.astype(f32), exact)
    head = mm(wh_ref[...], spread4[:, :LANES].astype(f32), exact)
    wr = mm_tn(wr_ref[...], spread.astype(bf)).astype(bf)
    wc = mm_tn(wc_ref[...], spread.astype(bf)).astype(bf)

    whole = eb.at[pl.ds(0, per)]
    bundles = [
        remote(whole, whole, send.at[row], erecv.at[0], per + row, 0)
        for row in range(per)
    ]

    @pl.when(collects)
    def _():
        embeds(per - 1, 1).wait_recv()
        for row in (0, per - 1, *range(1, per - 1)):
            pl.semaphore_wait(ncred.at[row], 1)
            bundles[row].start()

    relays = []
    for k, (row, there) in enumerate(beside):
        block = 2 * (1 - odd) if k == 0 else 2 * odd
        copy = remote(
            pk.at[block, :, edge, :],
            pk.at[block, :, side_at, :],
            send.at[at_side],
            recv.at[3],
            R,
            O,
        )
        relays.append((there, copy))
    halos[0].wait_recv()
    relays[0][1].start()
    when(slants, halos[2].wait_recv)
    when(slants, relays[1][1].start)

    when(slants & (C == 1), halos[3].start)
    when(C == 1, halos[1].start)
    awaited = jnp.where(fed, per, 0)
    for row in range(n):
        first = (per - 1) * C
        read = (row >= first) & (row <= first + per) & (row != R)
        read |= (row == R - 1) | (row == R + 1)
        if row < per:
            read &= jnp.logical_not(fed | collects)
        awaited += one(read)
    for count in range(1, n + 1):
        when(awaited == count, embeds(count, 0).wait_recv)
    held = -(-width // rows)
    for k in range(held):
        ct[k * rows : (k + 1) * rows, :] = mm(eb[(n - held) * C + k], wc)
    def row_terms_of(b):
        terms = mm(eb[jnp.clip(R + b - 1, 0, n - 1)], wr)
        out = []
        for g in range(groups):
            total = terms[PHASES * g : PHASES * g + 1]
            for p in range(1, PHASES):
                total = jnp.where(phase_of == p, terms[PHASES * g + p : PHASES * g + p + 1], total)
            out.append(total)
        return out

    row_terms = [row_terms_of(b) for b in range(3)]

    for count, there in ((3, slants), (2, jnp.logical_not(slants))):
        edges = block_of(pk.at[pl.ds(0, count), :, edge, :], send.at[at_side], recv.at[3])
        rests = block_of(pk.at[pl.ds(0, count - 1), :, rest, :], send.at[at_halo], recv.at[2])
        when(there, edges.wait_recv)
        when(there, rests.wait_recv)

    col_id = lax.broadcasted_iota(jnp.int32, (width, 1), 0)

    def before(v, d):
        if d % 8 == 0:
            return jnp.concatenate([jnp.zeros((d, LANES), f32), v[: width - d]], axis=0)
        return jnp.where(col_id < d, 0.0, pltpu.roll(v, d, axis=0))

    def after(v, d):
        if d % 8 == 0:
            return jnp.concatenate([v[d:], jnp.zeros((d, LANES), f32)], axis=0)
        return jnp.where(col_id >= width - d, 0.0, pltpu.roll(v, width - d, axis=0))

    def put_taps(dst, at, x, y, d):
        dst[at, :, :LANES] = before(x, d).astype(bf)
        dst[at, :, LANES : 2 * LANES] = x.astype(bf)
        dst[at, :, 2 * LANES : 3 * LANES] = after(x, d).astype(bf)
        dst[at, :, 3 * LANES : 4 * LANES] = jnp.where(lower, before(y, d), after(y, d)).astype(bf)
        dst[at, :, 4 * LANES :] = y.astype(bf)

    def base_block(b, valid):
        terms = row_terms[b]
        seconds = []
        for t in range(blocks - groups):
            g = 2 * t
            term = terms[g][:, LANES:]
            if g + 1 < groups:
                term = jnp.where(lower, term, terms[g + 1][:, LANES:])
            v = (pk[b, groups + t].astype(f32) + term + col_terms[:, LANES:]).astype(bf).astype(f32)
            turned = pltpu.roll(v, HALF, axis=1)
            seconds.append(jnp.where(lower, v, turned))
            seconds.append(jnp.where(lower, turned, v))
        for g in range(groups):
            x = pk[b, g].astype(f32) + terms[g][:, :LANES] + col_terms[:, :LANES]
            x, y = x.astype(bf).astype(f32), seconds[g]
            if valid is not None:
                x, y = jnp.where(valid, x, 0.0), jnp.where(valid, y, 0.0)
            at = b * groups + g
            xb[at, :, :LANES] = x.astype(bf)
            xb[at, :, LANES:] = y.astype(bf)
            put_taps(xs, at, jnp.maximum(x, 0.0), jnp.maximum(y, 0.0), FIRST_DILATION)

    step = FIRST_DILATION // PHASES
    step2 = SECOND_DILATION // PHASES
    ext = groups + 2 * step2
    skip = groups - step2 - step

    def first_layer(start, stop):
        left = jnp.concatenate(
            [
                xs[start + skip + a * step : stop + skip + a * step].reshape(-1, TAPS)
                for a in range(3)
            ],
            axis=1,
        )
        acc = mm(left, wa[...]).reshape(stop - start, width, WIDE)
        for u in range(start, stop):
            x = xb[u + skip + step].astype(f32) + acc[u - start] + bias1
            x = x.astype(bf).astype(f32)
            if u < step2:
                x = jnp.where(R > 0, x, 0.0)
            elif u >= step2 + groups:
                x = jnp.where(R < n - 1, x, 0.0)
            else:
                l1[u - step2] = x.astype(bf)
            x = jnp.maximum(x, 0.0)
            put_taps(xs2, u, x[:, :LANES], x[:, LANES:], SECOND_DILATION)

    col_terms = ct[pl.ds(pl.multiple_of((held * rows - width) * C, 8), width), :]
    base_block(1, None)
    base_block(0, R > 0)
    window = pl.ds(own_at, cols)

    def second_taps(a):
        return xs2[a * step2 : a * step2 + groups, window, :].reshape(groups * cols, TAPS)

    known = 2 * step2 + groups - step2
    first_layer(0, 4)
    base_block(2, R < n - 1)
    first_layer(4, known)
    left = [second_taps(0), second_taps(1), l1[:, window, :].reshape(groups * cols, WIDE)]
    mixed = mm(jnp.concatenate(left, axis=1), wb[: 2 * TAPS + WIDE])
    first_layer(known, ext)
    mixed = mixed + mm(second_taps(2), wb[2 * TAPS + WIDE :]) + bias2
    mixed = mixed.reshape(groups, cols, WIDE)

    def row_of(i):
        g, p = divmod(i, PHASES)
        at = p // 2 * LANES
        return mixed[g, :, at : at + LANES], p % 2

    for i in range(hr):
        (first, at), (second, _) = row_of(i), row_of(i + hr)
        if at == 0:
            second = pltpu.roll(second, HALF, axis=1)
        else:
            first = pltpu.roll(first, HALF, axis=1)
        pair = jnp.where(lower, first, second)
        yp[i] = pair
        for j in range(per):
            sf[j, i * rows : (i + 1) * rows, :] = pair[j * rows : (j + 1) * rows, :]
    used = hr * rows
    for j in range(per):
        sb[j, :used] = sf[j].astype(bf)

    when(jnp.logical_not(soon | collects) & (ahead > 0), pl.semaphore_wait, mcred, ahead)
    for j in range(per):
        peer = per * C + j
        is_self = (peer == R) & (quarter == C)
        copy = remote(sb.at[j], gb.at[mine], send.at[at_mirror], mrecv.at[mine], peer, quarter)
        local = pltpu.make_async_copy(sb.at[j], gb.at[j], send.at[0])

        @pl.when(jnp.logical_not(is_self))
        def _():
            copy.start()

        @pl.when(is_self)
        def _():
            local.start()

    for count, there in ((3, slants), (2, jnp.logical_not(slants))):
        edges = block_of(pk.at[pl.ds(0, count), :, edge, :], send.at[at_side], recv.at[3])
        tiles = pk.at[pl.ds(0, count - 1), :, pl.ds(own_at, cols), :]
        when(there, edges.wait_send)
        when(there, block_of(tiles, send.at[at_halo], recv.at[2]).wait_send)
    sent = 0
    for leaves, _ in embs:
        sent += one(leaves)
    for count in range(1, n + 1):
        when(sent == count, embeds(count, 0).wait_send)
    for copy in bundles:
        when(collects, copy.wait_send)

    early = lax.broadcasted_iota(jnp.int32, (used, 1), 0) % rows < hr
    for j in range(per):
        peer = per * C + j
        is_self = (peer == R) & (quarter == C)
        arrival = remote(sb.at[j], gb.at[j], send.at[at_mirror], mrecv.at[j], peer, quarter)
        local = pltpu.make_async_copy(sb.at[j], gb.at[j], send.at[0])

        @pl.when(jnp.logical_not(is_self))
        def _():
            arrival.wait_recv()

        @pl.when(is_self)
        def _():
            local.wait()

        piece = gb[j, :used].astype(f32)
        turned = pltpu.roll(piece, HALF, axis=1)
        at = 2 * j * used
        tb[at : at + used, :] = jnp.where(early, piece, turned)
        tb[at + used : at + 2 * used, :] = jnp.where(early, turned, piece)

    halves = jnp.where(
        lax.broadcasted_iota(jnp.int32, (8, WIDE), 1) % LANES // HALF
        == lax.broadcasted_iota(jnp.int32, (8, WIDE), 0),
        1.0,
        0.0,
    ).astype(bf)
    for i in range(hr):
        mirror = jnp.where(
            lower, tb[pl.ds(i, cols, stride=rows), :], tb[pl.ds(i + hr, cols, stride=rows), :]
        )
        z = jnp.maximum(yp[i] + mirror, 0.0) * head
        top = z.astype(bf)
        rest = (z - top.astype(f32)).astype(bf)
        sums = mm_nt(halves, jnp.concatenate([top, rest], axis=1))
        out_ref[i : i + 1, :] = sums[0:1]
        out_ref[i + hr : i + hr + 1, :] = sums[1:2]

    for count, there in ((per - 1, quarter == C), (per, quarter != C)):
        pieces = block_of(sb.at[pl.ds(0, count)], send.at[at_mirror], mrecv.at[0])
        when(there, pieces.wait_send)


def fused(map_in, embedding, w_row, w_col, w1, b1, w2, b2, w_mix, b_mix, w_head):
    rows, cols, ch = map_in.shape
    n = lax.axis_size("row")
    width, per, hr, groups = cols + SIDE, cols // rows, rows // 2, rows // PHASES
    blocks = groups + (groups + 1) // 2
    ext = groups + 2 * SECOND_DILATION // PHASES
    used = hr * rows
    held = -(-used // 16) * 16
    bf, f32 = jnp.bfloat16, jnp.float32
    dma = pltpu.SemaphoreType.DMA
    operands = (
        map_in,
        embedding,
        w_row.T,
        w_col.T,
        w1,
        b1.reshape(1, ch),
        w2,
        b2.reshape(1, ch),
        w_mix,
        b_mix.reshape(1, ch),
        w_head.reshape(1, ch),
    )
    return pl.pallas_call(
        functools.partial(fused_kernel, n),
        out_shape=pltpu.VMEM((rows, cols), f32),
        in_specs=[pl.BlockSpec(memory_space=pl.ANY)] * 11,
        out_specs=pl.BlockSpec(memory_space=pltpu.VMEM),
        scratch_shapes=[
            pltpu.VMEM((3, blocks, width, LANES), bf),
            pltpu.VMEM((n, rows, embedding.shape[1]), bf),
            pltpu.VMEM((-(-width // rows) * rows, WIDE), f32),
            pltpu.VMEM((3 * groups, width, WIDE), bf),
            pltpu.VMEM((3 * groups, width, TAPS), bf),
            pltpu.VMEM((groups, width, WIDE), bf),
            pltpu.VMEM((ext, width, TAPS), bf),
            pltpu.VMEM((3 * TAPS, WIDE), bf),
            pltpu.VMEM((3 * TAPS + WIDE, WIDE), bf),
            pltpu.VMEM((hr, cols, LANES), f32),
            pltpu.VMEM((per, used, LANES), f32),
            pltpu.VMEM((per, held, LANES), bf),
            pltpu.VMEM((per, held, LANES), bf),
            pltpu.VMEM((cols * rows, LANES), f32),
            dma((8,)),
            dma((4,)),
            dma((2,)),
            dma((per,)),
            pltpu.SemaphoreType.REGULAR,
            pltpu.SemaphoreType.REGULAR((per,)),
            pltpu.VMEM(map_in.shape, bf),
            pltpu.VMEM(embedding.shape, bf),
            pltpu.VMEM((2, *w_row.T.shape), bf),
            pltpu.VMEM((2, *w1.shape), bf),
            pltpu.VMEM(w_mix.shape, bf),
            pltpu.VMEM((4, 1, ch), f32),
        ],
        compiler_params=pltpu.CompilerParams(collective_id=0, has_side_effects=True),
    )(*operands)


def fits(rows, cols, channels, row_count, col_count):
    held = 2 * (cols + SIDE) * (3 * rows // PHASES) * (2 * TAPS + 2 * WIDE)
    weights = 2 * WIDE * (6 * TAPS + WIDE)
    halo = FIRST_DILATION + SECOND_DILATION
    return (
        held + weights <= FUSED_VMEM
        and rows == halo
        and row_count == 8
        and col_count == 2
        and cols % SIDE == 0
        and channels == 48
        and cols * col_count == rows * row_count
    )


def on_device(
    map_in,
    embedding,
    w_row,
    w_col,
    first_kernel_weight,
    first_bias,
    second_kernel_weight,
    second_bias,
    w_mix,
    b_mix,
    w_head,
):
    patch_rows, patch_columns, channels = map_in.shape
    row_count = lax.axis_size("row")
    if fits(patch_rows, patch_columns, channels, row_count, lax.axis_size("col")):
        return fused(
            map_in,
            embedding,
            w_row,
            w_col,
            first_kernel_weight,
            first_bias,
            second_kernel_weight,
            second_bias,
            w_mix,
            b_mix,
            w_head,
        )
    row_at = lax.axis_index("row")
    col_at = lax.axis_index("col")
    all_bins = lax.all_gather(embedding, "row", axis=0, tiled=True)
    row_terms = jnp.dot(all_bins, w_row, preferred_element_type=jnp.float32)
    col_terms = jnp.dot(all_bins, w_col, preferred_element_type=jnp.float32)
    own_rows = lax.dynamic_slice_in_dim(row_terms, row_at * patch_rows, patch_rows, 0)
    own_cols = lax.dynamic_slice_in_dim(col_terms, col_at * patch_columns, patch_columns, 0)
    contact_grid = (
        map_in.astype(jnp.float32) + own_rows[:, None, :] + own_cols[None, :, :]
    ).astype(jnp.bfloat16)
    first_padded = padded(contact_grid, (("row", 0), ("col", 1)), FIRST_DILATION)
    first_layer = (
        contact_grid.astype(jnp.float32)
        + dilated_conv(
            jnp.maximum(first_padded, 0),
            first_kernel_weight,
            FIRST_DILATION,
            patch_rows,
            patch_columns,
        )
        + first_bias
    ).astype(jnp.bfloat16)
    second_padded = padded(first_layer, (("row", 0), ("col", 1)), SECOND_DILATION)
    second_layer = (
        first_layer.astype(jnp.float32)
        + dilated_conv(
            jnp.maximum(second_padded, 0),
            second_kernel_weight,
            SECOND_DILATION,
            patch_rows,
            patch_columns,
        )
        + second_bias
    ).astype(jnp.bfloat16)
    half_rows = patch_rows // 2
    blocks_per = row_count // 2
    arranged = second_layer.reshape(2, half_rows, blocks_per, patch_rows, channels)
    arranged = arranged.transpose(0, 2, 1, 3, 4).reshape(
        2 * blocks_per, half_rows, patch_rows, channels
    )
    exchanged = lax.all_to_all(
        lax.all_to_all(arranged, "row", split_axis=0, concat_axis=0, tiled=True),
        "col",
        split_axis=0,
        concat_axis=0,
        tiled=True,
    )
    exchanged = exchanged.reshape(2, blocks_per, half_rows, patch_rows, channels)
    top_half = row_at // blocks_per
    kept_part = lax.dynamic_index_in_dim(exchanged, top_half, 0, keepdims=False)
    sent_part = lax.dynamic_index_in_dim(exchanged, 1 - top_half, 0, keepdims=False)
    came_back = swapped(sent_part, "row", blocks_per.bit_length() - 1)
    stacked = jnp.where(
        top_half == 0, jnp.stack([kept_part, came_back]), jnp.stack([came_back, kept_part])
    )
    mirrored = stacked.transpose(3, 1, 0, 2, 4).reshape(patch_rows, patch_columns, channels)
    symmetric = ((second_layer.astype(jnp.float32) + mirrored.astype(jnp.float32)) * 0.5).astype(
        jnp.bfloat16
    )
    mixture = (
        jnp.einsum("rch,hk->rck", symmetric, w_mix, preferred_element_type=jnp.float32) + b_mix
    )
    mixture = jnp.maximum(mixture, 0.0)
    return jnp.sum(mixture * w_head, axis=-1)


def solution(mesh):
    placed = (
        P(("group", "row"), "col", None),
        P(("group", "row"), None),
        P(),
        P(),
        P(),
        P(),
        P(),
        P(),
        P(),
        P(),
        P(),
    )
    return jax.shard_map(
        on_device, mesh=mesh, in_specs=placed, out_specs=P(("group", "row"), "col"), check_vma=False
    )
```

```python
import functools

import jax
import jax.numpy as jnp
from jax import lax
from jax.experimental import pallas as pl
from jax.experimental.pallas import tpu as pltpu
from jax.sharding import PartitionSpec as P

FIRST_DILATION = 4
SECOND_DILATION = 8


def padded(array, sides, width):
    for axis, dim in sides:
        peers, length = (lax.axis_size(axis), array.shape[dim])
        up = [(i, (i + 1) % peers) for i in range(peers - 1)]
        down = [(j, i) for i, j in up]
        last = lax.slice_in_dim(array, length - width, length, axis=dim)
        leading = lax.slice_in_dim(array, 0, width, axis=dim)
        before = lax.ppermute(last, axis, up)
        after = lax.ppermute(leading, axis, down)
        array = jnp.concatenate([before, array, after], axis=dim)
    return array


def swapped(value, axis, bit):
    mask = 2**bit
    pairs = [(source, source ^ mask) for source in range(lax.axis_size(axis))]
    return lax.ppermute(value, axis, pairs)


def dilated_conv(active, weight, spacing, out_rows, out_cols):
    windows = []
    for tap_row in range(3):
        for tap_col in range(3):
            windows.append(
                active[
                    tap_row * spacing : tap_row * spacing + out_rows,
                    tap_col * spacing : tap_col * spacing + out_cols,
                ]
            )
    stacked = jnp.concatenate(windows, axis=-1)
    flat_weight = weight.reshape(9 * weight.shape[2], weight.shape[3])
    return jnp.einsum("rch,hk->rck", stacked, flat_weight, preferred_element_type=jnp.float32)


LANES = 128
HALF = 64
SIDE = 16
PHASES = 4
WIDE = 2 * LANES
TAPS = 5 * LANES
FUSED_VMEM = 8 * 2**20


def one_hot(rows, columns, offsets):
    r = lax.broadcasted_iota(jnp.int32, (rows, columns), 0)
    c = lax.broadcasted_iota(jnp.int32, (rows, columns), 1)
    hit = c == r + offsets[0]
    for offset in offsets[1:]:
        hit = hit | (c == r + offset)
    return jnp.where(hit, 1.0, 0.0)


def mm(a, b, precision=None):
    return jnp.dot(a, b, preferred_element_type=jnp.float32, precision=precision)


def mm_tn(a, b):
    return lax.dot_general(a, b, (((0,), (0,)), ((), ())), preferred_element_type=jnp.float32)


def mm_nt(a, b):
    return lax.dot_general(a, b, (((1,), (1,)), ((), ())), preferred_element_type=jnp.float32)


def fused_kernel(
    n,
    m_hbm,
    e_hbm,
    wr_hbm,
    wc_hbm,
    w1_hbm,
    b1_hbm,
    w2_hbm,
    b2_hbm,
    wm_hbm,
    bm_hbm,
    wh_hbm,
    out_ref,
    pk,
    eb,
    ct,
    xb,
    xs,
    l1,
    xs2,
    wa,
    wb,
    yp,
    sb,
    gb,
    tb,
    send,
    recv,
    erecv,
    mrecv,
    mcred,
    ncred,
    m_ref,
    e_ref,
    wrc_ref,
    w12_ref,
    wm_ref,
    row_ref,
):
    bf, f32 = jnp.bfloat16, jnp.float32
    rows, cols, ch = m_ref.shape
    hr = rows // 2
    groups = rows // PHASES
    blocks = pk.shape[1]
    width = cols + SIDE
    per = cols // rows
    big = LANES // PHASES
    small = ch - big
    R = lax.axis_index("row")
    C = lax.axis_index("col")
    O = 1 - C
    group = lax.axis_index("group")
    mesh_type = pl.DeviceIdType.MESH

    at_side, at_mirror, at_halo, at_embed = 4, 5, 6, 7
    wr_ref, wc_ref = wrc_ref.at[0], wrc_ref.at[1]
    w1_ref, w2_ref = w12_ref.at[0], w12_ref.at[1]
    b1_ref, b2_ref, bm_ref, wh_ref = (row_ref.at[i] for i in range(4))
    groups_of = (
        ((w1_hbm, w1_ref), (w2_hbm, w2_ref)),
        ((wm_hbm, wm_ref),),
        ((wr_hbm, wr_ref), (wc_hbm, wc_ref)),
        ((b1_hbm, b1_ref), (b2_hbm, b2_ref), (bm_hbm, bm_ref), (wh_hbm, wh_ref)),
    )
    loads = [
        pltpu.make_async_copy(a, b, send.at[i]) for i, pairs in enumerate(groups_of) for a, b in pairs
    ]
    load_m = pltpu.make_async_copy(m_hbm, m_ref, send.at[at_side])
    load_e = pltpu.make_async_copy(e_hbm, e_ref, send.at[at_mirror])
    load_m.start()
    load_e.start()
    eb[...] = jnp.zeros_like(eb)
    quarter = lax.div(R, per)
    mine = lax.rem(R, per)
    odd = lax.rem(R, 2)
    hub = per - C
    across, slant = R + 1 - 2 * odd, R - 1 + 2 * odd
    slants = (slant >= 0) & (slant < n)
    slant = jnp.clip(slant, 0, n - 1)
    beside = ((across, None), (slant, slants))
    barrier = pltpu.get_barrier_semaphore()

    def signal(sem, row, col):
        pl.semaphore_signal(sem, inc=1, device_id=(group, row, col), device_id_type=mesh_type)

    def when(condition, act, *args):
        if condition is None:
            act(*args)
        else:
            pl.when(condition)(functools.partial(act, *args))

    def both(a, b):
        return a if b is None else a & b

    def one(condition):
        return jnp.where(condition, 1, 0)

    def far(peer):
        return (peer != R) & ((quarter != C) | (peer - R >= 2) | (R - peer >= 2))

    collects = (R == per - 2) & (C == 1)
    fed = (R >= per) & (C == 0)
    gives = (R == per) & (C == 1)
    feeds = (C == 1) & (R == 0)
    spreads = (C == 1) & (R == hub)

    @pl.when(gives)
    def _():
        for row in range(per + 1, n):
            signal(barrier, row, 0)

    when(collects, signal, barrier, 0, 1)
    @pl.when(spreads)
    def _():
        for row in range(per + 1, n):
            signal(barrier, row, 1)

    when(hub - R >= 2, signal, barrier, hub, C)
    greeted = jnp.where(R == hub, R - 1, one((C == 1) & (R - hub >= 2)))
    greeted += one(((C == 0) & (R > per)) | feeds)
    for j in range(per):
        peer = per * C + j
        when(far(peer) & (peer > R), signal, barrier, peer, quarter)
        greeted += one(far(peer) & (peer < R))
    for row, there in beside:
        when(there, signal, barrier, row, C)
        greeted += 1 if there is None else one(there)
    signal(barrier, R, O)
    greeted += 1

    h_at = lax.broadcasted_iota(jnp.int32, (ch, WIDE), 0)
    l_at = lax.broadcasted_iota(jnp.int32, (ch, WIDE), 1)
    in_big = l_at < LANES
    spread = jnp.where(
        jnp.where(in_big, l_at % big, big + l_at % small) == h_at, 1.0, 0.0
    )
    lanes = lax.broadcasted_iota(jnp.int32, (1, WIDE), 1)
    phase_of = jnp.where(lanes < LANES, lanes // big, (lanes % HALF) // small)
    spread4 = jnp.where(l_at % HALF == h_at, 1.0, 0.0).astype(bf)
    phase4_of = lanes // HALF
    lane = lax.broadcasted_iota(jnp.int32, (1, LANES), 1)
    lower = lane < HALF

    def remote(src, dst, s, r, row, col):
        return pltpu.make_async_remote_copy(
            src_ref=src,
            dst_ref=dst,
            send_sem=s,
            recv_sem=r,
            device_id=(group, row, col),
            device_id_type=mesh_type,
        )

    def embed(row, col):
        collected = one((row == per - 2) & (col == 1) & (R < per))
        return remote(e_hbm, eb.at[R], send.at[at_embed], erecv.at[collected], row, col)

    pl.semaphore_wait(barrier, greeted)
    to_collector = embed(per - 2, 1)
    when(feeds, to_collector.start)
    embs, soon_sent, late = [(feeds, to_collector)], [], []
    ahead = jnp.where(gives, n - 1 - per, 0)
    for j in range(per):
        peer = per * C + j
        answers = far(peer) & (peer < R)
        if j == per - 2:
            when(fed, signal, ncred.at[mine], peer, quarter)
            answers &= jnp.logical_not(fed)
        when(answers, signal, mcred, peer, quarter)
        copy = embed(peer, quarter)
        wanted = far(peer) & (quarter >= C)
        embs.append((wanted, copy))
        soon_sent.append((wanted & (peer < R), copy))
        late.append((wanted & (peer > R), copy))
        ahead += one(far(peer) & (peer > R))
    when((C == 1) & (R > hub + 1), signal, ncred.at[0], hub, C)
    when((C == 0) & (R > per), signal, mcred, per, 1)
    for row in range(per - 1):
        copy = embed(row, C)
        embs.append(((R == hub) & (hub - row >= 2), copy))
        soon_sent.append(embs[-1])
    for row in range(per + 1, n):
        copy = embed(row, C)
        embs.append((spreads, copy))
        late.append((spreads, copy))
        copy = embed(row, 0)
        embs.append((gives, copy))
        late.append((gives, copy))
    for k, (row, there) in enumerate(beside):
        copy = embed(row, C)
        wanted = (quarter != C) | (lax.div(row, per) == quarter)
        wanted = both(wanted & ((C == 1) | (R != per) | (row < R)), there)
        embs.append((wanted, copy))
        when(wanted, copy.start)
    for load in loads:
        load.start()

    own_at = pl.multiple_of(SIDE * C, SIDE)
    placed = [jnp.where(phase_of == p, spread, 0.0).astype(bf) for p in range(PHASES)]
    load_m.wait()
    tile = m_ref[...].reshape(groups, PHASES, cols, ch)
    packed = mm(tile[:, 0].reshape(groups * cols, ch), placed[0])
    for p in range(1, PHASES):
        packed = packed + mm(tile[:, p].reshape(groups * cols, ch), placed[p])
    packed = packed.reshape(groups, cols, WIDE)
    for g in range(groups):
        pk[1, g, pl.ds(own_at, cols), :] = packed[g, :, :LANES].astype(bf)
    for t in range(blocks - groups):
        piece = packed[2 * t, :, LANES:]
        if 2 * t + 1 < groups:
            piece = jnp.where(lower, piece, packed[2 * t + 1, :, LANES:])
        pk[1, groups + t, pl.ds(own_at, cols), :] = piece.astype(bf)
    edge = pl.ds(pl.multiple_of(cols - SIDE - (cols - 2 * SIDE) * C, SIDE), SIDE)
    rest = pl.ds(pl.multiple_of(2 * SIDE * C, SIDE), cols - SIDE)
    side_at = pl.ds(pl.multiple_of(cols * C, SIDE), SIDE)
    halos = []
    for k, (row, there) in enumerate(beside):
        block = 2 * odd if k == 0 else 2 * (1 - odd)
        for at, part in enumerate((edge, rest)):
            halos.append(
                remote(
                    pk.at[1, :, part, :],
                    pk.at[block, :, part, :],
                    send.at[at_halo],
                    recv.at[k if at == 0 else 2],
                    row,
                    C,
                )
            )
    when(slants, halos[2].start)
    halos[0].start()
    when(slants & (C == 0), halos[3].start)
    when(C == 0, halos[1].start)
    to_side = remote(
        pk.at[1, :, edge, :], pk.at[1, :, side_at, :], send.at[at_side], recv.at[3], R, O
    )
    to_side.start()
    for wanted, copy in soon_sent:
        when(wanted, copy.start)

    def block_of(ref, s, r):
        return remote(ref, ref, s, r, R, O)

    def embeds(count, r):
        return block_of(eb.at[pl.ds(0, count)], send.at[at_embed], erecv.at[r])

    load_e.wait()

    eb[R] = e_ref[...]

    soon = quarter >= C
    when(soon & (ahead > 0), pl.semaphore_wait, mcred, ahead)
    when(spreads, pl.semaphore_wait, ncred.at[0], n - 1 - per)
    for waits, copy in late:
        when(waits, copy.start)

    def spread_rows(y, phases):
        top, bottom = y[:big], y[big:]
        first = [jnp.where(phases == p, top, 0.0) for p in range(PHASES)]
        second = [jnp.where(phases == p, bottom, 0.0) for p in range(PHASES)]
        return (
            jnp.concatenate(first, axis=0).astype(bf),
            jnp.concatenate(second, axis=0).astype(bf),
        )

    def pack_weight(w_ref, across, phases, dst, places):
        for a, at in enumerate(places):
            for b in range(3):
                first, second = spread_rows(mm(w_ref[a, b], across), phases)
                dst[at + b * LANES : at + (b + 1) * LANES, :] = first
                low = at + 3 * LANES + (0, LANES, HALF)[b]
                dst[low : low + HALF, :] = second
            dst[at + TAPS - HALF : at + TAPS, :] = jnp.zeros((HALF, WIDE), bf)

    exact = lax.Precision.HIGHEST
    for i, held in enumerate((w12_ref, wm_ref, wrc_ref, row_ref)):
        pltpu.make_async_copy(held, held, send.at[i]).wait()
    pack_weight(w1_ref, spread.astype(bf), phase_of, wa, (0, TAPS, 2 * TAPS))
    half_mix = mm(wm_ref[...], spread4) * 0.5
    mix = half_mix.astype(bf)
    pack_weight(w2_ref, mix, phase4_of, wb, (0, TAPS, 2 * TAPS + WIDE))
    first, second = spread_rows(half_mix, phase4_of)
    at = 2 * TAPS
    wb[at : at + LANES, :] = first
    wb[at + LANES : at + LANES + HALF, :] = second
    wb[at + LANES + HALF : at + WIDE, :] = jnp.zeros((HALF, WIDE), bf)
    bias1 = mm(b1_ref[...], spread, exact)
    bias2 = mm(b2_ref[...], half_mix, exact) + 0.5 * mm(bm_ref[...], spread4.astype(f32), exact)
    head = mm(wh_ref[...], spread4[:, :LANES].astype(f32), exact)
    wr = mm_tn(wr_ref[...], spread.astype(bf)).astype(bf)
    wc = mm_tn(wc_ref[...], spread.astype(bf)).astype(bf)

    whole = eb.at[pl.ds(0, per)]
    bundles = [
        remote(whole, whole, send.at[row], erecv.at[0], per + row, 0)
        for row in range(per)
    ]

    @pl.when(collects)
    def _():
        embeds(per - 1, 1).wait_recv()
        for row in (0, per - 1, *range(1, per - 1)):
            pl.semaphore_wait(ncred.at[row], 1)
            bundles[row].start()

    relays = []
    for k, (row, there) in enumerate(beside):
        block = 2 * (1 - odd) if k == 0 else 2 * odd
        copy = remote(
            pk.at[block, :, edge, :],
            pk.at[block, :, side_at, :],
            send.at[at_side],
            recv.at[3],
            R,
            O,
        )
        relays.append((there, copy))
    halos[0].wait_recv()
    relays[0][1].start()
    when(slants, halos[2].wait_recv)
    when(slants, relays[1][1].start)

    when(slants & (C == 1), halos[3].start)
    when(C == 1, halos[1].start)
    awaited = jnp.where(fed, per, 0)
    for row in range(n):
        first = (per - 1) * C
        read = (row >= first) & (row <= first + per) & (row != R)
        read |= (row == R - 1) | (row == R + 1)
        if row < per:
            read &= jnp.logical_not(fed | collects)
        awaited += one(read)
    for count in range(1, n + 1):
        when(awaited == count, embeds(count, 0).wait_recv)
    held = -(-width // rows)
    for k in range(held):
        ct[k * rows : (k + 1) * rows, :] = mm(eb[(n - held) * C + k], wc)
    def row_terms_of(b):
        terms = mm(eb[jnp.clip(R + b - 1, 0, n - 1)], wr)
        out = []
        for g in range(groups):
            total = terms[PHASES * g : PHASES * g + 1]
            for p in range(1, PHASES):
                total = jnp.where(phase_of == p, terms[PHASES * g + p : PHASES * g + p + 1], total)
            out.append(total)
        return out

    row_terms = [row_terms_of(b) for b in range(3)]

    for count, there in ((3, slants), (2, jnp.logical_not(slants))):
        edges = block_of(pk.at[pl.ds(0, count), :, edge, :], send.at[at_side], recv.at[3])
        rests = block_of(pk.at[pl.ds(0, count - 1), :, rest, :], send.at[at_halo], recv.at[2])
        when(there, edges.wait_recv)
        when(there, rests.wait_recv)

    col_id = lax.broadcasted_iota(jnp.int32, (width, 1), 0)

    def before(v, d):
        if d % 8 == 0:
            return jnp.concatenate([jnp.zeros((d, LANES), f32), v[: width - d]], axis=0)
        return jnp.where(col_id < d, 0.0, pltpu.roll(v, d, axis=0))

    def after(v, d):
        if d % 8 == 0:
            return jnp.concatenate([v[d:], jnp.zeros((d, LANES), f32)], axis=0)
        return jnp.where(col_id >= width - d, 0.0, pltpu.roll(v, width - d, axis=0))

    def put_taps(dst, at, x, y, d):
        dst[at, :, :LANES] = before(x, d).astype(bf)
        dst[at, :, LANES : 2 * LANES] = x.astype(bf)
        dst[at, :, 2 * LANES : 3 * LANES] = after(x, d).astype(bf)
        dst[at, :, 3 * LANES : 4 * LANES] = jnp.where(lower, before(y, d), after(y, d)).astype(bf)
        dst[at, :, 4 * LANES :] = y.astype(bf)

    def base_block(b, valid):
        terms = row_terms[b]
        seconds = []
        for t in range(blocks - groups):
            g = 2 * t
            term = terms[g][:, LANES:]
            if g + 1 < groups:
                term = jnp.where(lower, term, terms[g + 1][:, LANES:])
            v = (pk[b, groups + t].astype(f32) + term + col_terms[:, LANES:]).astype(bf).astype(f32)
            turned = pltpu.roll(v, HALF, axis=1)
            seconds.append(jnp.where(lower, v, turned))
            seconds.append(jnp.where(lower, turned, v))
        for g in range(groups):
            x = pk[b, g].astype(f32) + terms[g][:, :LANES] + col_terms[:, :LANES]
            x, y = x.astype(bf).astype(f32), seconds[g]
            if valid is not None:
                x, y = jnp.where(valid, x, 0.0), jnp.where(valid, y, 0.0)
            at = b * groups + g
            xb[at, :, :LANES] = x.astype(bf)
            xb[at, :, LANES:] = y.astype(bf)
            put_taps(xs, at, jnp.maximum(x, 0.0), jnp.maximum(y, 0.0), FIRST_DILATION)

    step = FIRST_DILATION // PHASES
    step2 = SECOND_DILATION // PHASES
    ext = groups + 2 * step2
    skip = groups - step2 - step

    def first_layer(start, stop):
        left = jnp.concatenate(
            [
                xs[start + skip + a * step : stop + skip + a * step].reshape(-1, TAPS)
                for a in range(3)
            ],
            axis=1,
        )
        acc = mm(left, wa[...]).reshape(stop - start, width, WIDE)
        for u in range(start, stop):
            x = xb[u + skip + step].astype(f32) + acc[u - start] + bias1
            x = x.astype(bf).astype(f32)
            if u < step2:
                x = jnp.where(R > 0, x, 0.0)
            elif u >= step2 + groups:
                x = jnp.where(R < n - 1, x, 0.0)
            else:
                l1[u - step2] = x.astype(bf)
            x = jnp.maximum(x, 0.0)
            put_taps(xs2, u, x[:, :LANES], x[:, LANES:], SECOND_DILATION)

    col_terms = ct[pl.ds(pl.multiple_of((held * rows - width) * C, 8), width), :]
    base_block(1, None)
    base_block(0, R > 0)
    window = pl.ds(own_at, cols)

    def second_taps(a):
        return xs2[a * step2 : a * step2 + groups, window, :].reshape(groups * cols, TAPS)

    known = 2 * step2 + groups - step2
    first_layer(0, 4)
    base_block(2, R < n - 1)
    first_layer(4, known)
    left = [second_taps(0), second_taps(1), l1[:, window, :].reshape(groups * cols, WIDE)]
    mixed = mm(jnp.concatenate(left, axis=1), wb[: 2 * TAPS + WIDE])
    first_layer(known, ext)
    mixed = mixed + mm(second_taps(2), wb[2 * TAPS + WIDE :]) + bias2
    mixed = mixed.reshape(groups, cols, WIDE)

    def row_of(i):
        g, p = divmod(i, PHASES)
        at = p // 2 * LANES
        return mixed[g, :, at : at + LANES], p % 2

    for i in range(hr):
        (first, at), (second, _) = row_of(i), row_of(i + hr)
        if at == 0:
            second = pltpu.roll(second, HALF, axis=1)
        else:
            first = pltpu.roll(first, HALF, axis=1)
        pair = jnp.where(lower, first, second)
        yp[i] = pair
        for j in range(per):
            sb[j, i * rows : (i + 1) * rows, :] = pair[j * rows : (j + 1) * rows, :].astype(bf)
    used = hr * rows

    when(jnp.logical_not(soon | collects) & (ahead > 0), pl.semaphore_wait, mcred, ahead)
    pieces_out = []
    for j in range(per):
        peer = per * C + j
        is_self = (peer == R) & (quarter == C)
        copy = remote(sb.at[j], gb.at[mine], send.at[at_mirror], mrecv.at[mine], peer, quarter)
        local = pltpu.make_async_copy(sb.at[j], gb.at[j], send.at[0])
        pieces_out.append((is_self, copy, local))

    @pl.when(quarter != C)
    def _():
        for _, copy, _ in pieces_out:
            copy.start()

    @pl.when(quarter == C)
    def _():
        for is_self, copy, local in pieces_out:
            pl.when(jnp.logical_not(is_self))(copy.start)
            pl.when(is_self)(local.start)

    for count, there in ((3, slants), (2, jnp.logical_not(slants))):
        edges = block_of(pk.at[pl.ds(0, count), :, edge, :], send.at[at_side], recv.at[3])
        tiles = pk.at[pl.ds(0, count - 1), :, pl.ds(own_at, cols), :]
        when(there, edges.wait_send)
        when(there, block_of(tiles, send.at[at_halo], recv.at[2]).wait_send)
    sent = 0
    for leaves, _ in embs:
        sent += one(leaves)
    for count in range(1, n + 1):
        when(sent == count, embeds(count, 0).wait_send)
    for copy in bundles:
        when(collects, copy.wait_send)

    early = lax.broadcasted_iota(jnp.int32, (used, 1), 0) % rows < hr
    for j in range(per):
        peer = per * C + j
        is_self = (peer == R) & (quarter == C)
        arrival = remote(sb.at[j], gb.at[j], send.at[at_mirror], mrecv.at[j], peer, quarter)
        local = pltpu.make_async_copy(sb.at[j], gb.at[j], send.at[0])

        @pl.when(jnp.logical_not(is_self))
        def _():
            arrival.wait_recv()

        @pl.when(is_self)
        def _():
            local.wait()

        piece = gb[j, :used].astype(f32)
        turned = pltpu.roll(piece, HALF, axis=1)
        at = 2 * j * used
        tb[at : at + used, :] = jnp.where(early, piece, turned)
        tb[at + used : at + 2 * used, :] = jnp.where(early, turned, piece)

    halves = jnp.where(
        lax.broadcasted_iota(jnp.int32, (8, WIDE), 1) % LANES // HALF
        == lax.broadcasted_iota(jnp.int32, (8, WIDE), 0),
        1.0,
        0.0,
    ).astype(bf)
    for i in range(hr):
        mirror = jnp.where(
            lower, tb[pl.ds(i, cols, stride=rows), :], tb[pl.ds(i + hr, cols, stride=rows), :]
        )
        z = jnp.maximum(yp[i] + mirror, 0.0) * head
        top = z.astype(bf)
        rest = (z - top.astype(f32)).astype(bf)
        sums = mm_nt(halves, jnp.concatenate([top, rest], axis=1))
        out_ref[i : i + 1, :] = sums[0:1]
        out_ref[i + hr : i + hr + 1, :] = sums[1:2]

    for count, there in ((per - 1, quarter == C), (per, quarter != C)):
        pieces = block_of(sb.at[pl.ds(0, count)], send.at[at_mirror], mrecv.at[0])
        when(there, pieces.wait_send)


def fused(map_in, embedding, w_row, w_col, w1, b1, w2, b2, w_mix, b_mix, w_head):
    rows, cols, ch = map_in.shape
    n = lax.axis_size("row")
    width, per, hr, groups = cols + SIDE, cols // rows, rows // 2, rows // PHASES
    blocks = groups + (groups + 1) // 2
    ext = groups + 2 * SECOND_DILATION // PHASES
    used = hr * rows
    held = used
    bf, f32 = jnp.bfloat16, jnp.float32
    dma = pltpu.SemaphoreType.DMA
    operands = (
        map_in,
        embedding,
        w_row.T,
        w_col.T,
        w1,
        b1.reshape(1, ch),
        w2,
        b2.reshape(1, ch),
        w_mix,
        b_mix.reshape(1, ch),
        w_head.reshape(1, ch),
    )
    return pl.pallas_call(
        functools.partial(fused_kernel, n),
        out_shape=pltpu.VMEM((rows, cols), f32),
        in_specs=[pl.BlockSpec(memory_space=pl.ANY)] * 11,
        out_specs=pl.BlockSpec(memory_space=pltpu.VMEM),
        scratch_shapes=[
            pltpu.VMEM((3, blocks, width, LANES), bf),
            pltpu.VMEM((n, rows, embedding.shape[1]), bf),
            pltpu.VMEM((-(-width // rows) * rows, WIDE), f32),
            pltpu.VMEM((3 * groups, width, WIDE), bf),
            pltpu.VMEM((3 * groups, width, TAPS), bf),
            pltpu.VMEM((groups, width, WIDE), bf),
            pltpu.VMEM((ext, width, TAPS), bf),
            pltpu.VMEM((3 * TAPS, WIDE), bf),
            pltpu.VMEM((3 * TAPS + WIDE, WIDE), bf),
            pltpu.VMEM((hr, cols, LANES), f32),
            pltpu.VMEM((per, held, LANES), bf),
            pltpu.VMEM((per, held, LANES), bf),
            pltpu.VMEM((cols * rows, LANES), f32),
            dma((8,)),
            dma((4,)),
            dma((2,)),
            dma((per,)),
            pltpu.SemaphoreType.REGULAR,
            pltpu.SemaphoreType.REGULAR((per,)),
            pltpu.VMEM(map_in.shape, bf),
            pltpu.VMEM(embedding.shape, bf),
            pltpu.VMEM((2, *w_row.T.shape), bf),
            pltpu.VMEM((2, *w1.shape), bf),
            pltpu.VMEM(w_mix.shape, bf),
            pltpu.VMEM((4, 1, ch), f32),
        ],
        compiler_params=pltpu.CompilerParams(collective_id=0, has_side_effects=True),
    )(*operands)


def fits(rows, cols, channels, row_count, col_count):
    held = 2 * (cols + SIDE) * (3 * rows // PHASES) * (2 * TAPS + 2 * WIDE)
    weights = 2 * WIDE * (6 * TAPS + WIDE)
    halo = FIRST_DILATION + SECOND_DILATION
    return (
        held + weights <= FUSED_VMEM
        and rows == halo
        and row_count == 8
        and col_count == 2
        and cols % SIDE == 0
        and channels == 48
        and cols * col_count == rows * row_count
    )


def on_device(
    map_in,
    embedding,
    w_row,
    w_col,
    first_kernel_weight,
    first_bias,
    second_kernel_weight,
    second_bias,
    w_mix,
    b_mix,
    w_head,
):
    patch_rows, patch_columns, channels = map_in.shape
    row_count = lax.axis_size("row")
    if fits(patch_rows, patch_columns, channels, row_count, lax.axis_size("col")):
        return fused(
            map_in,
            embedding,
            w_row,
            w_col,
            first_kernel_weight,
            first_bias,
            second_kernel_weight,
            second_bias,
            w_mix,
            b_mix,
            w_head,
        )
    row_at = lax.axis_index("row")
    col_at = lax.axis_index("col")
    all_bins = lax.all_gather(embedding, "row", axis=0, tiled=True)
    row_terms = jnp.dot(all_bins, w_row, preferred_element_type=jnp.float32)
    col_terms = jnp.dot(all_bins, w_col, preferred_element_type=jnp.float32)
    own_rows = lax.dynamic_slice_in_dim(row_terms, row_at * patch_rows, patch_rows, 0)
    own_cols = lax.dynamic_slice_in_dim(col_terms, col_at * patch_columns, patch_columns, 0)
    contact_grid = (
        map_in.astype(jnp.float32) + own_rows[:, None, :] + own_cols[None, :, :]
    ).astype(jnp.bfloat16)
    first_padded = padded(contact_grid, (("row", 0), ("col", 1)), FIRST_DILATION)
    first_layer = (
        contact_grid.astype(jnp.float32)
        + dilated_conv(
            jnp.maximum(first_padded, 0),
            first_kernel_weight,
            FIRST_DILATION,
            patch_rows,
            patch_columns,
        )
        + first_bias
    ).astype(jnp.bfloat16)
    second_padded = padded(first_layer, (("row", 0), ("col", 1)), SECOND_DILATION)
    second_layer = (
        first_layer.astype(jnp.float32)
        + dilated_conv(
            jnp.maximum(second_padded, 0),
            second_kernel_weight,
            SECOND_DILATION,
            patch_rows,
            patch_columns,
        )
        + second_bias
    ).astype(jnp.bfloat16)
    half_rows = patch_rows // 2
    blocks_per = row_count // 2
    arranged = second_layer.reshape(2, half_rows, blocks_per, patch_rows, channels)
    arranged = arranged.transpose(0, 2, 1, 3, 4).reshape(
        2 * blocks_per, half_rows, patch_rows, channels
    )
    exchanged = lax.all_to_all(
        lax.all_to_all(arranged, "row", split_axis=0, concat_axis=0, tiled=True),
        "col",
        split_axis=0,
        concat_axis=0,
        tiled=True,
    )
    exchanged = exchanged.reshape(2, blocks_per, half_rows, patch_rows, channels)
    top_half = row_at // blocks_per
    kept_part = lax.dynamic_index_in_dim(exchanged, top_half, 0, keepdims=False)
    sent_part = lax.dynamic_index_in_dim(exchanged, 1 - top_half, 0, keepdims=False)
    came_back = swapped(sent_part, "row", blocks_per.bit_length() - 1)
    stacked = jnp.where(
        top_half == 0, jnp.stack([kept_part, came_back]), jnp.stack([came_back, kept_part])
    )
    mirrored = stacked.transpose(3, 1, 0, 2, 4).reshape(patch_rows, patch_columns, channels)
    symmetric = ((second_layer.astype(jnp.float32) + mirrored.astype(jnp.float32)) * 0.5).astype(
        jnp.bfloat16
    )
    mixture = (
        jnp.einsum("rch,hk->rck", symmetric, w_mix, preferred_element_type=jnp.float32) + b_mix
    )
    mixture = jnp.maximum(mixture, 0.0)
    return jnp.sum(mixture * w_head, axis=-1)


def solution(mesh):
    placed = (
        P(("group", "row"), "col", None),
        P(("group", "row"), None),
        P(),
        P(),
        P(),
        P(),
        P(),
        P(),
        P(),
        P(),
        P(),
    )
    return jax.shard_map(
        on_device, mesh=mesh, in_specs=placed, out_specs=P(("group", "row"), "col"), check_vma=False
    )
```
